32 devices in a mesh: dp: 4 (over z), head: 4 (over x, core), tensor: 2 (over y).
Axes of the slice: x: 2, y: 2, z: 4, core: 2. Of those that a mesh axis runs over, the one named last changes fastest.
Arguments:
- tokens: bfloat16 [8192, 768], P(('dp', 'head', 'tensor')), may hold values from -6 to 6
- seg_ids: int32 [4, 2048], P('dp'), may hold values from 0 to 2, never falling along the last dimension, each value on 1 to 1024 neighbouring positions
- norm1_gain: float32 [768], replicated, may hold values from 0.5 to 1.5
- norm1_bias: float32 [768], replicated, may hold values from -3 to 3
- norm2_gain: float32 [768], replicated, may hold values from 0.5 to 1.5
- norm2_bias: float32 [768], replicated, may hold values from -3 to 3
- q_weight: bfloat16 [768, 768], P('dp', ('head', 'tensor')), may hold values from -0.21875 to 0.21875
- k_weight: bfloat16 [768, 768], P('dp', ('head', 'tensor')), may hold values from -0.21875 to 0.21875
- v_weight: bfloat16 [768, 768], P('dp', ('head', 'tensor')), may hold values from -0.21875 to 0.21875
- out_weight: bfloat16 [768, 768], P('dp', ('head', 'tensor')), may hold values from -0.21875 to 0.21875
- up_weight: bfloat16 [768, 3072], P('dp', ('head', 'tensor')), may hold values from -0.21875 to 0.21875
- down_weight: bfloat16 [768, 3072], P('dp', ('head', 'tensor')), may hold values from -0.109375 to 0.109375
- shift_weight: float32 [4, 768], P(None, ('head', 'tensor')), may hold values from -3 to 3
- decay_rate: float32 [64, 768], P(None, ('head', 'tensor')), may hold values from 0.002 to 0.5
- in_coef: float32 [64, 768], P(None, ('head', 'tensor')), may hold values from -0.75 to 0.75
- out_coef: float32 [64, 768], P(None, ('head', 'tensor')), may hold values from -0.75 to 0.75
- skip_coef: float32 [768], P(('head', 'tensor')), may hold values from -4 to 4
- cotangent: bfloat16 [8192, 768], P(('dp', 'head', 'tensor')), may hold values from -6 to 6
Outputs:
- block_out: bfloat16 [8192, 768], P(('dp', 'head', 'tensor'))
- grad_tokens: float32 [8192, 768], P(('dp', 'head', 'tensor'))
- grad_norm1_gain: float32 [768], replicated
- grad_norm1_bias: float32 [768], replicated
- grad_norm2_gain: float32 [768], replicated
- grad_norm2_bias: float32 [768], replicated
- grad_q_weight: float32 [768, 768], P('dp', ('head', 'tensor'))
- grad_k_weight: float32 [768, 768], P('dp', ('head', 'tensor'))
- grad_v_weight: float32 [768, 768], P('dp', ('head', 'tensor'))
- grad_out_weight: float32 [768, 768], P('dp', ('head', 'tensor'))
- grad_up_weight: float32 [768, 3072], P('dp', ('head', 'tensor'))
- grad_down_weight: float32 [768, 3072], P('dp', ('head', 'tensor'))
- grad_shift_weight: float32 [4, 768], P(None, ('head', 'tensor'))
- grad_decay_rate: float32 [64, 768], P(None, ('head', 'tensor'))
- grad_in_coef: float32 [64, 768], P(None, ('head', 'tensor'))
- grad_out_coef: float32 [64, 768], P(None, ('head', 'tensor'))
- grad_skip_coef: float32 [768], P(('head', 'tensor'))
The draws below stay inside these ranges and needn't reach their ends.
Inputs may be any that keep to these rules, and one draw needn't show every extreme that they name: `seg_ids`: along a row the sequence numbers never fall; each sequence has 1 to 1024 tokens and one has exactly 1024.
All inputs are finite; a program needn't handle non-finite values.
Results may differ from the reference program's by a relative error of at most 0.012.
The reference program's roundings to bfloat16 on the way count: a program that leaves them out, or rounds other values in their place, can miss the bound.
Values may be sent and summed in bfloat16 or wider, within the bound.
A program may use at most 128 MiB of HBM per device.

```python
import math
import jax
import jax.numpy as jnp
import numpy as np
from jax import lax

D = 768
FF = 3072
NS = 64
SHIFT = 4
BLOCK = 128
SEQS = 3
TOK_DEV = 2048
SEQ_MOST = 1024
TOKENS = 8192
N_DP = 4


def steps_of(own_key, dims, shards, smallest, high):
    def one(position, shards_of):
        draws = jax.random.uniform(jax.random.fold_in(jax.random.fold_in(own_key, 6), position), (shards_of,), jnp.float32, smallest / len(shards), high / len(shards))
        return jnp.repeat(jnp.exp(draws), dims[position] // shards_of).reshape((-1,) + (1,) * (len(dims) - position - 1))

    level = one(*shards[0])
    for cut in shards[1:]:
        level = level * one(*cut)
    return level


def split_up(amount, total, most, skew):
    loads = [(1 << 20) // math.isqrt(standing ** skew) + 1 for standing in range(2, amount + 1)]
    surplus, given = total - most - (amount - 1), [1] * (amount - 1)
    while surplus > 0:
        candidates = [i for i in range(amount - 1) if given[i] < most]
        mass, remaining = sum([loads[i] for i in candidates]), surplus
        for i in candidates:
            extra = min(most - given[i], max(1, remaining * loads[i] // mass), surplus)
            given[i] = given[i] + extra
            surplus = surplus - extra
    return np.array([most] + given)


def uneven(own_key, number_of, total, limit, skew):
    if number_of == 2:
        one = jax.random.randint(own_key, (), max(1, total - limit), min(limit, total - 1) + 1)
        return jnp.stack([one, total - one])
    sizes = jnp.asarray(split_up(number_of, total, limit, skew), jnp.int32)
    pairs = (number_of - 1) // 2
    donor, taker = sizes[1:1 + 2 * pairs:2], sizes[2:2 + 2 * pairs:2]
    margin = jnp.minimum(donor - 1, limit - taker)
    moved = jax.random.randint(jax.random.fold_in(own_key, 1), (pairs,), 0, 1 << 20) % (margin + 1)
    sizes = sizes.at[1:1 + 2 * pairs:2].set(donor - moved).at[2:2 + 2 * pairs:2].set(taker + moved)
    return sizes[jax.random.permutation(jax.random.fold_in(own_key, 2), number_of)]


def scatter_about(stream_key, dims, scale, most, pieces=(), kind=jnp.bfloat16):
    values = scale * jax.random.normal(stream_key, dims, jnp.float32)
    if pieces:
        values = values * steps_of(stream_key, dims, pieces, -0.22, 0.18)
    return jnp.clip(values, -most, most).astype(kind)


def setup_inputs(seed: int = 0) -> dict:
    key_list = jax.random.split(jax.random.key(seed), 19)
    return {
        "tokens": scatter_about(key_list[0], (TOKENS, D), 1.0, 6.0, ((0, 32),)),
        "seg_ids": jax.vmap(lambda own: jnp.searchsorted(jnp.cumsum(uneven(own, SEQS, TOK_DEV, SEQ_MOST, 1)), jnp.arange(TOK_DEV), side="right"))(jax.random.split(key_list[1], N_DP)).reshape((N_DP, TOK_DEV)).astype(jnp.int32),
        "norm1_gain": jnp.clip(1.0 + 0.1 * jax.random.normal(key_list[2], (D,), jnp.float32), 0.5, 1.5),
        "norm1_bias": scatter_about(key_list[3], (D,), 0.5, 3.0, (), jnp.float32),
        "norm2_gain": jnp.clip(1.0 + 0.1 * jax.random.normal(key_list[4], (D,), jnp.float32), 0.5, 1.5),
        "norm2_bias": scatter_about(key_list[5], (D,), 0.5, 3.0, (), jnp.float32),
        "q_weight": scatter_about(key_list[6], (D, D), D ** -0.5, 0.21875, ((0, 4), (1, 8))),
        "k_weight": scatter_about(key_list[7], (D, D), D ** -0.5, 0.21875, ((0, 4), (1, 8))),
        "v_weight": scatter_about(key_list[8], (D, D), D ** -0.5, 0.21875, ((0, 4), (1, 8))),
        "out_weight": scatter_about(key_list[9], (D, D), D ** -0.5, 0.21875, ((0, 4), (1, 8))),
        "up_weight": scatter_about(key_list[10], (D, FF), D ** -0.5, 0.21875, ((0, 4), (1, 8))),
        "down_weight": scatter_about(key_list[11], (D, FF), FF ** -0.5, 0.109375, ((0, 4), (1, 8))),
        "shift_weight": scatter_about(key_list[12], (SHIFT, D), SHIFT ** -0.5, 3.0, ((1, 8),), jnp.float32),
        "decay_rate": jnp.clip(jnp.exp(math.log(0.5) - 5.521461 * jax.random.uniform(key_list[13], (NS, D), jnp.float32) ** steps_of(key_list[13], (NS, D), ((1, 8),), -0.2, 0.2)), 0.002, 0.5),
        "in_coef": scatter_about(key_list[14], (NS, D), NS ** -0.5, 0.75, ((1, 8),), jnp.float32),
        "out_coef": scatter_about(key_list[15], (NS, D), NS ** -0.5, 0.75, ((1, 8),), jnp.float32),
        "skip_coef": scatter_about(key_list[16], (D,), 1.0, 4.0, ((0, 8),), jnp.float32),
        "cotangent": scatter_about(key_list[17], (TOKENS, D), 1.0, 6.0, ((0, 32),)),
    }


@jax.custom_vjp
def low(v):
    return lax.optimization_barrier(v.astype(jnp.bfloat16)).astype(jnp.float32)

@jax.custom_vjp
def low_back(v):
    return v

def low_keep(v):
    return (low(v), None)

def low_pass(kept, grad):
    return (grad,)

def back_keep(v):
    return (v, None)

def back_low(kept, grad):
    return (low(grad),)
low.defvjp(low_keep, low_pass)
low_back.defvjp(back_keep, back_low)

def layer_norm(values, gain, bias):
    centre = lax.optimization_barrier(jnp.mean(values, axis=-1, keepdims=True))
    centred = values - centre
    spread = lax.optimization_barrier(jnp.mean(centred * centred, axis=-1, keepdims=True))
    return centred * lax.rsqrt(spread + 1e-05) * gain + bias

def exact_gelu(values):
    return jax.nn.gelu(values, approximate=False)

def mixer_core(q_proj, k_proj, v_proj, shift_w, rate, in_b, out_c, skip, segment):
    length, chans = k_proj.shape
    shifted = shift_w[0] * k_proj
    for lag_step in range(1, SHIFT):
        same_seq = (segment[lag_step:] == segment[:-lag_step]).astype(k_proj.dtype)
        prior = k_proj[:-lag_step] * same_seq[:, None]
        prior = jnp.concatenate([jnp.zeros((lag_step, chans), k_proj.dtype), prior], axis=0)
        shifted = shifted + shift_w[lag_step] * prior
    drive = shifted * v_proj
    lag_pos = jnp.arange(BLOCK).astype(k_proj.dtype)
    powers = jnp.exp(-rate[None] * lag_pos[:, None, None])
    kernel = jnp.einsum('lnc,nc->lc', powers, in_b * out_c, precision=lax.Precision.HIGHEST)
    places = jnp.arange(BLOCK)
    offset = places[:, None] - places[None, :]
    toeplitz = kernel[jnp.clip(offset, 0, BLOCK - 1)]
    causal = offset >= 0
    ahead = powers * jnp.exp(-rate)[None]
    behind = powers[::-1]
    across = jnp.exp(-rate * BLOCK)
    blocks_in = drive.reshape(length // BLOCK, BLOCK, chans)
    blocks_seg = segment.reshape(length // BLOCK, BLOCK)

    def advance(carry, item):
        state, last_seg = carry
        part, seg_part = item
        same_mask = (causal & (seg_part[:, None] == seg_part[None, :])).astype(part.dtype)
        inner = jnp.einsum('abc,ab,bc->ac', toeplitz, same_mask, part, precision=lax.Precision.HIGHEST)
        live = (seg_part == last_seg).astype(part.dtype)
        outer = jnp.einsum('pnc,nc->pc', ahead, out_c * state, precision=lax.Precision.HIGHEST) * live[:, None]
        end_seg = seg_part[BLOCK - 1]
        keep_mask = (seg_part == end_seg).astype(part.dtype)
        fresh = jnp.einsum('pnc,pc->nc', behind, part * keep_mask[:, None], precision=lax.Precision.HIGHEST) * in_b
        carry_on = (end_seg == last_seg).astype(part.dtype)
        return ((fresh + across * state * carry_on, end_seg), inner + outer)
    start_state = (jnp.zeros_like(rate), jnp.array(-1, jnp.int32))
    _, outputs = lax.scan(jax.checkpoint(advance), start_state, (blocks_in, blocks_seg))
    return q_proj * (outputs.reshape(length, chans) + skip * drive)

def high_dot(left, right):
    return jnp.dot(left, right, precision=lax.Precision.HIGHEST)

def block_forward(x_rows, segment, n1_gain, n1_bias, n2_gain, n2_bias, w_q, w_k, w_v, w_out, w_up, w_down, shift_w, rate, in_b, out_c, skip):
    xn_one = low(layer_norm(x_rows, n1_gain, n1_bias))
    q_proj = low_back(high_dot(xn_one, w_q))
    k_proj = low_back(high_dot(xn_one, w_k))
    v_proj = low_back(high_dot(xn_one, w_v))
    mixed = low(mixer_core(q_proj, k_proj, v_proj, shift_w, rate, in_b, out_c, skip, segment))
    mix_out = low_back(high_dot(mixed, w_out.T))
    hidden = x_rows + mix_out
    xn_two = low(layer_norm(hidden, n2_gain, n2_bias))
    pre_act = low_back(high_dot(xn_two, w_up))
    act_out = low(exact_gelu(pre_act))
    return hidden + high_dot(act_out, w_down.T)

def reference(tokens, seg_ids, norm1_gain, norm1_bias, norm2_gain, norm2_bias, q_weight, k_weight, v_weight, out_weight, up_weight, down_weight, shift_weight, decay_rate, in_coef, out_coef, skip_coef, cotangent):
    params = (norm1_gain.astype(jnp.float32), norm1_bias.astype(jnp.float32), norm2_gain.astype(jnp.float32), norm2_bias.astype(jnp.float32), q_weight.astype(jnp.float32), k_weight.astype(jnp.float32), v_weight.astype(jnp.float32), out_weight.astype(jnp.float32), up_weight.astype(jnp.float32), down_weight.astype(jnp.float32), shift_weight.astype(jnp.float32), decay_rate.astype(jnp.float32), in_coef.astype(jnp.float32), out_coef.astype(jnp.float32), skip_coef.astype(jnp.float32))
    x_blocks = tokens.astype(jnp.float32).reshape(N_DP, TOK_DEV, D)
    cot_blocks = cotangent.astype(jnp.float32).reshape(N_DP, TOK_DEV, D)

    def one_group(carry, item):
        x_rows, cot_rows, segment = item

        def local_forward(x_in, *weights):
            return block_forward(x_in, segment, *weights)
        out_rows, back_fn = jax.vjp(local_forward, x_rows, *params)
        grads = back_fn(cot_rows)
        summed = tuple((acc + new for acc, new in zip(carry, grads[1:])))
        return (summed, (out_rows.astype(jnp.bfloat16), grads[0]))
    start_sums = tuple((jnp.zeros_like(p) for p in params))
    sums, (out_blocks, grad_blocks) = lax.scan(one_group, start_sums, (x_blocks, cot_blocks, seg_ids))
    return (out_blocks.reshape(TOKENS, D), grad_blocks.reshape(TOKENS, D), sums[0], sums[1], sums[2], sums[3], sums[4], sums[5], sums[6], sums[7], sums[8], sums[9], sums[10], sums[11], sums[12], sums[13], sums[14])
```

```python
import functools
import jax, jax.numpy as jnp
from jax import lax
from jax.experimental import pallas as pl
from jax.experimental.pallas import tpu as pltpu

LANES = 128
SHIFT = 4
SEQS = 3
NT = (((1,), (1,)), ((), ()))
TN = (((0,), (0,)), ((), ()))
NN = (((1,), (0,)), ((), ()))


def mm(left, right, dims=NN):
    return lax.dot_general(left, right, dims, preferred_element_type=jnp.float32)


def iota(shape, axis):
    return lax.broadcasted_iota(jnp.int32, shape, axis)


def seg_masks(seg, nb):
    lane = iota((nb, LANES), 1)
    row = iota((nb, LANES), 0)
    masks = [(seg == k).astype(jnp.float32) for k in range(SEQS)]
    end = jnp.broadcast_to(seg[:, LANES - 1 :], (nb, LANES))
    last = jnp.where(row == 0, -1, pltpu.roll(end, 1, axis=0))
    live = (seg == last).astype(jnp.float32)
    keep = (seg == end).astype(jnp.float32)
    carry = (end == last).astype(jnp.float32)
    same = []
    for j in range(1, SHIFT):
        r = pltpu.roll(seg, j, axis=1)
        r2 = pltpu.roll(r, 1, axis=0)
        prior = jnp.where(lane < j, r2, r)
        ok = (prior == seg) & ((row > 0) | (lane >= j))
        same.append(ok.astype(jnp.float32))
    return masks, live, keep, carry, same


def priors(k, same):
    lane = iota(k.shape, 1)
    out = []
    for j in range(1, SHIFT):
        r = pltpu.roll(k, j, axis=1)
        r2 = pltpu.roll(r, 1, axis=0)
        out.append(jnp.where(lane < j, r2, r) * same[j - 1])
    return out


def flip_matrix():
    return (iota((LANES, LANES), 0) + iota((LANES, LANES), 1) == LANES - 1).astype(jnp.bfloat16)


def read_seg(seg_ref, nb):
    return jnp.concatenate([seg_ref[:, b * LANES : (b + 1) * LANES] for b in range(nb)], axis=0)


def transposed(scr, top, bottom):
    ns, chans = top.shape
    scr[...] = jnp.zeros_like(scr)
    scr[0:ns, 0:chans] = top
    if bottom is not None:
        scr[ns : 2 * ns, 0:chans] = bottom
    return scr[...].T


def stack_masked(x, masks):
    return jnp.concatenate([x * m for m in masks], axis=0).astype(jnp.bfloat16)


def merge_masked(y, masks):
    nb = masks[0].shape[0]
    return sum(y[i * nb : (i + 1) * nb] * m for i, m in enumerate(masks))


def toeplitz(krow):
    t = pltpu.roll(jnp.broadcast_to(krow, (LANES, LANES)), 0, axis=1, stride=1, stride_axis=0)
    return jnp.where(iota((LANES, LANES), 1) >= iota((LANES, LANES), 0), t, 0.0).astype(jnp.bfloat16)


def mixer_fwd_kernel(
    un, qkv_ref, seg_ref, sw_ref, skip_ref, rate_ref, inb_ref, outc_ref,
    mixed_ref, core_ref, s_ref, f_ref, urev_ref, pp_ref, kern_ref,
    tscr, a_scr, b_scr, c_scr, e_scr, u_scr, kscr,
):
    ns, chans = rate_ref.shape
    nb = qkv_ref.shape[1] // chans
    masks, live, keep, carry, same = seg_masks(read_seg(seg_ref, nb), nb)
    flip = flip_matrix()
    keep_rev = mm(keep.astype(jnp.bfloat16), flip)
    rate, in_b, out_c = rate_ref[...], inb_ref[...], outc_ref[...]
    decay = jnp.exp(-rate)
    a_scr[...] = transposed(tscr, rate, rate)
    b_scr[...] = transposed(tscr, in_b * decay, None)
    c_scr[...] = transposed(tscr, out_c, None)
    e_scr[...] = transposed(tscr, jnp.exp(-rate * LANES), None)

    def kern_step(i, e):
        for j in range(8):
            kscr[pl.ds(i * 8 + j, 1), 0:chans] = jnp.sum(e, axis=0, keepdims=True)
            e = e * decay
        return e

    kscr[...] = jnp.zeros_like(kscr)
    lax.fori_loop(0, LANES // 8, kern_step, in_b * out_c)
    kern_ref[...] = kscr[...].T[0:chans]

    def drive_step(i, _):
        for j in range(un):
            c = i * un + j
            rows = pl.ds(pl.multiple_of(c * nb, nb), nb)
            k = qkv_ref[1, rows]
            shifted = sw_ref[0, c] * k
            for lag, prior in enumerate(priors(k, same)):
                shifted = shifted + sw_ref[lag + 1, c] * prior
            u_scr[rows, :] = shifted * qkv_ref[2, rows]
        return 0

    lax.fori_loop(0, chans // un, drive_step, 0)
    step_rows = 16 * nb

    def rev_step(i, _):
        rows = pl.ds(pl.multiple_of(i * step_rows, step_rows), step_rows)
        urev_ref[rows, :] = mm(u_scr[rows, :].astype(jnp.bfloat16), flip).astype(jnp.bfloat16)
        return 0

    lax.fori_loop(0, chans // 16, rev_step, 0)
    pos = iota((LANES, LANES), 0).astype(jnp.float32)
    factor = jnp.where(iota((LANES, LANES), 1) < ns, 1.0, pos)
    i8 = iota((8, LANES), 0).astype(jnp.float32)
    i16 = iota((LANES // 8, LANES), 0).astype(jnp.float32) * 8.0

    def fresh_step(i, _):
        for j in range(un):
            c = i * un + j
            rows = pl.ds(pl.multiple_of(c * nb, nb), nb)
            a = a_scr[pl.ds(c, 1), :]
            base = jnp.exp(-a * i8)
            tall = jnp.exp(-a * i16)
            p = (tall[:, None, :] * base[None]).reshape(LANES, LANES)
            pp = (p * factor).astype(jnp.bfloat16)
            pp_ref[pl.ds(pl.multiple_of(c * LANES, LANES), LANES), :] = pp
            urk = (urev_ref[rows, :].astype(jnp.float32) * keep_rev).astype(jnp.bfloat16)
            f_ref[rows, :] = mm(urk, pp)
        return 0

    lax.fori_loop(0, chans // un, fresh_step, 0)
    across = e_scr[0:chans, :]
    b_ext = b_scr[0:chans, :]
    state = jnp.zeros((chans, LANES), jnp.float32)
    for b in range(nb):
        s_ref[pl.ds(b, chans, stride=nb), :] = state + pltpu.roll(state, ns, axis=1)
        fresh = f_ref[pl.ds(b, chans, stride=nb), :]
        state = across * carry[b : b + 1, :] * state + b_ext * fresh

    def out_step(i, _):
        for j in range(un):
            c = i * un + j
            rows = pl.ds(pl.multiple_of(c * nb, nb), nb)
            t = toeplitz(kern_ref[pl.ds(c, 1), :])
            u = u_scr[rows, :]
            y = merge_masked(mm(stack_masked(u, masks), t), masks)
            sc = (s_ref[rows, :] * c_scr[pl.ds(c, 1), :]).astype(jnp.bfloat16)
            pp = pp_ref[pl.ds(pl.multiple_of(c * LANES, LANES), LANES), :]
            core = y + live * mm(sc, pp, NT) + skip_ref[0, c] * u
            core_ref[rows, :] = core
            u_scr[rows, :] = qkv_ref[0, rows] * core
        return 0

    lax.fori_loop(0, chans // un, out_step, 0)
    for b in range(nb):
        half = b % 2
        mixed_ref[b // 2, :, half * LANES : (half + 1) * LANES] = u_scr[
            pl.ds(b, chans, stride=nb), :
        ].astype(jnp.bfloat16)


def mixer_fwd(qkv, seg, shift_w, skip, rate, in_b, out_c, un=4):
    ns, chans = rate.shape
    rows = qkv.shape[1]
    nb = rows // chans
    f32, bf16 = jnp.float32, jnp.bfloat16
    sds = jax.ShapeDtypeStruct
    vm = pl.BlockSpec(memory_space=pltpu.VMEM)
    sm = pl.BlockSpec(memory_space=pltpu.SMEM)
    sq = pltpu.VMEM((LANES, LANES), f32)
    return pl.pallas_call(
        functools.partial(mixer_fwd_kernel, un),
        out_shape=(
            sds((nb // 2, chans, 2 * LANES), bf16),
            sds((rows, LANES), f32),
            sds((rows, LANES), f32),
            sds((rows, LANES), f32),
            sds((rows, LANES), bf16),
            sds((chans * LANES, LANES), bf16),
            sds((chans, LANES), f32),
        ),
        in_specs=[vm, vm, sm, sm, vm, vm, vm],
        out_specs=(vm,) * 7,
        scratch_shapes=[sq, sq, sq, sq, sq, pltpu.VMEM((rows, LANES), f32), sq],
        compiler_params=pltpu.CompilerParams(vmem_limit_bytes=48 << 20),
        name="mixer_fwd",
    )(qkv, seg, shift_w, skip, rate, in_b, out_c)


def mixer_bwd_kernel(
    un, gm_ref, qkv_ref, core_ref, s_ref, f_ref, urev_ref, pp_ref, kern_ref, seg_ref,
    sw_ref, skip_ref, rate_ref, inb_ref, outc_ref,
    dqkv_ref, dsw_ref, drate_ref, dinb_ref, doutc_ref, dskip_ref,
    tscr, b_scr, c_scr, e_scr, g_scr, sh_scr, h_scr, x_scr, dur_scr, dui_scr, dq_scr, dk_scr, dv_scr, gr_scr, red_scr,
):
    ns, chans = rate_ref.shape
    nb = qkv_ref.shape[1] // chans
    masks, live, keep, carry, same = seg_masks(read_seg(seg_ref, nb), nb)
    flip = flip_matrix()
    keep_rev = mm(keep.astype(jnp.bfloat16), flip)
    masks_rev = [mm(m.astype(jnp.bfloat16), flip) for m in masks]
    rate, in_b, out_c = rate_ref[...], inb_ref[...], outc_ref[...]
    decay = jnp.exp(-rate)
    b_scr[...] = transposed(tscr, in_b * decay, None)
    c_scr[...] = transposed(tscr, out_c, None)
    e_scr[...] = transposed(tscr, jnp.exp(-rate * LANES), None)
    red_scr[...] = jnp.zeros_like(red_scr)
    gr_scr[...] = jnp.zeros_like(gr_scr)

    for b in range(nb):
        half = b % 2
        x_scr[pl.ds(b, chans, stride=nb), :] = gm_ref[
            b // 2, :, half * LANES : (half + 1) * LANES
        ].astype(jnp.float32)
    corner = iota((LANES, LANES), 0) + iota((LANES, LANES), 1) >= LANES - 1

    def grad_step(i, _):
        for j in range(un):
            c = i * un + j
            rows = pl.ds(pl.multiple_of(c * nb, nb), nb)
            gm = x_scr[rows, :]
            dq_scr[rows, :] = gm * core_ref[rows, :]
            g = gm * qkv_ref[0, rows]
            g_scr[rows, :] = g
            k = qkv_ref[1, rows]
            shifted = sw_ref[0, c] * k
            for lag, prior in enumerate(priors(k, same)):
                shifted = shifted + sw_ref[lag + 1, c] * prior
            sh_scr[rows, :] = shifted
            red_scr[SHIFT, pl.ds(c, 1), :] = jnp.sum(
                g * shifted * qkv_ref[2, rows], axis=0, keepdims=True
            )
            ur = stack_masked(urev_ref[rows, :].astype(jnp.float32), masks_rev)
            cross = mm(ur, stack_masked(g, masks), TN)
            skew = pltpu.roll(jnp.where(corner, cross, 0.0), 1, axis=1, stride=1, stride_axis=0)
            gr_scr[pl.ds(c, 1), :] = jnp.sum(skew, axis=0, keepdims=True)
            pp = pp_ref[pl.ds(pl.multiple_of(c * LANES, LANES), LANES), :]
            h_scr[rows, :] = mm((g * live).astype(jnp.bfloat16), pp)
        return 0

    lax.fori_loop(0, chans // un, grad_step, 0)
    across = e_scr[0:chans, :]
    b_ext = b_scr[0:chans, :]
    c_ext = c_scr[0:chans, :]
    zero = jnp.zeros((chans, LANES), jnp.float32)
    adj, acc_out, acc_in, acc_carry = zero, zero, zero, zero
    for b in range(nb - 1, -1, -1):
        here = pl.ds(b, chans, stride=nb)
        h = h_scr[here, :]
        s = s_ref[here, :]
        acc_out = acc_out + s * h
        acc_in = acc_in + (adj + pltpu.roll(adj, ns, axis=1)) * f_ref[here, :]
        acc_carry = acc_carry + carry[b : b + 1, :] * adj * s
        x_scr[here, :] = b_ext * adj
        adj = c_ext * h + across * carry[b : b + 1, :] * adj

    def back_step(i, _):
        for j in range(un):
            c = i * un + j
            rows = pl.ds(pl.multiple_of(c * nb, nb), nb)
            t = toeplitz(kern_ref[pl.ds(c, 1), :])
            g = g_scr[rows, :]
            inner = merge_masked(mm(stack_masked(g, masks), t, NT), masks)
            pp = pp_ref[pl.ds(pl.multiple_of(c * LANES, LANES), LANES), :]
            dur_scr[rows, :] = (mm(x_scr[rows, :].astype(jnp.bfloat16), pp, NT) * keep_rev).astype(jnp.bfloat16)
            g_scr[rows, :] = inner + skip_ref[0, c] * g
        return 0

    lax.fori_loop(0, chans // un, back_step, 0)
    step_rows = 16 * nb

    def rev_step(i, _):
        rows = pl.ds(pl.multiple_of(i * step_rows, step_rows), step_rows)
        dui_scr[rows, :] = mm(dur_scr[rows, :], flip)
        return 0

    lax.fori_loop(0, chans // 16, rev_step, 0)

    def last_step(i, _):
        for j in range(un):
            c = i * un + j
            rows = pl.ds(pl.multiple_of(c * nb, nb), nb)
            du = g_scr[rows, :] + dui_scr[rows, :]
            dv_scr[rows, :] = du * sh_scr[rows, :]
            ds = du * qkv_ref[2, rows]
            k = qkv_ref[1, rows]
            lane = iota(k.shape, 1)
            red_scr[0, pl.ds(c, 1), :] = jnp.sum(ds * k, axis=0, keepdims=True)
            dk = sw_ref[0, c] * ds
            for lag, prior in enumerate(priors(k, same)):
                red_scr[lag + 1, pl.ds(c, 1), :] = jnp.sum(ds * prior, axis=0, keepdims=True)
                d = ds * same[lag]
                r = pltpu.roll(d, LANES - (lag + 1), axis=1)
                r2 = pltpu.roll(r, nb - 1, axis=0)
                dk = dk + sw_ref[lag + 1, c] * jnp.where(lane < LANES - (lag + 1), r, r2)
            dk_scr[rows, :] = dk
        return 0

    lax.fori_loop(0, chans // un, last_step, 0)
    for b in range(nb):
        half = b % 2
        for i, scr in enumerate((dq_scr, dk_scr, dv_scr)):
            dqkv_ref[b // 2, i, :, half * LANES : (half + 1) * LANES] = scr[
                pl.ds(b, chans, stride=nb), :
            ].astype(jnp.bfloat16)
    for j in range(SHIFT):
        dsw_ref[j : j + 1, :] = jnp.sum(red_scr[j].T, axis=0, keepdims=True)[:, 0:chans]
    dskip_ref[...] = jnp.sum(red_scr[SHIFT].T, axis=0, keepdims=True)[:, 0:chans]
    tscr[...] = gr_scr[...].T

    def kern_back(i, carried):
        e, zeroth, first = carried
        block = tscr[pl.ds(pl.multiple_of(i * 8, 8), 8), 0:chans]
        for j in range(8):
            term = e * block[j : j + 1, :]
            zeroth = zeroth + term
            first = first + term * (i * 8 + j).astype(jnp.float32)
            e = e * decay
        return e, zeroth, first

    blank = jnp.zeros((ns, chans), jnp.float32)
    _, zeroth, first = lax.fori_loop(0, LANES // 8, kern_back, (blank + 1.0, blank, blank))

    def back(x):
        tscr[...] = jnp.zeros_like(tscr)
        tscr[0:chans, :] = x
        y = tscr[...].T
        return y[0:ns, 0:chans], y[ns : 2 * ns, 0:chans]

    d_out, s_h1 = back(acc_out)
    d_inp, ds_f1 = back(acc_in)
    d_carry, _ = back(acc_carry)
    dinb_ref[...] = decay * d_inp + out_c * zeroth
    doutc_ref[...] = d_out + in_b * zeroth
    drate_ref[...] = -(
        out_c * s_h1
        + in_b * decay * (ds_f1 + d_inp)
        + LANES * jnp.exp(-rate * LANES) * d_carry
        + in_b * out_c * first
    )


def mixer_bwd(gm, qkv, core, s, f, urev, pp, kern, seg, shift_w, skip, rate, in_b, out_c, un=4):
    ns, chans = rate.shape
    rows = qkv.shape[1]
    nb = rows // chans
    f32, bf16 = jnp.float32, jnp.bfloat16
    sds = jax.ShapeDtypeStruct
    vm = pl.BlockSpec(memory_space=pltpu.VMEM)
    sm = pl.BlockSpec(memory_space=pltpu.SMEM)
    sq = pltpu.VMEM((LANES, LANES), f32)
    full = pltpu.VMEM((rows, LANES), f32)
    half = pltpu.VMEM((rows, LANES), bf16)
    return pl.pallas_call(
        functools.partial(mixer_bwd_kernel, un),
        out_shape=(
            sds((nb // 2, 3, chans, 2 * LANES), bf16),
            sds((SHIFT, chans), f32),
            sds((ns, chans), f32),
            sds((ns, chans), f32),
            sds((ns, chans), f32),
            sds((1, chans), f32),
        ),
        in_specs=[vm] * 9 + [sm, sm, vm, vm, vm],
        out_specs=(vm,) * 6,
        scratch_shapes=[
            sq, sq, sq, sq, full, full, full, full, half, full, full, full, full, sq,
            pltpu.VMEM((SHIFT + 1, LANES, LANES), f32),
        ],
        compiler_params=pltpu.CompilerParams(vmem_limit_bytes=56 << 20),
        name="mixer_bwd",
    )(gm, qkv, core, s, f, urev, pp, kern, seg, shift_w, skip, rate, in_b, out_c)


from jax.sharding import PartitionSpec as P

GROUP = ("head", "tensor")


def norm_stats(x):
    centred = x - jnp.mean(x, axis=0, keepdims=True)
    spread = jnp.mean(centred * centred, axis=0, keepdims=True)
    inv = lax.rsqrt(spread + 1e-05)
    return centred * inv, inv


def norm_back(grad, gain, hat, inv):
    scaled = grad * gain
    return inv * (
        scaled
        - jnp.mean(scaled, axis=0, keepdims=True)
        - hat * jnp.mean(scaled * hat, axis=0, keepdims=True)
    )


def lanes_sum(x):
    return jnp.sum(x, axis=1)


def gelu_pair(pre):
    cdf = 0.5 * (1.0 + lax.erf(pre * 0.7071067811865476))
    return pre * cdf, cdf + pre * (0.3989422804014327 * jnp.exp(-0.5 * pre * pre))


def on_device(
    tokens, seg_ids, norm1_gain, norm1_bias, norm2_gain, norm2_bias, q_weight, k_weight, v_weight,
    out_weight, up_weight, down_weight, shift_weight, decay_rate, in_coef, out_coef, skip_coef, cotangent,
):
    bf16, f32 = jnp.bfloat16, jnp.float32
    chans = q_weight.shape[1]
    own = tokens.shape[0]
    feats = tokens.shape[1]
    gather = lambda w: lax.all_gather(w, "dp", axis=0, tiled=True)
    w_joint = gather(jnp.concatenate([q_weight, k_weight, v_weight], axis=1))
    w_out = lax.all_gather(gather(out_weight), GROUP, axis=1, tiled=True)
    w_up, w_down = gather(up_weight), gather(down_weight)
    group_gather = lambda x: lax.all_gather(x, GROUP, axis=0, tiled=False)
    scatter = lambda x: lax.psum_scatter(x, GROUP, scatter_dimension=0, tiled=False).astype(f32)
    swap = lambda x: lax.all_to_all(x, GROUP, split_axis=0, concat_axis=0, tiled=True)
    x = tokens.T.astype(f32)
    g = cotangent.T
    column = lambda v: v[:, None]
    hat1, inv1 = norm_stats(x)
    xn1 = group_gather((hat1 * column(norm1_gain) + column(norm1_bias)).astype(bf16))
    cot = group_gather(g)
    group = xn1.shape[0]
    qkv = jnp.einsum("gdt,dc->cgt", xn1, w_joint, preferred_element_type=f32)
    qkv = qkv.reshape(3, chans * group * own // LANES, LANES)
    mixed, *saved = mixer_fwd(
        qkv, seg_ids, shift_weight, skip_coef[None], decay_rate, in_coef, out_coef, un=16
    )
    mixed = swap(mixed).reshape(group * chans, own)
    hidden = x + jnp.dot(w_out, mixed, preferred_element_type=f32)
    hat2, inv2 = norm_stats(hidden)
    xn2 = group_gather((hat2 * column(norm2_gain) + column(norm2_bias)).astype(bf16))
    pre = jnp.einsum("gdt,df->gft", xn2, w_up, preferred_element_type=f32)
    act, slope = gelu_pair(pre)
    act = act.astype(bf16)
    grad_act = jnp.einsum("gdt,df->gft", cot, w_down, preferred_element_type=f32)
    grad_pre = (grad_act * slope).astype(bf16)
    mlp = scatter(jnp.einsum("gft,df->gdt", act, w_down, preferred_element_type=f32).astype(bf16))
    grad_xn2 = scatter(
        jnp.einsum("gft,df->gdt", grad_pre, w_up, preferred_element_type=f32).astype(bf16)
    )
    grad_down = jnp.einsum("gdt,gft->df", cot, act, preferred_element_type=f32)
    grad_up = jnp.einsum("gdt,gft->df", xn2, grad_pre, preferred_element_type=f32)
    result = (hidden + mlp).astype(bf16).T
    grad_hidden = g.astype(f32) + norm_back(grad_xn2, column(norm2_gain), hat2, inv2)
    gain2, bias2 = lanes_sum(grad_xn2 * hat2), lanes_sum(grad_xn2)
    grad_mix = grad_hidden.astype(bf16)
    grad_mixed = lax.dot_general(w_out, grad_mix, TN, preferred_element_type=f32).astype(bf16)
    grad_out = lax.dot_general(grad_mix, mixed, NT, preferred_element_type=f32)
    grad_out = lax.psum_scatter(grad_out.astype(bf16), GROUP, scatter_dimension=1, tiled=True)
    grad_mixed = swap(grad_mixed.reshape(group, chans, own))
    dqkv, dshift, drate, dinb, doutc, dskip = mixer_bwd(
        grad_mixed, qkv, *saved, seg_ids, shift_weight, skip_coef[None], decay_rate, in_coef, out_coef, un=16
    )
    dqkv = dqkv.reshape(group, 3 * chans, own)
    grad_w = jnp.einsum("gdt,gct->dc", xn1, dqkv, preferred_element_type=f32)
    grad_xn1 = scatter(
        jnp.einsum("gct,dc->gdt", dqkv, w_joint, preferred_element_type=f32).astype(bf16)
    )
    grad_x = (grad_hidden + norm_back(grad_xn1, column(norm1_gain), hat1, inv1)).T
    gain1, bias1 = lanes_sum(grad_xn1 * hat1), lanes_sum(grad_xn1)
    reduce = lambda v: lax.psum_scatter(v, "dp", scatter_dimension=0, tiled=True)
    grad_w = reduce(grad_w)
    sums = lax.psum((dshift, drate, dinb, doutc, dskip[0]), "dp")
    norms = lax.psum((gain1, bias1, gain2, bias2), ("dp", "head", "tensor"))
    return (
        result, grad_x, *norms, grad_w[:, :chans], grad_w[:, chans : 2 * chans], grad_w[:, 2 * chans :],
        reduce(grad_out.astype(f32)), reduce(grad_up), reduce(grad_down), *sums,
    )


def solution(mesh):
    rows = P(("dp", "head", "tensor"), None)
    weight = P("dp", GROUP)
    chan = P(None, GROUP)
    in_specs = (rows, P("dp", None)) + (P(),) * 4 + (weight,) * 6 + (chan,) * 4 + (P(GROUP), rows)
    out_specs = (rows, rows) + (P(),) * 4 + (weight,) * 6 + (chan,) * 4 + (P(GROUP),)
    return jax.shard_map(on_device, mesh=mesh, in_specs=in_specs, out_specs=out_specs, check_vma=False)
```

```python
import functools
import jax, jax.numpy as jnp
from jax import lax
from jax.experimental import pallas as pl
from jax.experimental.pallas import tpu as pltpu

LANES = 128
SHIFT = 4
SEQS = 3
NT = (((1,), (1,)), ((), ()))
TN = (((0,), (0,)), ((), ()))
NN = (((1,), (0,)), ((), ()))


def mm(left, right, dims=NN):
    return lax.dot_general(left, right, dims, preferred_element_type=jnp.float32)


def iota(shape, axis):
    return lax.broadcasted_iota(jnp.int32, shape, axis)


def seg_masks(seg, nb):
    lane = iota((nb, LANES), 1)
    row = iota((nb, LANES), 0)
    masks = [(seg == k).astype(jnp.float32) for k in range(SEQS)]
    end = jnp.broadcast_to(seg[:, LANES - 1 :], (nb, LANES))
    last = jnp.where(row == 0, -1, pltpu.roll(end, 1, axis=0))
    live = (seg == last).astype(jnp.float32)
    keep = (seg == end).astype(jnp.float32)
    carry = (end == last).astype(jnp.float32)
    same = []
    for j in range(1, SHIFT):
        r = pltpu.roll(seg, j, axis=1)
        r2 = pltpu.roll(r, 1, axis=0)
        prior = jnp.where(lane < j, r2, r)
        ok = (prior == seg) & ((row > 0) | (lane >= j))
        same.append(ok.astype(jnp.float32))
    return masks, live, keep, carry, same


def priors(k, same):
    lane = iota(k.shape, 1)
    out = []
    for j in range(1, SHIFT):
        r = pltpu.roll(k, j, axis=1)
        r2 = pltpu.roll(r, 1, axis=0)
        out.append(jnp.where(lane < j, r2, r) * same[j - 1])
    return out


def flip_matrix():
    return (iota((LANES, LANES), 0) + iota((LANES, LANES), 1) == LANES - 1).astype(jnp.bfloat16)


def read_seg(seg_ref, nb):
    return jnp.concatenate([seg_ref[:, b * LANES : (b + 1) * LANES] for b in range(nb)], axis=0)


def transposed(scr, top, bottom):
    ns, chans = top.shape
    scr[...] = jnp.zeros_like(scr)
    scr[0:ns, 0:chans] = top
    if bottom is not None:
        scr[ns : 2 * ns, 0:chans] = bottom
    return scr[...].T


def stack_masked(x, masks):
    return jnp.concatenate([x * m for m in masks], axis=0).astype(jnp.bfloat16)


def merge_masked(y, masks):
    nb = masks[0].shape[0]
    return sum(y[i * nb : (i + 1) * nb] * m for i, m in enumerate(masks))


def toeplitz(krow):
    t = pltpu.roll(jnp.broadcast_to(krow, (LANES, LANES)), 0, axis=1, stride=1, stride_axis=0)
    return jnp.where(iota((LANES, LANES), 1) >= iota((LANES, LANES), 0), t, 0.0).astype(jnp.bfloat16)


def mixer_fwd_kernel(
    un, qkv_ref, seg_ref, sw_ref, skip_ref, rate_ref, inb_ref, outc_ref,
    mixed_ref, core_ref, s_ref, f_ref, urev_ref, pp_ref, kern_ref,
    tscr, a_scr, b_scr, c_scr, e_scr, u_scr, kscr,
):
    ns, chans = rate_ref.shape
    nb = qkv_ref.shape[1] // chans
    masks, live, keep, carry, same = seg_masks(read_seg(seg_ref, nb), nb)
    flip = flip_matrix()
    keep_rev = mm(keep.astype(jnp.bfloat16), flip)
    rate, in_b, out_c = rate_ref[...], inb_ref[...], outc_ref[...]
    decay = jnp.exp(-rate)
    a_scr[...] = transposed(tscr, rate, rate)
    b_scr[...] = transposed(tscr, in_b * decay, None)
    c_scr[...] = transposed(tscr, out_c, None)
    e_scr[...] = transposed(tscr, jnp.exp(-rate * LANES), None)

    def kern_step(i, e):
        for j in range(8):
            kscr[pl.ds(i * 8 + j, 1), 0:chans] = jnp.sum(e, axis=0, keepdims=True)
            e = e * decay
        return e

    kscr[...] = jnp.zeros_like(kscr)
    lax.fori_loop(0, LANES // 8, kern_step, in_b * out_c)
    kern_ref[...] = kscr[...].T[0:chans]

    def drive_step(i, _):
        for j in range(un):
            c = i * un + j
            rows = pl.ds(pl.multiple_of(c * nb, nb), nb)
            k = qkv_ref[1, rows]
            shifted = sw_ref[0, c] * k
            for lag, prior in enumerate(priors(k, same)):
                shifted = shifted + sw_ref[lag + 1, c] * prior
            u_scr[rows, :] = shifted * qkv_ref[2, rows]
        return 0

    lax.fori_loop(0, chans // un, drive_step, 0)
    step_rows = 16 * nb

    def rev_step(i, _):
        rows = pl.ds(pl.multiple_of(i * step_rows, step_rows), step_rows)
        urev_ref[rows, :] = mm(u_scr[rows, :].astype(jnp.bfloat16), flip).astype(jnp.bfloat16)
        return 0

    lax.fori_loop(0, chans // 16, rev_step, 0)
    pos = iota((LANES, LANES), 0).astype(jnp.float32)
    factor = jnp.where(iota((LANES, LANES), 1) < ns, 1.0, pos)
    i8 = iota((8, LANES), 0).astype(jnp.float32)
    i16 = iota((LANES // 8, LANES), 0).astype(jnp.float32) * 8.0

    def fresh_step(i, _):
        for j in range(un):
            c = i * un + j
            rows = pl.ds(pl.multiple_of(c * nb, nb), nb)
            a = a_scr[pl.ds(c, 1), :]
            base = jnp.exp(-a * i8)
            tall = jnp.exp(-a * i16)
            p = (tall[:, None, :] * base[None]).reshape(LANES, LANES)
            pp = (p * factor).astype(jnp.bfloat16)
            pp_ref[pl.ds(pl.multiple_of(c * LANES, LANES), LANES), :] = pp
            urk = (urev_ref[rows, :].astype(jnp.float32) * keep_rev).astype(jnp.bfloat16)
            f_ref[rows, :] = mm(urk, pp)
        return 0

    lax.fori_loop(0, chans // un, fresh_step, 0)
    across = e_scr[0:chans, :]
    b_ext = b_scr[0:chans, :]
    state = jnp.zeros((chans, LANES), jnp.float32)
    for b in range(nb):
        s_ref[pl.ds(b, chans, stride=nb), :] = state + pltpu.roll(state, ns, axis=1)
        fresh = f_ref[pl.ds(b, chans, stride=nb), :]
        state = across * carry[b : b + 1, :] * state + b_ext * fresh

    def out_step(i, _):
        for j in range(un):
            c = i * un + j
            rows = pl.ds(pl.multiple_of(c * nb, nb), nb)
            t = toeplitz(kern_ref[pl.ds(c, 1), :])
            u = u_scr[rows, :]
            y = merge_masked(mm(stack_masked(u, masks), t), masks)
            sc = (s_ref[rows, :] * c_scr[pl.ds(c, 1), :]).astype(jnp.bfloat16)
            pp = pp_ref[pl.ds(pl.multiple_of(c * LANES, LANES), LANES), :]
            core = y + live * mm(sc, pp, NT) + skip_ref[0, c] * u
            core_ref[rows, :] = core
            u_scr[rows, :] = qkv_ref[0, rows] * core
        return 0

    lax.fori_loop(0, chans // un, out_step, 0)
    for b in range(nb):
        half = b % 2
        mixed_ref[b // 2, :, half * LANES : (half + 1) * LANES] = u_scr[
            pl.ds(b, chans, stride=nb), :
        ].astype(jnp.bfloat16)


def mixer_fwd(qkv, seg, shift_w, skip, rate, in_b, out_c, un=4):
    ns, chans = rate.shape
    rows = qkv.shape[1]
    nb = rows // chans
    f32, bf16 = jnp.float32, jnp.bfloat16
    sds = jax.ShapeDtypeStruct
    vm = pl.BlockSpec(memory_space=pltpu.VMEM)
    sm = pl.BlockSpec(memory_space=pltpu.SMEM)
    sq = pltpu.VMEM((LANES, LANES), f32)
    return pl.pallas_call(
        functools.partial(mixer_fwd_kernel, un),
        out_shape=(
            sds((nb // 2, chans, 2 * LANES), bf16),
            sds((rows, LANES), f32),
            sds((rows, LANES), f32),
            sds((rows, LANES), f32),
            sds((rows, LANES), bf16),
            sds((chans * LANES, LANES), bf16),
            sds((chans, LANES), f32),
        ),
        in_specs=[vm, vm, sm, sm, vm, vm, vm],
        out_specs=(vm,) * 7,
        scratch_shapes=[sq, sq, sq, sq, sq, pltpu.VMEM((rows, LANES), f32), sq],
        compiler_params=pltpu.CompilerParams(vmem_limit_bytes=48 << 20),
        name="mixer_fwd",
    )(qkv, seg, shift_w, skip, rate, in_b, out_c)


def mixer_bwd_kernel(
    un, gm_ref, qkv_ref, core_ref, s_ref, f_ref, urev_ref, pp_ref, kern_ref, seg_ref,
    sw_ref, skip_ref, rate_ref, inb_ref, outc_ref,
    dqkv_ref, dsw_ref, drate_ref, dinb_ref, doutc_ref, dskip_ref,
    tscr, b_scr, c_scr, e_scr, g_scr, sh_scr, h_scr, x_scr, dur_scr, dui_scr, dq_scr, dk_scr, dv_scr, gr_scr, red_scr,
):
    ns, chans = rate_ref.shape
    nb = qkv_ref.shape[1] // chans
    masks, live, keep, carry, same = seg_masks(read_seg(seg_ref, nb), nb)
    flip = flip_matrix()
    keep_rev = mm(keep.astype(jnp.bfloat16), flip)
    masks_rev = [mm(m.astype(jnp.bfloat16), flip) for m in masks]
    rate, in_b, out_c = rate_ref[...], inb_ref[...], outc_ref[...]
    decay = jnp.exp(-rate)
    b_scr[...] = transposed(tscr, in_b * decay, None)
    c_scr[...] = transposed(tscr, out_c, None)
    e_scr[...] = transposed(tscr, jnp.exp(-rate * LANES), None)
    red_scr[...] = jnp.zeros_like(red_scr)
    gr_scr[...] = jnp.zeros_like(gr_scr)

    for b in range(nb):
        half = b % 2
        x_scr[pl.ds(b, chans, stride=nb), :] = gm_ref[
            b // 2, :, half * LANES : (half + 1) * LANES
        ].astype(jnp.float32)
    corner = iota((LANES, LANES), 0) + iota((LANES, LANES), 1) >= LANES - 1

    def grad_step(i, _):
        for j in range(un):
            c = i * un + j
            rows = pl.ds(pl.multiple_of(c * nb, nb), nb)
            gm = x_scr[rows, :]
            dq_scr[rows, :] = gm * core_ref[rows, :]
            g = gm * qkv_ref[0, rows]
            g_scr[rows, :] = g
            k = qkv_ref[1, rows]
            shifted = sw_ref[0, c] * k
            for lag, prior in enumerate(priors(k, same)):
                shifted = shifted + sw_ref[lag + 1, c] * prior
            sh_scr[rows, :] = shifted
            red_scr[SHIFT, pl.ds(c, 1), :] = jnp.sum(
                g * shifted * qkv_ref[2, rows], axis=0, keepdims=True
            )
            ur = stack_masked(urev_ref[rows, :].astype(jnp.float32), masks_rev)
            cross = mm(ur, stack_masked(g, masks), TN)
            skew = pltpu.roll(jnp.where(corner, cross, 0.0), 1, axis=1, stride=1, stride_axis=0)
            gr_scr[pl.ds(c, 1), :] = jnp.sum(skew, axis=0, keepdims=True)
            pp = pp_ref[pl.ds(pl.multiple_of(c * LANES, LANES), LANES), :]
            h_scr[rows, :] = mm((g * live).astype(jnp.bfloat16), pp)
        return 0

    lax.fori_loop(0, chans // un, grad_step, 0)
    across = e_scr[0:chans, :]
    b_ext = b_scr[0:chans, :]
    c_ext = c_scr[0:chans, :]
    zero = jnp.zeros((chans, LANES), jnp.float32)
    adj, acc_out, acc_in, acc_carry = zero, zero, zero, zero
    for b in range(nb - 1, -1, -1):
        here = pl.ds(b, chans, stride=nb)
        h = h_scr[here, :]
        s = s_ref[here, :]
        acc_out = acc_out + s * h
        acc_in = acc_in + (adj + pltpu.roll(adj, ns, axis=1)) * f_ref[here, :]
        acc_carry = acc_carry + carry[b : b + 1, :] * adj * s
        x_scr[here, :] = b_ext * adj
        adj = c_ext * h + across * carry[b : b + 1, :] * adj

    def back_step(i, _):
        for j in range(un):
            c = i * un + j
            rows = pl.ds(pl.multiple_of(c * nb, nb), nb)
            t = toeplitz(kern_ref[pl.ds(c, 1), :])
            g = g_scr[rows, :]
            inner = merge_masked(mm(stack_masked(g, masks), t, NT), masks)
            pp = pp_ref[pl.ds(pl.multiple_of(c * LANES, LANES), LANES), :]
            dur_scr[rows, :] = (mm(x_scr[rows, :].astype(jnp.bfloat16), pp, NT) * keep_rev).astype(jnp.bfloat16)
            g_scr[rows, :] = inner + skip_ref[0, c] * g
        return 0

    lax.fori_loop(0, chans // un, back_step, 0)
    step_rows = 16 * nb

    def rev_step(i, _):
        rows = pl.ds(pl.multiple_of(i * step_rows, step_rows), step_rows)
        dui_scr[rows, :] = mm(dur_scr[rows, :], flip)
        return 0

    lax.fori_loop(0, chans // 16, rev_step, 0)

    def last_step(i, _):
        for j in range(un):
            c = i * un + j
            rows = pl.ds(pl.multiple_of(c * nb, nb), nb)
            du = g_scr[rows, :] + dui_scr[rows, :]
            dv_scr[rows, :] = du * sh_scr[rows, :]
            ds = du * qkv_ref[2, rows]
            k = qkv_ref[1, rows]
            lane = iota(k.shape, 1)
            red_scr[0, pl.ds(c, 1), :] = jnp.sum(ds * k, axis=0, keepdims=True)
            dk = sw_ref[0, c] * ds
            for lag, prior in enumerate(priors(k, same)):
                red_scr[lag + 1, pl.ds(c, 1), :] = jnp.sum(ds * prior, axis=0, keepdims=True)
                d = ds * same[lag]
                r = pltpu.roll(d, LANES - (lag + 1), axis=1)
                r2 = pltpu.roll(r, nb - 1, axis=0)
                dk = dk + sw_ref[lag + 1, c] * jnp.where(lane < LANES - (lag + 1), r, r2)
            dk_scr[rows, :] = dk
        return 0

    lax.fori_loop(0, chans // un, last_step, 0)
    for b in range(nb):
        half = b % 2
        for i, scr in enumerate((dq_scr, dk_scr, dv_scr)):
            dqkv_ref[b // 2, i, :, half * LANES : (half + 1) * LANES] = scr[
                pl.ds(b, chans, stride=nb), :
            ].astype(jnp.bfloat16)
    for j in range(SHIFT):
        dsw_ref[j : j + 1, :] = jnp.sum(red_scr[j].T, axis=0, keepdims=True)[:, 0:chans]
    dskip_ref[...] = jnp.sum(red_scr[SHIFT].T, axis=0, keepdims=True)[:, 0:chans]
    tscr[...] = gr_scr[...].T

    def kern_back(i, carried):
        e, zeroth, first = carried
        block = tscr[pl.ds(pl.multiple_of(i * 8, 8), 8), 0:chans]
        for j in range(8):
            term = e * block[j : j + 1, :]
            zeroth = zeroth + term
            first = first + term * (i * 8 + j).astype(jnp.float32)
            e = e * decay
        return e, zeroth, first

    blank = jnp.zeros((ns, chans), jnp.float32)
    _, zeroth, first = lax.fori_loop(0, LANES // 8, kern_back, (blank + 1.0, blank, blank))

    def back(x):
        tscr[...] = jnp.zeros_like(tscr)
        tscr[0:chans, :] = x
        y = tscr[...].T
        return y[0:ns, 0:chans], y[ns : 2 * ns, 0:chans]

    d_out, s_h1 = back(acc_out)
    d_inp, ds_f1 = back(acc_in)
    d_carry, _ = back(acc_carry)
    dinb_ref[...] = decay * d_inp + out_c * zeroth
    doutc_ref[...] = d_out + in_b * zeroth
    drate_ref[...] = -(
        out_c * s_h1
        + in_b * decay * (ds_f1 + d_inp)
        + LANES * jnp.exp(-rate * LANES) * d_carry
        + in_b * out_c * first
    )


def mixer_bwd(gm, qkv, core, s, f, urev, pp, kern, seg, shift_w, skip, rate, in_b, out_c, un=4):
    ns, chans = rate.shape
    rows = qkv.shape[1]
    nb = rows // chans
    f32, bf16 = jnp.float32, jnp.bfloat16
    sds = jax.ShapeDtypeStruct
    vm = pl.BlockSpec(memory_space=pltpu.VMEM)
    sm = pl.BlockSpec(memory_space=pltpu.SMEM)
    sq = pltpu.VMEM((LANES, LANES), f32)
    full = pltpu.VMEM((rows, LANES), f32)
    half = pltpu.VMEM((rows, LANES), bf16)
    return pl.pallas_call(
        functools.partial(mixer_bwd_kernel, un),
        out_shape=(
            sds((nb // 2, 3, chans, 2 * LANES), bf16),
            sds((SHIFT, chans), f32),
            sds((ns, chans), f32),
            sds((ns, chans), f32),
            sds((ns, chans), f32),
            sds((1, chans), f32),
        ),
        in_specs=[vm] * 9 + [sm, sm, vm, vm, vm],
        out_specs=(vm,) * 6,
        scratch_shapes=[
            sq, sq, sq, sq, full, full, full, full, half, full, full, full, full, sq,
            pltpu.VMEM((SHIFT + 1, LANES, LANES), f32),
        ],
        compiler_params=pltpu.CompilerParams(vmem_limit_bytes=56 << 20),
        name="mixer_bwd",
    )(gm, qkv, core, s, f, urev, pp, kern, seg, shift_w, skip, rate, in_b, out_c)


MESH = pl.DeviceIdType.MESH


class Place:
    def __init__(self, n_dp, n_head, n_tensor):
        self.n_dp, self.n_head, self.n_tensor = n_dp, n_head, n_tensor
        self.dp = lax.axis_index("dp")
        h, t = lax.axis_index("head"), lax.axis_index("tensor")
        self.size = n_head * n_tensor
        ph, xh, yt = h + 1 - 2 * (h % 2), (h + 2) % n_head, 1 - t
        pxh = (ph + 2) % n_head
        slot = lambda a, b: a * n_tensor + b
        self.me, self.p, self.x, self.y, self.d = (
            slot(h, t), slot(ph, t), slot(xh, t), slot(h, yt), slot(xh, yt),
        )
        self.px, self.py, self.pd = slot(pxh, t), slot(ph, yt), slot(pxh, yt)
        self.to_p, self.to_x, self.to_y = {"head": ph}, {"head": xh}, {"tensor": yt}

    def dp_peer(self, step):
        return (self.dp + step) % self.n_dp

    def barrier(self, over_dp):
        sem = pltpu.get_barrier_semaphore()
        for where in (self.to_p, self.to_x, self.to_y):
            pl.semaphore_signal(sem, inc=1, device_id=where, device_id_type=MESH)
        count = 3
        if over_dp:
            def greet(step, _):
                pl.semaphore_signal(
                    sem, inc=1, device_id={"dp": self.dp_peer(step)}, device_id_type=MESH
                )
                return 0

            lax.fori_loop(1, self.n_dp, greet, 0)
            count += self.n_dp - 1
        pl.semaphore_wait(sem, count)


def remote(src, dst, ssem, rsem, where):
    return pltpu.make_async_remote_copy(
        src_ref=src, dst_ref=dst, send_sem=ssem, recv_sem=rsem, device_id=where, device_id_type=MESH
    )


class GroupGather:
    COPIES = 9

    def __init__(self, place, ref, ssem, rsem):
        self.ssem, self.rsem = ssem, rsem
        half = ref.shape[1] // 2
        top, low = pl.ds(0, half), pl.ds(half, half)
        pc = place
        full = lambda s: ref.at[s]
        part = lambda s, rows: ref.at[s, rows]
        self.out = [
            (full(pc.me), pc.to_p), (full(pc.me), pc.to_x), (full(pc.me), pc.to_y),
            (part(pc.x, top), pc.to_y), (part(pc.y, low), pc.to_x),
            (full(pc.x), pc.to_p), (full(pc.y), pc.to_p),
            (part(pc.d, top), pc.to_p), (part(pc.d, low), pc.to_p),
        ]
        self.into = [
            full(pc.p), full(pc.x), full(pc.y), part(pc.d, top), part(pc.d, low),
            full(pc.px), full(pc.py), part(pc.pd, top), part(pc.pd, low),
        ]

    def send(self, *which):
        for i in which:
            src, where = self.out[i]
            remote(src, src, self.ssem.at[i], self.rsem.at[i], where).start()

    def arrive(self, *which):
        for i in which:
            dst = self.into[i]
            remote(dst, dst, self.ssem.at[i], self.rsem.at[i], self.out[i][1]).wait_recv()

    def start(self):
        self.send(1, 2, 0)

    def middle(self):
        self.arrive(1, 2)
        self.send(3, 4, 5, 6)

    def late(self):
        self.arrive(3, 4)
        self.send(7, 8)

    def finish(self):
        self.arrive(0, 5, 6, 7, 8)

    def drain(self):
        for i in range(self.COPIES):
            src, where = self.out[i]
            remote(src, src, self.ssem.at[i], self.rsem.at[i], where).wait_send()


class DepthGather:
    def __init__(self, place, ref, ssem, rsem):
        self.place, self.ref, self.ssem, self.rsem = place, ref, ssem, rsem

    def _copy(self, step, slot, peer):
        return remote(
            self.ref.at[slot], self.ref.at[slot], self.ssem.at[step], self.rsem.at[step], {"dp": peer}
        )

    def _loop(self, body):
        def step(i, _):
            body(i)
            return 0

        lax.fori_loop(1, self.place.n_dp, step, 0)

    def start(self):
        pc = self.place
        self._loop(lambda i: self._copy(i, pc.dp, pc.dp_peer(i)).start())

    def finish(self):
        pc = self.place
        source = lambda i: (pc.dp + pc.n_dp - i) % pc.n_dp
        self._loop(lambda i: self._copy(i, source(i), pc.dp_peer(i)).wait_recv())

    def drain(self):
        pc = self.place
        self._loop(lambda i: self._copy(i, pc.dp, pc.dp_peer(i)).wait_send())


def joined(ref):
    n, rows, columns = ref.shape
    if rows % 16 == 0:
        return ref[...].reshape(n * rows, columns)
    parts = [ref[j].astype(jnp.float32) for j in range(n)]
    return jnp.concatenate(parts, axis=0).astype(ref.dtype)


def row_norm(x):
    centred = x - jnp.mean(x, axis=1, keepdims=True)
    inv = lax.rsqrt(jnp.mean(centred * centred, axis=1, keepdims=True) + 1e-05)
    return centred * inv, inv


def first_kernel(
    axes, tok_ref, cot_ref, gain_ref, bias_ref, qkvo_ref, up_ref,
    xn_all, cot_all, qkv_ref, wqkvo_all, wup_all, wupt_ref, wout_all,
    wt_scr, gs, gr, cs, cr, os, orr, zs, zr, lsem,
):
    pc = Place(*axes)
    pc.barrier(True)
    chans = wout_all.shape[1]
    own = tok_ref.shape[0]
    keep_qkvo = pltpu.make_async_copy(qkvo_ref, wqkvo_all.at[pc.dp], lsem.at[0])
    keep_up = pltpu.make_async_copy(up_ref, wup_all.at[pc.dp], lsem.at[1])
    keep_qkvo.start()
    keep_up.start()
    z_qkvo = DepthGather(pc, wqkvo_all, zs.at[0], zr.at[0])
    z_up = DepthGather(pc, wup_all, zs.at[1], zr.at[1])
    xn_g = GroupGather(pc, xn_all, gs, gr)
    cot_g = GroupGather(pc, cot_all, cs, cr)
    out_g = GroupGather(pc, wout_all, os, orr)
    keep_qkvo.wait()
    z_qkvo.start()
    keep_up.wait()
    z_up.start()
    hat, _ = row_norm(tok_ref[...].astype(jnp.float32))
    xn_all[pc.me] = (hat * gain_ref[...] + bias_ref[...]).astype(jnp.bfloat16).T
    xn_g.start()
    cot_all[pc.me] = cot_ref[...].T
    cot_g.start()
    z_qkvo.finish()
    wt_scr[...] = joined(wqkvo_all).T
    wout_all[pc.me] = wt_scr[3 * chans :, :]
    xn_g.middle()
    xn_g.late()
    out_g.start()
    cot_g.middle()
    xn_g.finish()
    for s in range(pc.size):
        y = mm(wt_scr[0 : 3 * chans, :], xn_all[s])
        for h in range(own // LANES):
            qkv_ref[pl.ds(s * (own // LANES) + h, 3 * chans, stride=pc.size * (own // LANES)), :] = y[
                :, h * LANES : (h + 1) * LANES
            ]
    z_up.finish()
    wupt_ref[...] = joined(wup_all).T
    cot_g.late()
    out_g.middle()
    out_g.late()
    cot_g.finish()
    out_g.finish()
    for work in (xn_g, cot_g, out_g, z_qkvo, z_up):
        work.drain()


def first_stage(axes, tokens, cot, gain, bias, qkvo, up):
    n_dp, n_head, n_tensor = axes
    group = n_head * n_tensor
    own, feats = tokens.shape
    chans = qkvo.shape[1] // 4
    f32, bf16 = jnp.float32, jnp.bfloat16
    sds = jax.ShapeDtypeStruct
    vm = pl.BlockSpec(memory_space=pltpu.VMEM)
    dma = pltpu.SemaphoreType.DMA
    return pl.pallas_call(
        functools.partial(first_kernel, axes),
        out_shape=(
            sds((group, feats, own), bf16),
            sds((group, feats, own), bf16),
            sds((3 * chans * group * own // LANES, LANES), f32),
            sds((n_dp,) + qkvo.shape, bf16),
            sds((n_dp,) + up.shape, bf16),
            sds((up.shape[1], feats), bf16),
            sds((group, chans, feats), bf16),
        ),
        in_specs=[vm] * 6,
        out_specs=(vm,) * 7,
        scratch_shapes=[
            pltpu.VMEM((4 * chans, feats), bf16),
            dma((9,)), dma((9,)), dma((9,)), dma((9,)), dma((9,)), dma((9,)),
            dma((2, n_dp)), dma((2, n_dp)), dma((2,)),
        ],
        compiler_params=pltpu.CompilerParams(
            collective_id=1, has_side_effects=True, vmem_limit_bytes=56 << 20
        ),
        name="first_stage",
    )(tokens, cot, gain, bias, qkvo, up)


from jax.sharding import PartitionSpec as P

GROUP = ("head", "tensor")


def norm_stats(x):
    centred = x - jnp.mean(x, axis=0, keepdims=True)
    spread = jnp.mean(centred * centred, axis=0, keepdims=True)
    inv = lax.rsqrt(spread + 1e-05)
    return centred * inv, inv


def norm_back(grad, gain, hat, inv):
    scaled = grad * gain
    return inv * (
        scaled
        - jnp.mean(scaled, axis=0, keepdims=True)
        - hat * jnp.mean(scaled * hat, axis=0, keepdims=True)
    )


def lanes_sum(x):
    return jnp.sum(x, axis=1)


def gelu_pair(pre):
    cdf = 0.5 * (1.0 + lax.erf(pre * 0.7071067811865476))
    return pre * cdf, cdf + pre * (0.3989422804014327 * jnp.exp(-0.5 * pre * pre))


def on_device(
    tokens, seg_ids, norm1_gain, norm1_bias, norm2_gain, norm2_bias, q_weight, k_weight, v_weight,
    out_weight, up_weight, down_weight, shift_weight, decay_rate, in_coef, out_coef, skip_coef, cotangent,
):
    bf16, f32 = jnp.bfloat16, jnp.float32
    chans = q_weight.shape[1]
    axes = (lax.axis_size("dp"), lax.axis_size("head"), lax.axis_size("tensor"))
    own = tokens.shape[0]
    feats = tokens.shape[1]
    gather = lambda w: lax.all_gather(w, "dp", axis=0, tiled=True)
    packed = jnp.concatenate([q_weight, k_weight, v_weight, out_weight], axis=1)
    xn1, cot, qkv, w_packed, w_up, w_up_t, w_out_t = first_stage(
        axes, tokens, cotangent, norm1_gain[None], norm1_bias[None], packed, up_weight
    )
    w_joint = w_packed.reshape(feats, 4 * chans)[:, : 3 * chans]
    w_up = w_up.reshape(feats, -1)
    w_out = w_out_t.reshape(feats, feats).T
    w_down = gather(down_weight)
    group_gather = lambda x: lax.all_gather(x, GROUP, axis=0, tiled=False)
    scatter = lambda x: lax.psum_scatter(x, GROUP, scatter_dimension=0, tiled=False).astype(f32)
    swap = lambda x: lax.all_to_all(x, GROUP, split_axis=0, concat_axis=0, tiled=True)
    x = tokens.T.astype(f32)
    g = cotangent.T
    column = lambda v: v[:, None]
    hat1, inv1 = norm_stats(x)
    group = xn1.shape[0]
    qkv = qkv.reshape(3, chans * group * own // LANES, LANES)
    mixed, *saved = mixer_fwd(
        qkv, seg_ids, shift_weight, skip_coef[None], decay_rate, in_coef, out_coef, un=16
    )
    mixed = swap(mixed).reshape(group * chans, own)
    hidden = x + jnp.dot(w_out, mixed, preferred_element_type=f32)
    hat2, inv2 = norm_stats(hidden)
    xn2 = group_gather((hat2 * column(norm2_gain) + column(norm2_bias)).astype(bf16))
    pre = jnp.einsum("gdt,df->gft", xn2, w_up, preferred_element_type=f32)
    act, slope = gelu_pair(pre)
    act = act.astype(bf16)
    grad_act = jnp.einsum("gdt,df->gft", cot, w_down, preferred_element_type=f32)
    grad_pre = (grad_act * slope).astype(bf16)
    mlp = scatter(jnp.einsum("gft,df->gdt", act, w_down, preferred_element_type=f32).astype(bf16))
    grad_xn2 = scatter(
        jnp.einsum("gft,df->gdt", grad_pre, w_up, preferred_element_type=f32).astype(bf16)
    )
    grad_down = jnp.einsum("gdt,gft->df", cot, act, preferred_element_type=f32)
    grad_up = jnp.einsum("gdt,gft->df", xn2, grad_pre, preferred_element_type=f32)
    result = (hidden + mlp).astype(bf16).T
    grad_hidden = g.astype(f32) + norm_back(grad_xn2, column(norm2_gain), hat2, inv2)
    gain2, bias2 = lanes_sum(grad_xn2 * hat2), lanes_sum(grad_xn2)
    grad_mix = grad_hidden.astype(bf16)
    grad_mixed = lax.dot_general(w_out, grad_mix, TN, preferred_element_type=f32).astype(bf16)
    grad_out = lax.dot_general(grad_mix, mixed, NT, preferred_element_type=f32)
    grad_out = lax.psum_scatter(grad_out.astype(bf16), GROUP, scatter_dimension=1, tiled=True)
    grad_mixed = swap(grad_mixed.reshape(group, chans, own))
    dqkv, dshift, drate, dinb, doutc, dskip = mixer_bwd(
        grad_mixed, qkv, *saved, seg_ids, shift_weight, skip_coef[None], decay_rate, in_coef, out_coef, un=16
    )
    dqkv = dqkv.reshape(group, 3 * chans, own)
    grad_w = jnp.einsum("gdt,gct->dc", xn1, dqkv, preferred_element_type=f32)
    grad_xn1 = scatter(
        jnp.einsum("gct,dc->gdt", dqkv, w_joint, preferred_element_type=f32).astype(bf16)
    )
    grad_x = (grad_hidden + norm_back(grad_xn1, column(norm1_gain), hat1, inv1)).T
    gain1, bias1 = lanes_sum(grad_xn1 * hat1), lanes_sum(grad_xn1)
    reduce = lambda v: lax.psum_scatter(v, "dp", scatter_dimension=0, tiled=True)
    grad_w = reduce(grad_w)
    sums = lax.psum((dshift, drate, dinb, doutc, dskip[0]), "dp")
    norms = lax.psum((gain1, bias1, gain2, bias2), ("dp", "head", "tensor"))
    return (
        result, grad_x, *norms, grad_w[:, :chans], grad_w[:, chans : 2 * chans], grad_w[:, 2 * chans :],
        reduce(grad_out.astype(f32)), reduce(grad_up), reduce(grad_down), *sums,
    )


def solution(mesh):
    rows = P(("dp", "head", "tensor"), None)
    weight = P("dp", GROUP)
    chan = P(None, GROUP)
    in_specs = (rows, P("dp", None)) + (P(),) * 4 + (weight,) * 6 + (chan,) * 4 + (P(GROUP), rows)
    out_specs = (rows, rows) + (P(),) * 4 + (weight,) * 6 + (chan,) * 4 + (P(GROUP),)
    return jax.shard_map(on_device, mesh=mesh, in_specs=in_specs, out_specs=out_specs, check_vma=False)
```

```python
import functools
import jax, jax.numpy as jnp
from jax import lax
from jax.experimental import pallas as pl
from jax.experimental.pallas import tpu as pltpu

LANES = 128
SHIFT = 4
SEQS = 3
NT = (((1,), (1,)), ((), ()))
TN = (((0,), (0,)), ((), ()))
NN = (((1,), (0,)), ((), ()))


def mm(left, right, dims=NN):
    return lax.dot_general(left, right, dims, preferred_element_type=jnp.float32)


def iota(shape, axis):
    return lax.broadcasted_iota(jnp.int32, shape, axis)


def seg_masks(seg, nb):
    lane = iota((nb, LANES), 1)
    row = iota((nb, LANES), 0)
    masks = [(seg == k).astype(jnp.float32) for k in range(SEQS)]
    end = jnp.broadcast_to(seg[:, LANES - 1 :], (nb, LANES))
    last = jnp.where(row == 0, -1, pltpu.roll(end, 1, axis=0))
    live = (seg == last).astype(jnp.float32)
    keep = (seg == end).astype(jnp.float32)
    carry = (end == last).astype(jnp.float32)
    same = []
    for j in range(1, SHIFT):
        r = pltpu.roll(seg, j, axis=1)
        r2 = pltpu.roll(r, 1, axis=0)
        prior = jnp.where(lane < j, r2, r)
        ok = (prior == seg) & ((row > 0) | (lane >= j))
        same.append(ok.astype(jnp.float32))
    return masks, live, keep, carry, same


def priors(k, same):
    lane = iota(k.shape, 1)
    out = []
    for j in range(1, SHIFT):
        r = pltpu.roll(k, j, axis=1)
        r2 = pltpu.roll(r, 1, axis=0)
        out.append(jnp.where(lane < j, r2, r) * same[j - 1])
    return out


def flip_matrix():
    return (iota((LANES, LANES), 0) + iota((LANES, LANES), 1) == LANES - 1).astype(jnp.bfloat16)


def read_seg(seg_ref, nb):
    return jnp.concatenate([seg_ref[:, b * LANES : (b + 1) * LANES] for b in range(nb)], axis=0)


def transposed(scr, top, bottom):
    ns, chans = top.shape
    scr[...] = jnp.zeros_like(scr)
    scr[0:ns, 0:chans] = top
    if bottom is not None:
        scr[ns : 2 * ns, 0:chans] = bottom
    return scr[...].T


def stack_masked(x, masks):
    return jnp.concatenate([x * m for m in masks], axis=0).astype(jnp.bfloat16)


def merge_masked(y, masks):
    nb = masks[0].shape[0]
    return sum(y[i * nb : (i + 1) * nb] * m for i, m in enumerate(masks))


def toeplitz(krow):
    t = pltpu.roll(jnp.broadcast_to(krow, (LANES, LANES)), 0, axis=1, stride=1, stride_axis=0)
    return jnp.where(iota((LANES, LANES), 1) >= iota((LANES, LANES), 0), t, 0.0).astype(jnp.bfloat16)


def mixer_fwd_kernel(
    un, qkv_ref, seg_ref, sw_ref, skip_ref, rate_ref, inb_ref, outc_ref,
    mixed_ref, core_ref, s_ref, f_ref, urev_ref, pp_ref, kern_ref,
    tscr, a_scr, b_scr, c_scr, e_scr, u_scr, kscr,
):
    ns, chans = rate_ref.shape
    nb = qkv_ref.shape[1] // chans
    masks, live, keep, carry, same = seg_masks(read_seg(seg_ref, nb), nb)
    flip = flip_matrix()
    keep_rev = mm(keep.astype(jnp.bfloat16), flip)
    rate, in_b, out_c = rate_ref[...], inb_ref[...], outc_ref[...]
    decay = jnp.exp(-rate)
    a_scr[...] = transposed(tscr, rate, rate)
    b_scr[...] = transposed(tscr, in_b * decay, None)
    c_scr[...] = transposed(tscr, out_c, None)
    e_scr[...] = transposed(tscr, jnp.exp(-rate * LANES), None)

    def kern_step(i, e):
        for j in range(8):
            kscr[pl.ds(i * 8 + j, 1), 0:chans] = jnp.sum(e, axis=0, keepdims=True)
            e = e * decay
        return e

    kscr[...] = jnp.zeros_like(kscr)
    lax.fori_loop(0, LANES // 8, kern_step, in_b * out_c)
    kern_ref[...] = kscr[...].T[0:chans]

    def drive_step(i, _):
        for j in range(un):
            c = i * un + j
            rows = pl.ds(pl.multiple_of(c * nb, nb), nb)
            k = qkv_ref[1, rows]
            shifted = sw_ref[0, c] * k
            for lag, prior in enumerate(priors(k, same)):
                shifted = shifted + sw_ref[lag + 1, c] * prior
            u_scr[rows, :] = shifted * qkv_ref[2, rows]
        return 0

    lax.fori_loop(0, chans // un, drive_step, 0)
    step_rows = 16 * nb

    def rev_step(i, _):
        rows = pl.ds(pl.multiple_of(i * step_rows, step_rows), step_rows)
        urev_ref[rows, :] = mm(u_scr[rows, :].astype(jnp.bfloat16), flip).astype(jnp.bfloat16)
        return 0

    lax.fori_loop(0, chans // 16, rev_step, 0)
    pos = iota((LANES, LANES), 0).astype(jnp.float32)
    factor = jnp.where(iota((LANES, LANES), 1) < ns, 1.0, pos)
    i8 = iota((8, LANES), 0).astype(jnp.float32)
    i16 = iota((LANES // 8, LANES), 0).astype(jnp.float32) * 8.0

    def fresh_step(i, _):
        for j in range(un):
            c = i * un + j
            rows = pl.ds(pl.multiple_of(c * nb, nb), nb)
            a = a_scr[pl.ds(c, 1), :]
            base = jnp.exp(-a * i8)
            tall = jnp.exp(-a * i16)
            p = (tall[:, None, :] * base[None]).reshape(LANES, LANES)
            pp = (p * factor).astype(jnp.bfloat16)
            pp_ref[pl.ds(pl.multiple_of(c * LANES, LANES), LANES), :] = pp
            urk = (urev_ref[rows, :].astype(jnp.float32) * keep_rev).astype(jnp.bfloat16)
            f_ref[rows, :] = mm(urk, pp)
        return 0

    lax.fori_loop(0, chans // un, fresh_step, 0)
    across = e_scr[0:chans, :]
    b_ext = b_scr[0:chans, :]
    state = jnp.zeros((chans, LANES), jnp.float32)
    for b in range(nb):
        s_ref[pl.ds(b, chans, stride=nb), :] = state + pltpu.roll(state, ns, axis=1)
        fresh = f_ref[pl.ds(b, chans, stride=nb), :]
        state = across * carry[b : b + 1, :] * state + b_ext * fresh

    def out_step(i, _):
        for j in range(un):
            c = i * un + j
            rows = pl.ds(pl.multiple_of(c * nb, nb), nb)
            t = toeplitz(kern_ref[pl.ds(c, 1), :])
            u = u_scr[rows, :]
            y = merge_masked(mm(stack_masked(u, masks), t), masks)
            sc = (s_ref[rows, :] * c_scr[pl.ds(c, 1), :]).astype(jnp.bfloat16)
            pp = pp_ref[pl.ds(pl.multiple_of(c * LANES, LANES), LANES), :]
            core = y + live * mm(sc, pp, NT) + skip_ref[0, c] * u
            core_ref[rows, :] = core
            u_scr[rows, :] = qkv_ref[0, rows] * core
        return 0

    lax.fori_loop(0, chans // un, out_step, 0)
    for b in range(nb):
        half = b % 2
        mixed_ref[b // 2, :, half * LANES : (half + 1) * LANES] = u_scr[
            pl.ds(b, chans, stride=nb), :
        ].astype(jnp.bfloat16)


def mixer_fwd(qkv, seg, shift_w, skip, rate, in_b, out_c, un=4):
    ns, chans = rate.shape
    rows = qkv.shape[1]
    nb = rows // chans
    f32, bf16 = jnp.float32, jnp.bfloat16
    sds = jax.ShapeDtypeStruct
    vm = pl.BlockSpec(memory_space=pltpu.VMEM)
    sm = pl.BlockSpec(memory_space=pltpu.SMEM)
    sq = pltpu.VMEM((LANES, LANES), f32)
    return pl.pallas_call(
        functools.partial(mixer_fwd_kernel, un),
        out_shape=(
            sds((nb // 2, chans, 2 * LANES), bf16),
            sds((rows, LANES), f32),
            sds((rows, LANES), f32),
            sds((rows, LANES), f32),
            sds((rows, LANES), bf16),
            sds((chans * LANES, LANES), bf16),
            sds((chans, LANES), f32),
        ),
        in_specs=[vm, vm, sm, sm, vm, vm, vm],
        out_specs=(vm,) * 7,
        scratch_shapes=[sq, sq, sq, sq, sq, pltpu.VMEM((rows, LANES), f32), sq],
        compiler_params=pltpu.CompilerParams(vmem_limit_bytes=48 << 20),
        name="mixer_fwd",
    )(qkv, seg, shift_w, skip, rate, in_b, out_c)


def mixer_bwd_kernel(
    un, gm_ref, qkv_ref, core_ref, s_ref, f_ref, urev_ref, pp_ref, kern_ref, seg_ref,
    sw_ref, skip_ref, rate_ref, inb_ref, outc_ref,
    dqkv_ref, dsw_ref, drate_ref, dinb_ref, doutc_ref, dskip_ref,
    tscr, b_scr, c_scr, e_scr, g_scr, sh_scr, h_scr, x_scr, dur_scr, dui_scr, dq_scr, dk_scr, dv_scr, gr_scr, red_scr,
):
    ns, chans = rate_ref.shape
    nb = qkv_ref.shape[1] // chans
    masks, live, keep, carry, same = seg_masks(read_seg(seg_ref, nb), nb)
    flip = flip_matrix()
    keep_rev = mm(keep.astype(jnp.bfloat16), flip)
    masks_rev = [mm(m.astype(jnp.bfloat16), flip) for m in masks]
    rate, in_b, out_c = rate_ref[...], inb_ref[...], outc_ref[...]
    decay = jnp.exp(-rate)
    b_scr[...] = transposed(tscr, in_b * decay, None)
    c_scr[...] = transposed(tscr, out_c, None)
    e_scr[...] = transposed(tscr, jnp.exp(-rate * LANES), None)
    red_scr[...] = jnp.zeros_like(red_scr)
    gr_scr[...] = jnp.zeros_like(gr_scr)

    for b in range(nb):
        half = b % 2
        x_scr[pl.ds(b, chans, stride=nb), :] = gm_ref[
            b // 2, :, half * LANES : (half + 1) * LANES
        ].astype(jnp.float32)
    corner = iota((LANES, LANES), 0) + iota((LANES, LANES), 1) >= LANES - 1

    def grad_step(i, _):
        for j in range(un):
            c = i * un + j
            rows = pl.ds(pl.multiple_of(c * nb, nb), nb)
            gm = x_scr[rows, :]
            dq_scr[rows, :] = gm * core_ref[rows, :]
            g = gm * qkv_ref[0, rows]
            g_scr[rows, :] = g
            k = qkv_ref[1, rows]
            shifted = sw_ref[0, c] * k
            for lag, prior in enumerate(priors(k, same)):
                shifted = shifted + sw_ref[lag + 1, c] * prior
            sh_scr[rows, :] = shifted
            red_scr[SHIFT, pl.ds(c, 1), :] = jnp.sum(
                g * shifted * qkv_ref[2, rows], axis=0, keepdims=True
            )
            ur = stack_masked(urev_ref[rows, :].astype(jnp.float32), masks_rev)
            cross = mm(ur, stack_masked(g, masks), TN)
            skew = pltpu.roll(jnp.where(corner, cross, 0.0), 1, axis=1, stride=1, stride_axis=0)
            gr_scr[pl.ds(c, 1), :] = jnp.sum(skew, axis=0, keepdims=True)
            pp = pp_ref[pl.ds(pl.multiple_of(c * LANES, LANES), LANES), :]
            h_scr[rows, :] = mm((g * live).astype(jnp.bfloat16), pp)
        return 0

    lax.fori_loop(0, chans // un, grad_step, 0)
    across = e_scr[0:chans, :]
    b_ext = b_scr[0:chans, :]
    c_ext = c_scr[0:chans, :]
    zero = jnp.zeros((chans, LANES), jnp.float32)
    adj, acc_out, acc_in, acc_carry = zero, zero, zero, zero
    for b in range(nb - 1, -1, -1):
        here = pl.ds(b, chans, stride=nb)
        h = h_scr[here, :]
        s = s_ref[here, :]
        acc_out = acc_out + s * h
        acc_in = acc_in + (adj + pltpu.roll(adj, ns, axis=1)) * f_ref[here, :]
        acc_carry = acc_carry + carry[b : b + 1, :] * adj * s
        x_scr[here, :] = b_ext * adj
        adj = c_ext * h + across * carry[b : b + 1, :] * adj

    def back_step(i, _):
        for j in range(un):
            c = i * un + j
            rows = pl.ds(pl.multiple_of(c * nb, nb), nb)
            t = toeplitz(kern_ref[pl.ds(c, 1), :])
            g = g_scr[rows, :]
            inner = merge_masked(mm(stack_masked(g, masks), t, NT), masks)
            pp = pp_ref[pl.ds(pl.multiple_of(c * LANES, LANES), LANES), :]
            dur_scr[rows, :] = (mm(x_scr[rows, :].astype(jnp.bfloat16), pp, NT) * keep_rev).astype(jnp.bfloat16)
            g_scr[rows, :] = inner + skip_ref[0, c] * g
        return 0

    lax.fori_loop(0, chans // un, back_step, 0)
    step_rows = 16 * nb

    def rev_step(i, _):
        rows = pl.ds(pl.multiple_of(i * step_rows, step_rows), step_rows)
        dui_scr[rows, :] = mm(dur_scr[rows, :], flip)
        return 0

    lax.fori_loop(0, chans // 16, rev_step, 0)

    def last_step(i, _):
        for j in range(un):
            c = i * un + j
            rows = pl.ds(pl.multiple_of(c * nb, nb), nb)
            du = g_scr[rows, :] + dui_scr[rows, :]
            dv_scr[rows, :] = du * sh_scr[rows, :]
            ds = du * qkv_ref[2, rows]
            k = qkv_ref[1, rows]
            lane = iota(k.shape, 1)
            red_scr[0, pl.ds(c, 1), :] = jnp.sum(ds * k, axis=0, keepdims=True)
            dk = sw_ref[0, c] * ds
            for lag, prior in enumerate(priors(k, same)):
                red_scr[lag + 1, pl.ds(c, 1), :] = jnp.sum(ds * prior, axis=0, keepdims=True)
                d = ds * same[lag]
                r = pltpu.roll(d, LANES - (lag + 1), axis=1)
                r2 = pltpu.roll(r, nb - 1, axis=0)
                dk = dk + sw_ref[lag + 1, c] * jnp.where(lane < LANES - (lag + 1), r, r2)
            dk_scr[rows, :] = dk
        return 0

    lax.fori_loop(0, chans // un, last_step, 0)
    for b in range(nb):
        half = b % 2
        for i, scr in enumerate((dq_scr, dk_scr, dv_scr)):
            dqkv_ref[b // 2, i, :, half * LANES : (half + 1) * LANES] = scr[
                pl.ds(b, chans, stride=nb), :
            ].astype(jnp.bfloat16)
    for j in range(SHIFT):
        dsw_ref[j : j + 1, :] = jnp.sum(red_scr[j].T, axis=0, keepdims=True)[:, 0:chans]
    dskip_ref[...] = jnp.sum(red_scr[SHIFT].T, axis=0, keepdims=True)[:, 0:chans]
    tscr[...] = gr_scr[...].T

    def kern_back(i, carried):
        e, zeroth, first = carried
        block = tscr[pl.ds(pl.multiple_of(i * 8, 8), 8), 0:chans]
        for j in range(8):
            term = e * block[j : j + 1, :]
            zeroth = zeroth + term
            first = first + term * (i * 8 + j).astype(jnp.float32)
            e = e * decay
        return e, zeroth, first

    blank = jnp.zeros((ns, chans), jnp.float32)
    _, zeroth, first = lax.fori_loop(0, LANES // 8, kern_back, (blank + 1.0, blank, blank))

    def back(x):
        tscr[...] = jnp.zeros_like(tscr)
        tscr[0:chans, :] = x
        y = tscr[...].T
        return y[0:ns, 0:chans], y[ns : 2 * ns, 0:chans]

    d_out, s_h1 = back(acc_out)
    d_inp, ds_f1 = back(acc_in)
    d_carry, _ = back(acc_carry)
    dinb_ref[...] = decay * d_inp + out_c * zeroth
    doutc_ref[...] = d_out + in_b * zeroth
    drate_ref[...] = -(
        out_c * s_h1
        + in_b * decay * (ds_f1 + d_inp)
        + LANES * jnp.exp(-rate * LANES) * d_carry
        + in_b * out_c * first
    )


def mixer_bwd(gm, qkv, core, s, f, urev, pp, kern, seg, shift_w, skip, rate, in_b, out_c, un=4):
    ns, chans = rate.shape
    rows = qkv.shape[1]
    nb = rows // chans
    f32, bf16 = jnp.float32, jnp.bfloat16
    sds = jax.ShapeDtypeStruct
    vm = pl.BlockSpec(memory_space=pltpu.VMEM)
    sm = pl.BlockSpec(memory_space=pltpu.SMEM)
    sq = pltpu.VMEM((LANES, LANES), f32)
    full = pltpu.VMEM((rows, LANES), f32)
    half = pltpu.VMEM((rows, LANES), bf16)
    return pl.pallas_call(
        functools.partial(mixer_bwd_kernel, un),
        out_shape=(
            sds((nb // 2, 3, chans, 2 * LANES), bf16),
            sds((SHIFT, chans), f32),
            sds((ns, chans), f32),
            sds((ns, chans), f32),
            sds((ns, chans), f32),
            sds((1, chans), f32),
        ),
        in_specs=[vm] * 9 + [sm, sm, vm, vm, vm],
        out_specs=(vm,) * 6,
        scratch_shapes=[
            sq, sq, sq, sq, full, full, full, full, half, full, full, full, full, sq,
            pltpu.VMEM((SHIFT + 1, LANES, LANES), f32),
        ],
        compiler_params=pltpu.CompilerParams(vmem_limit_bytes=56 << 20),
        name="mixer_bwd",
    )(gm, qkv, core, s, f, urev, pp, kern, seg, shift_w, skip, rate, in_b, out_c)


MESH = pl.DeviceIdType.MESH


class Place:
    def __init__(self, n_dp, n_head, n_tensor):
        self.n_dp, self.n_head, self.n_tensor = n_dp, n_head, n_tensor
        self.dp = lax.axis_index("dp")
        h, t = lax.axis_index("head"), lax.axis_index("tensor")
        self.size = n_head * n_tensor
        ph, xh, yt = h + 1 - 2 * (h % 2), (h + 2) % n_head, 1 - t
        pxh = (ph + 2) % n_head
        slot = lambda a, b: a * n_tensor + b
        self.me, self.p, self.x, self.y, self.d = (
            slot(h, t), slot(ph, t), slot(xh, t), slot(h, yt), slot(xh, yt),
        )
        self.px, self.py, self.pd = slot(pxh, t), slot(ph, yt), slot(pxh, yt)
        self.to_p, self.to_x, self.to_y = {"head": ph}, {"head": xh}, {"tensor": yt}

    def dp_peer(self, step):
        return (self.dp + step) % self.n_dp

    def barrier(self, whole_group, over_dp):
        sem = pltpu.get_barrier_semaphore()

        def greet(where):
            pl.semaphore_signal(sem, inc=1, device_id=where, device_id_type=MESH)

        if whole_group:
            for i in range(1, self.size):
                peer = (self.me + i) % self.size
                greet({"head": peer // self.n_tensor, "tensor": peer % self.n_tensor})
            count = self.size - 1
        else:
            for where in (self.to_p, self.to_x, self.to_y):
                greet(where)
            count = 3
        if over_dp:
            def step(i, _):
                greet({"dp": self.dp_peer(i)})
                return 0

            lax.fori_loop(1, self.n_dp, step, 0)
            count += self.n_dp - 1
        pl.semaphore_wait(sem, count)


def remote(src, dst, ssem, rsem, where):
    return pltpu.make_async_remote_copy(
        src_ref=src, dst_ref=dst, send_sem=ssem, recv_sem=rsem, device_id=where, device_id_type=MESH
    )


class GroupGather:
    COPIES = 9

    def __init__(self, place, ref, ssem, rsem):
        self.ssem, self.rsem = ssem, rsem
        half = ref.shape[1] // 2
        top, low = pl.ds(0, half), pl.ds(half, half)
        pc = place
        full = lambda s: ref.at[s]
        part = lambda s, rows: ref.at[s, rows]
        self.out = [
            (full(pc.me), pc.to_p), (full(pc.me), pc.to_x), (full(pc.me), pc.to_y),
            (part(pc.x, top), pc.to_y), (part(pc.y, low), pc.to_x),
            (full(pc.x), pc.to_p), (full(pc.y), pc.to_p),
            (part(pc.d, top), pc.to_p), (part(pc.d, low), pc.to_p),
        ]
        self.into = [
            full(pc.p), full(pc.x), full(pc.y), part(pc.d, top), part(pc.d, low),
            full(pc.px), full(pc.py), part(pc.pd, top), part(pc.pd, low),
        ]

    def send(self, *which):
        for i in which:
            src, where = self.out[i]
            remote(src, src, self.ssem.at[i], self.rsem.at[i], where).start()

    def arrive(self, *which):
        for i in which:
            dst = self.into[i]
            remote(dst, dst, self.ssem.at[i], self.rsem.at[i], self.out[i][1]).wait_recv()

    def start(self):
        self.send(1, 2, 0)

    def middle(self):
        self.arrive(1, 2)
        self.send(3, 4, 5, 6)

    def late(self):
        self.arrive(3, 4)
        self.send(7, 8)

    def finish(self):
        self.arrive(0, 5, 6, 7, 8)

    def drain(self):
        for i in range(self.COPIES):
            src, where = self.out[i]
            remote(src, src, self.ssem.at[i], self.rsem.at[i], where).wait_send()


class DepthGather:
    def __init__(self, place, ref, ssem, rsem):
        self.place, self.ref, self.ssem, self.rsem = place, ref, ssem, rsem

    def _copy(self, step, slot, peer):
        return remote(
            self.ref.at[slot], self.ref.at[slot], self.ssem.at[step], self.rsem.at[step], {"dp": peer}
        )

    def _loop(self, body):
        def step(i, _):
            body(i)
            return 0

        lax.fori_loop(1, self.place.n_dp, step, 0)

    def start(self):
        pc = self.place
        self._loop(lambda i: self._copy(i, pc.dp, pc.dp_peer(i)).start())

    def finish(self):
        pc = self.place
        source = lambda i: (pc.dp + pc.n_dp - i) % pc.n_dp
        self._loop(lambda i: self._copy(i, source(i), pc.dp_peer(i)).wait_recv())

    def drain(self):
        pc = self.place
        self._loop(lambda i: self._copy(i, pc.dp, pc.dp_peer(i)).wait_send())


def joined(ref):
    n, rows, columns = ref.shape
    if rows % 16 == 0:
        return ref[...].reshape(n * rows, columns)
    parts = [ref[j].astype(jnp.float32) for j in range(n)]
    return jnp.concatenate(parts, axis=0).astype(ref.dtype)


def row_norm(x):
    centred = x - jnp.mean(x, axis=1, keepdims=True)
    inv = lax.rsqrt(jnp.mean(centred * centred, axis=1, keepdims=True) + 1e-05)
    return centred * inv, inv


def first_kernel(
    axes, tok_ref, cot_ref, gain_ref, bias_ref, qkvo_ref, up_ref,
    xn_all, cot_all, qkv_ref, wqkvo_all, wup_all, wupt_ref, wout_all,
    wt_scr, gs, gr, cs, cr, os, orr, zs, zr, lsem,
):
    pc = Place(*axes)
    pc.barrier(False, True)
    chans = wout_all.shape[1]
    own = tok_ref.shape[0]
    keep_qkvo = pltpu.make_async_copy(qkvo_ref, wqkvo_all.at[pc.dp], lsem.at[0])
    keep_up = pltpu.make_async_copy(up_ref, wup_all.at[pc.dp], lsem.at[1])
    keep_qkvo.start()
    keep_up.start()
    z_qkvo = DepthGather(pc, wqkvo_all, zs.at[0], zr.at[0])
    z_up = DepthGather(pc, wup_all, zs.at[1], zr.at[1])
    xn_g = GroupGather(pc, xn_all, gs, gr)
    cot_g = GroupGather(pc, cot_all, cs, cr)
    out_g = GroupGather(pc, wout_all, os, orr)
    keep_qkvo.wait()
    z_qkvo.start()
    keep_up.wait()
    z_up.start()
    hat, _ = row_norm(tok_ref[...].astype(jnp.float32))
    xn_all[pc.me] = (hat * gain_ref[...] + bias_ref[...]).astype(jnp.bfloat16).T
    xn_g.start()
    cot_all[pc.me] = cot_ref[...].T
    cot_g.start()
    z_qkvo.finish()
    wt_scr[...] = joined(wqkvo_all).T
    wout_all[pc.me] = wt_scr[3 * chans :, :]
    xn_g.middle()
    xn_g.late()
    out_g.start()
    cot_g.middle()
    xn_g.finish()
    for s in range(pc.size):
        y = mm(wt_scr[0 : 3 * chans, :], xn_all[s])
        for h in range(own // LANES):
            qkv_ref[pl.ds(s * (own // LANES) + h, 3 * chans, stride=pc.size * (own // LANES)), :] = y[
                :, h * LANES : (h + 1) * LANES
            ]
    z_up.finish()
    wupt_ref[...] = joined(wup_all).T
    cot_g.late()
    out_g.middle()
    out_g.late()
    cot_g.finish()
    out_g.finish()
    for work in (xn_g, cot_g, out_g, z_qkvo, z_up):
        work.drain()


def first_stage(axes, tokens, cot, gain, bias, qkvo, up):
    n_dp, n_head, n_tensor = axes
    group = n_head * n_tensor
    own, feats = tokens.shape
    chans = qkvo.shape[1] // 4
    f32, bf16 = jnp.float32, jnp.bfloat16
    sds = jax.ShapeDtypeStruct
    vm = pl.BlockSpec(memory_space=pltpu.VMEM)
    dma = pltpu.SemaphoreType.DMA
    return pl.pallas_call(
        functools.partial(first_kernel, axes),
        out_shape=(
            sds((group, feats, own), bf16),
            sds((group, feats, own), bf16),
            sds((3 * chans * group * own // LANES, LANES), f32),
            sds((n_dp,) + qkvo.shape, bf16),
            sds((n_dp,) + up.shape, bf16),
            sds((up.shape[1], feats), bf16),
            sds((group, chans, feats), bf16),
        ),
        in_specs=[vm] * 6,
        out_specs=(vm,) * 7,
        scratch_shapes=[
            pltpu.VMEM((4 * chans, feats), bf16),
            dma((9,)), dma((9,)), dma((9,)), dma((9,)), dma((9,)), dma((9,)),
            dma((2, n_dp)), dma((2, n_dp)), dma((2,)),
        ],
        compiler_params=pltpu.CompilerParams(
            collective_id=1, has_side_effects=True, vmem_limit_bytes=56 << 20
        ),
        name="first_stage",
    )(tokens, cot, gain, bias, qkvo, up)


class GroupReduce:
    def __init__(self, place, part, land, half_land, last_land, ssem, rsem):
        pc = place
        self.part, self.land, self.half_land, self.last_land = part, land, half_land, last_land
        self.ssem, self.rsem = ssem, rsem
        half = part.shape[1] // 2
        self.top, self.low = pl.ds(0, half), pl.ds(half, half)
        self.mine = [pc.d, pc.x, pc.y, pc.me]
        theirs = [pc.pd, pc.px, pc.py, pc.p]
        self.copies = [(part.at[theirs[i]], land.at[i], pc.to_p) for i in range(4)] + [
            (part.at[pc.d, self.top], half_land.at[0], pc.to_x),
            (part.at[pc.d, self.low], half_land.at[1], pc.to_y),
            (part.at[pc.x], last_land.at[0], pc.to_x),
            (part.at[pc.y], last_land.at[1], pc.to_y),
        ]
        self.pc = pc

    COPIES = 8

    def _copy(self, i):
        src, dst, where = self.copies[i]
        return remote(src, dst, self.ssem.at[i], self.rsem.at[i], where)

    def give(self, i):
        self._copy(i).start()

    def pair(self, i):
        self._copy(i).wait_recv()
        s = self.mine[i]
        self.part[s] = (self.part[s].astype(jnp.float32) + self.land[i].astype(jnp.float32)).astype(
            self.part.dtype
        )

    def far(self):
        self._copy(4).start()
        self._copy(5).start()

    def near(self):
        for i, s, rows in ((4, self.pc.y, self.top), (5, self.pc.x, self.low)):
            self._copy(i).wait_recv()
            self.part[s, rows] = (
                self.part[s, rows].astype(jnp.float32) + self.half_land[i - 4].astype(jnp.float32)
            ).astype(self.part.dtype)
            self._copy(7 if i == 4 else 6).start()

    def total(self):
        self._copy(6).wait_recv()
        self._copy(7).wait_recv()
        return (
            self.part[self.pc.me].astype(jnp.float32)
            + self.last_land[0].astype(jnp.float32)
            + self.last_land[1].astype(jnp.float32)
        )

    def drain(self):
        for i in range(self.COPIES):
            self._copy(i).wait_send()

    @staticmethod
    def scratch(group, rows, columns):
        bf16 = jnp.bfloat16
        return [
            pltpu.VMEM((group, rows, columns), bf16),
            pltpu.VMEM((4, rows, columns), bf16),
            pltpu.VMEM((2, rows // 2, columns), bf16),
            pltpu.VMEM((2, rows, columns), bf16),
            pltpu.SemaphoreType.DMA((8,)),
            pltpu.SemaphoreType.DMA((8,)),
        ]


class GroupSwap:
    def __init__(self, place, src, dst, ssem, rsem, lsem):
        self.pc, self.src, self.dst, self.ssem, self.rsem, self.lsem = place, src, dst, ssem, rsem, lsem

    def _peer(self, i):
        return (self.pc.me + i) % self.pc.size

    def _copy(self, i, slot):
        peer = self._peer(i)
        where = {"head": peer // self.pc.n_tensor, "tensor": peer % self.pc.n_tensor}
        return remote(self.src.at[peer], self.dst.at[slot], self.ssem.at[i], self.rsem.at[i], where)

    def _own(self):
        return pltpu.make_async_copy(self.src.at[self.pc.me], self.dst.at[self.pc.me], self.lsem)

    def start(self):
        for i in range(1, self.pc.size):
            self._copy(i, self.pc.me).start()
        self._own().start()

    def finish(self):
        for i in range(1, self.pc.size):
            self._copy(i, (self.pc.me + self.pc.size - i) % self.pc.size).wait_recv()
        self._own().wait()

    def drain(self):
        for i in range(1, self.pc.size):
            self._copy(i, self.pc.me).wait_send()


class DepthReduce:
    def __init__(self, place, src, land, ssem, rsem):
        self.place, self.src, self.land, self.ssem, self.rsem = place, src, land, ssem, rsem

    def _copy(self, step, mine, slot, peer):
        return remote(
            self.src.at[mine], self.land.at[slot], self.ssem.at[step], self.rsem.at[step], {"dp": peer}
        )

    def _loop(self, body, start):
        return lax.fori_loop(1, self.place.n_dp, body, start)

    def start(self):
        pc = self.place

        def step(i, _):
            self._copy(i, pc.dp_peer(i), pc.dp, pc.dp_peer(i)).start()
            return 0

        self._loop(step, 0)

    def total(self):
        pc = self.place

        def step(i, acc):
            source = (pc.dp + pc.n_dp - i) % pc.n_dp
            self._copy(i, source, source, pc.dp_peer(i)).wait_recv()
            return acc + self.land[source].astype(jnp.float32)

        return self._loop(step, self.src[pc.dp].astype(jnp.float32))

    def drain(self):
        pc = self.place

        def step(i, _):
            self._copy(i, pc.dp_peer(i), pc.dp, pc.dp_peer(i)).wait_send()
            return 0

        self._loop(step, 0)


def split_rows(ref, value):
    n, rows, columns = ref.shape
    if rows % 16 == 0:
        ref[...] = value.astype(ref.dtype).reshape(n, rows, columns)
    else:
        for j in range(n):
            ref[j] = value[j * rows : (j + 1) * rows].astype(ref.dtype)


def row_norm_back(grad, gain, hat, inv):
    scaled = grad * gain
    return inv * (
        scaled
        - jnp.mean(scaled, axis=1, keepdims=True)
        - hat * jnp.mean(scaled * hat, axis=1, keepdims=True)
    )


def gelu_pair(pre):
    cdf = 0.5 * (1.0 + lax.erf(pre * 0.7071067811865476))
    return pre * cdf, cdf + pre * (0.3989422804014327 * jnp.exp(-0.5 * pre * pre))


def middle_kernel(
    axes, mixed_ref, tok_ref, cot_ref, cot_all, woutt_ref, wup_ref, wupt_ref, down_ref, gain_ref, bias_ref,
    hid_ref, ghid_ref, gmix_all, mlp_part, down_part, up_ref, out_part, norm_ref,
    mixed_in, xn_all, wdown_all, wdownt, hat_scr, act_all, gpre_all, gm_scr, up_part, up_land,
    part, land, half_land, last_land, rs, rr, gs, gr, ms, mr, bs, br, zs, zr, us, ur, lsem,
):
    pc = Place(*axes)
    pc.barrier(True, True)
    f32, bf16 = jnp.float32, jnp.bfloat16
    group, chans, own = mixed_in.shape
    feats = group * chans
    own_down = pltpu.make_async_copy(down_ref, wdown_all.at[pc.dp], lsem.at[0])
    own_down.start()
    swap_in = GroupSwap(pc, mixed_ref, mixed_in, ms, mr, lsem.at[1])
    swap_in.start()
    own_down.wait()
    z_down = DepthGather(pc, wdown_all, zs, zr)
    z_down.start()
    xn_g = GroupGather(pc, xn_all, gs, gr)
    red = GroupReduce(pc, part, land, half_land, last_land, rs, rr)
    x = tok_ref[...].astype(f32)
    swap_in.finish()
    mixed_t = mixed_in[...].reshape(feats, own)
    wout_t = woutt_ref[...].reshape(feats, feats)
    hidden = x + mm(mixed_t, wout_t, TN)
    hid_ref[...] = hidden
    hat, inv = row_norm(hidden)
    xn_all[pc.me] = (hat * gain_ref[...] + bias_ref[...]).astype(bf16).T
    xn_g.start()
    hat_scr[...] = hat
    z_down.finish()
    w_down = joined(wdown_all)
    wdownt[...] = w_down.T
    w_up = joined(wup_ref)

    def chunk(s):
        act, slope = gelu_pair(mm(wupt_ref[...], xn_all[s]))
        act_all[s] = act.astype(bf16)
        grad_act = mm(wdownt[...], cot_all[s])
        grad_pre = (grad_act * slope).astype(bf16)
        gpre_all[s] = grad_pre
        part[s] = mm(w_up, grad_pre).astype(bf16)

    chunk(pc.me)
    xn_g.arrive(0)
    chunk(pc.p)
    red.give(3)
    xn_g.middle()
    chunk(pc.x)
    xn_g.late()
    chunk(pc.y)
    xn_g.arrive(5)
    chunk(pc.px)
    red.give(1)
    xn_g.arrive(6)
    chunk(pc.py)
    red.give(2)
    chunk(pc.d)
    xn_g.arrive(7, 8)
    chunk(pc.pd)
    red.give(0)
    red.pair(1)
    red.pair(2)
    red.pair(0)
    red.far()
    red.pair(3)
    grad_up = jnp.zeros((feats, wupt_ref.shape[0]), f32)
    for s in range(group):
        grad_up = grad_up + mm(xn_all[s], gpre_all[s], NT)
    split_rows(up_part, grad_up)
    z_up = DepthReduce(pc, up_part, up_land, us, ur)
    z_up.start()
    red.near()
    for s in range(group):
        mlp_part[s] = mm(w_down, act_all[s]).astype(bf16)
    grad_down = jnp.zeros((feats, wupt_ref.shape[0]), f32)
    for s in range(group):
        grad_down = grad_down + mm(cot_all[s], act_all[s], NT)
    split_rows(down_part, grad_down)
    grad_xn = red.total().T
    norm_ref[0:1, :] = jnp.sum(grad_xn * hat_scr[...], axis=0, keepdims=True)
    norm_ref[1:2, :] = jnp.sum(grad_xn, axis=0, keepdims=True)
    grad_hidden = cot_ref[...].astype(f32) + row_norm_back(grad_xn, gain_ref[...], hat_scr[...], inv)
    ghid_ref[...] = grad_hidden
    grad_mix = grad_hidden.astype(bf16)
    gm_scr[...] = mm(wout_t, grad_mix, NT).astype(bf16).reshape(group, chans, own)
    swap_out = GroupSwap(pc, gm_scr, gmix_all, bs, br, lsem.at[2])
    swap_out.start()
    out_part[...] = mm(mixed_t, grad_mix).astype(bf16).reshape(group, chans, feats)
    swap_out.finish()
    up_ref[...] = z_up.total()
    for work in (swap_in, z_down, xn_g, red, z_up, swap_out):
        work.drain()


def middle_stage(axes, mixed, tokens, cot_own, cot_all, wout_t, wup, wup_t, down, gain, bias):
    n_dp, n_head, n_tensor = axes
    group = n_head * n_tensor
    own, feats = tokens.shape
    _, chans, _ = mixed.shape
    rows, units = down.shape
    f32, bf16 = jnp.float32, jnp.bfloat16
    sds = jax.ShapeDtypeStruct
    vm = pl.BlockSpec(memory_space=pltpu.VMEM)
    dma = pltpu.SemaphoreType.DMA
    return pl.pallas_call(
        functools.partial(middle_kernel, axes),
        out_shape=(
            sds((own, feats), f32),
            sds((own, feats), f32),
            sds((group, chans, own), bf16),
            sds((group, feats, own), bf16),
            sds((n_dp, rows, units), bf16),
            sds((rows, units), f32),
            sds((group, chans, feats), bf16),
            sds((2, feats), f32),
        ),
        in_specs=[vm] * 10,
        out_specs=(vm,) * 8,
        scratch_shapes=[
            pltpu.VMEM((group, chans, own), bf16),
            pltpu.VMEM((group, feats, own), bf16),
            pltpu.VMEM((n_dp, rows, units), bf16),
            pltpu.VMEM((units, feats), bf16),
            pltpu.VMEM((own, feats), f32),
            pltpu.VMEM((group, units, own), bf16),
            pltpu.VMEM((group, units, own), bf16),
            pltpu.VMEM((group, chans, own), bf16),
            pltpu.VMEM((n_dp, rows, units), bf16),
            pltpu.VMEM((n_dp, rows, units), bf16),
            *GroupReduce.scratch(group, feats, own),
            dma((9,)), dma((9,)), dma((8,)), dma((8,)), dma((8,)), dma((8,)),
            dma((n_dp,)), dma((n_dp,)), dma((n_dp,)), dma((n_dp,)), dma((3,)),
        ],
        compiler_params=pltpu.CompilerParams(
            collective_id=2, has_side_effects=True, vmem_limit_bytes=60 << 20
        ),
        name="middle_stage",
    )(mixed, tokens, cot_own, cot_all, wout_t, wup, wup_t, down, gain, bias)


class GroupSpread:
    def __init__(self, place, ref, ssem, rsem):
        self.pc, self.ref, self.ssem, self.rsem = place, ref, ssem, rsem

    def _copy(self, i, slot):
        peer = (self.pc.me + i) % self.pc.size
        where = {"head": peer // self.pc.n_tensor, "tensor": peer % self.pc.n_tensor}
        return remote(self.ref.at[slot], self.ref.at[slot], self.ssem.at[i], self.rsem.at[i], where)

    def start(self):
        for i in range(1, self.pc.size):
            self._copy(i, self.pc.me).start()

    def finish(self):
        for i in range(1, self.pc.size):
            self._copy(i, (self.pc.me + self.pc.size - i) % self.pc.size).wait_recv()

    def drain(self):
        for i in range(1, self.pc.size):
            self._copy(i, self.pc.me).wait_send()


RATE, INB, OUTC, TAPS, SKIP, PARAM_ROWS = 0, 64, 128, 192, 208, 224


def last_kernel(
    axes, dqkv_ref, xn_all, wqkvo_ref, mlp_hbm, out_hbm, down_ref, hid_ref, ghid_ref, tok_ref, gain_ref, norm2_ref,
    dsw_ref, drate_ref, dinb_ref, doutc_ref, dskip_ref,
    res_ref, gx_ref, g1_ref, b1_ref, g2_ref, b2_ref, wq_ref, wk_ref, wv_ref, wo_ref, wd_ref,
    sw_ref, rate_ref, inb_ref, outc_ref, skip_ref,
    w_part, w_land, d_land, p_all, n_all, m_all,
    xp, xl, xh, xe, xs, xr, op, ol, oh, oe, os, orr, mp, ml, mh, me, ms, mr,
    ds, dr, ws, wr, ps, pr, ns, nr, qs, qr, lsem,
):
    pc = Place(*axes)
    f32, bf16 = jnp.float32, jnp.bfloat16
    load_out = pltpu.make_async_copy(out_hbm, op, lsem.at[0])
    load_mlp = pltpu.make_async_copy(mlp_hbm, mp, lsem.at[1])
    load_out.start()
    load_mlp.start()
    group, chans, feats = out_hbm.shape
    own = tok_ref.shape[0]
    pc.barrier(True, True)
    z_down = DepthReduce(pc, down_ref, d_land, ds, dr)
    z_down.start()
    p_all[pc.dp] = jnp.zeros(p_all.shape[1:], bf16)
    for at, ref in ((RATE, drate_ref), (INB, dinb_ref), (OUTC, doutc_ref), (TAPS, dsw_ref), (SKIP, dskip_ref)):
        p_all[pc.dp, at : at + ref.shape[0], 0:chans] = ref[...].astype(bf16)
    z_par = DepthGather(pc, p_all, ps, pr)
    z_par.start()
    red_o = GroupReduce(pc, op, ol, oh, oe, os, orr)
    red_x = GroupReduce(pc, xp, xl, xh, xe, xs, xr)
    red_m = GroupReduce(pc, mp, ml, mh, me, ms, mr)
    load_out.wait()
    for i in range(4):
        red_o.give(i)
    w_joint = joined(wqkvo_ref)

    def grads(s):
        return dqkv_ref[s].reshape(3 * chans, own)

    def chunk(s):
        padded = jnp.concatenate([grads(s), jnp.zeros((chans, own), bf16)], axis=0)
        xp[s] = mm(w_joint, padded).astype(bf16)

    for i, s in enumerate((pc.pd, pc.px, pc.py, pc.p)):
        chunk(s)
        red_x.give(i)
    red_o.pair(0)
    red_o.far()
    load_mlp.wait()
    for i in range(4):
        red_m.give(i)
    chunk(pc.d)
    red_x.pair(0)
    red_x.far()
    for i in (1, 2):
        red_o.pair(i)
    chunk(pc.x)
    chunk(pc.y)
    red_o.near()
    red_o.pair(3)
    red_x.pair(1)
    red_x.pair(2)
    red_x.near()
    chunk(pc.me)
    red_x.pair(3)
    grad_w = jnp.zeros((feats, 3 * chans), f32)
    for s in range(group):
        grad_w = grad_w + mm(xn_all[s], grads(s), NT)
    split_rows(w_part, jnp.concatenate([grad_w, red_o.total().T], axis=1))
    z_w = DepthReduce(pc, w_part, w_land, ws, wr)
    z_w.start()
    red_m.pair(0)
    red_m.far()
    for i in (1, 2, 3):
        red_m.pair(i)
    hat, inv = row_norm(tok_ref[...].astype(f32))
    grad_xn = red_x.total().T
    n_all[pc.me, 0:1, :] = jnp.sum(grad_xn * hat, axis=0, keepdims=True)
    n_all[pc.me, 1:2, :] = jnp.sum(grad_xn, axis=0, keepdims=True)
    n_all[pc.me, 2:4, :] = norm2_ref[...]
    n_all[pc.me, 4:8, :] = jnp.zeros((4, feats), f32)
    spread = GroupSpread(pc, n_all, ns, nr)
    spread.start()
    red_m.near()
    gx_ref[...] = ghid_ref[...] + row_norm_back(grad_xn, gain_ref[...], hat, inv)
    spread.finish()
    m_all[pc.dp] = jnp.sum(n_all[...], axis=0)
    z_norm = DepthGather(pc, m_all, qs, qr)
    z_norm.start()
    z_par.finish()
    params = jnp.sum(p_all[...].astype(f32), axis=0)
    for at, ref in ((RATE, rate_ref), (INB, inb_ref), (OUTC, outc_ref), (TAPS, sw_ref), (SKIP, skip_ref)):
        ref[...] = params[at : at + ref.shape[0], 0:chans]
    wd_ref[...] = z_down.total()
    res_ref[...] = (hid_ref[...] + red_m.total().T).astype(bf16)
    z_norm.finish()
    norms = jnp.sum(m_all[...], axis=0)
    for i, ref in enumerate((g1_ref, b1_ref, g2_ref, b2_ref)):
        ref[...] = norms[i : i + 1, :]
    w_sum = z_w.total()
    for i, ref in enumerate((wq_ref, wk_ref, wv_ref, wo_ref)):
        ref[...] = w_sum[:, i * chans : (i + 1) * chans]
    for work in (z_down, z_par, red_o, red_x, red_m, z_w, spread, z_norm):
        work.drain()


def last_stage(axes, dqkv, xn_all, wqkvo, mlp, out, down, hidden, ghid, tokens, gain, norm2, dsw, drate, dinb, doutc, dskip):
    n_dp, n_head, n_tensor = axes
    group = n_head * n_tensor
    own, feats = tokens.shape
    chans = out.shape[1]
    _, rows, units = down.shape
    f32, bf16 = jnp.float32, jnp.bfloat16
    sds = jax.ShapeDtypeStruct
    vm = pl.BlockSpec(memory_space=pltpu.VMEM)
    hbm = pl.BlockSpec(memory_space=pl.ANY)
    dma = pltpu.SemaphoreType.DMA
    wide, thin = GroupReduce.scratch(group, feats, own), GroupReduce.scratch(group, chans, feats)
    return pl.pallas_call(
        functools.partial(last_kernel, axes),
        out_shape=(
            sds((own, feats), bf16),
            sds((own, feats), f32),
            *(sds((1, feats), f32),) * 4,
            *(sds((rows, chans), f32),) * 4,
            sds((rows, units), f32),
            *(sds(a.shape, f32) for a in (dsw, drate, dinb, doutc, dskip)),
        ),
        in_specs=[vm, vm, vm, hbm, hbm] + [vm] * 11,
        out_specs=(vm,) * 16,
        scratch_shapes=[
            pltpu.VMEM(wqkvo.shape, bf16),
            pltpu.VMEM(wqkvo.shape, bf16),
            pltpu.VMEM((n_dp, rows, units), bf16),
            pltpu.VMEM((n_dp, PARAM_ROWS, LANES), bf16),
            pltpu.VMEM((group, 8, feats), f32),
            pltpu.VMEM((n_dp, 8, feats), f32),
            *wide, *thin, *wide,
            *(dma((n_dp,)),) * 6,
            dma((8,)), dma((8,)), dma((n_dp,)), dma((n_dp,)), dma((2,)),
        ],
        compiler_params=pltpu.CompilerParams(
            collective_id=3, has_side_effects=True, vmem_limit_bytes=62 << 20
        ),
        name="last_stage",
    )(dqkv, xn_all, wqkvo, mlp, out, down, hidden, ghid, tokens, gain, norm2, dsw, drate, dinb, doutc, dskip)


from jax.sharding import PartitionSpec as P

GROUP = ("head", "tensor")


def on_device(
    tokens, seg_ids, norm1_gain, norm1_bias, norm2_gain, norm2_bias, q_weight, k_weight, v_weight,
    out_weight, up_weight, down_weight, shift_weight, decay_rate, in_coef, out_coef, skip_coef, cotangent,
):
    chans = q_weight.shape[1]
    axes = (lax.axis_size("dp"), lax.axis_size("head"), lax.axis_size("tensor"))
    packed = jnp.concatenate([q_weight, k_weight, v_weight, out_weight], axis=1)
    xn1, cot, qkv, w_packed, w_up, w_up_t, w_out_t = first_stage(
        axes, tokens, cotangent, norm1_gain[None], norm1_bias[None], packed, up_weight
    )
    qkv = qkv.reshape(3, qkv.shape[0] // 3, LANES)
    mixer = (seg_ids, shift_weight, skip_coef[None], decay_rate, in_coef, out_coef)
    mixed, *saved = mixer_fwd(qkv, *mixer, un=16)
    hidden, grad_hidden, grad_mixed, mlp_part, down_part, sum_up, out_part, norms2 = middle_stage(
        axes, mixed, tokens, cotangent, cot, w_out_t, w_up, w_up_t, down_weight, norm2_gain[None], norm2_bias[None]
    )
    dqkv, *mixer_grads = mixer_bwd(grad_mixed, qkv, *saved, *mixer, un=16)
    (
        result, grad_x, gain1, bias1, gain2, bias2, sum_q, sum_k, sum_v, sum_o, sum_down,
        sum_shift, sum_rate, sum_in, sum_out, sum_skip,
    ) = last_stage(
        axes, dqkv, xn1, w_packed, mlp_part, out_part, down_part, hidden, grad_hidden, tokens,
        norm1_gain[None], norms2, *mixer_grads
    )
    return (
        result, grad_x, gain1[0], bias1[0], gain2[0], bias2[0], sum_q, sum_k, sum_v, sum_o, sum_up, sum_down,
        sum_shift, sum_rate, sum_in, sum_out, sum_skip[0],
    )


def solution(mesh):
    rows = P(("dp", "head", "tensor"), None)
    weight = P("dp", GROUP)
    chan = P(None, GROUP)
    in_specs = (rows, P("dp", None)) + (P(),) * 4 + (weight,) * 6 + (chan,) * 4 + (P(GROUP), rows)
    out_specs = (rows, rows) + (P(),) * 4 + (weight,) * 6 + (chan,) * 4 + (P(GROUP),)
    return jax.shard_map(on_device, mesh=mesh, in_specs=in_specs, out_specs=out_specs, check_vma=False)
```

```python
import functools
import jax, jax.numpy as jnp
from jax import lax
from jax.experimental import pallas as pl
from jax.experimental.pallas import tpu as pltpu

LANES = 128
SHIFT = 4
SEQS = 3
NT = (((1,), (1,)), ((), ()))
TN = (((0,), (0,)), ((), ()))
NN = (((1,), (0,)), ((), ()))


def mm(left, right, dims=NN):
    return lax.dot_general(left, right, dims, preferred_element_type=jnp.float32)


def iota(shape, axis):
    return lax.broadcasted_iota(jnp.int32, shape, axis)


def seg_masks(seg, nb):
    lane = iota((nb, LANES), 1)
    row = iota((nb, LANES), 0)
    masks = [(seg == k).astype(jnp.float32) for k in range(SEQS)]
    end = jnp.broadcast_to(seg[:, LANES - 1 :], (nb, LANES))
    last = jnp.where(row == 0, -1, pltpu.roll(end, 1, axis=0))
    live = (seg == last).astype(jnp.float32)
    keep = (seg == end).astype(jnp.float32)
    carry = (end == last).astype(jnp.float32)
    same = []
    for j in range(1, SHIFT):
        r = pltpu.roll(seg, j, axis=1)
        r2 = pltpu.roll(r, 1, axis=0)
        prior = jnp.where(lane < j, r2, r)
        ok = (prior == seg) & ((row > 0) | (lane >= j))
        same.append(ok.astype(jnp.float32))
    return masks, live, keep, carry, same


def priors(k, same):
    lane = iota(k.shape, 1)
    out = []
    for j in range(1, SHIFT):
        r = pltpu.roll(k, j, axis=1)
        r2 = pltpu.roll(r, 1, axis=0)
        out.append(jnp.where(lane < j, r2, r) * same[j - 1])
    return out


def flip_matrix():
    return (iota((LANES, LANES), 0) + iota((LANES, LANES), 1) == LANES - 1).astype(jnp.bfloat16)


def read_seg(seg_ref, nb):
    return jnp.concatenate([seg_ref[:, b * LANES : (b + 1) * LANES] for b in range(nb)], axis=0)


def transposed(scr, top, bottom):
    ns, chans = top.shape
    scr[...] = jnp.zeros_like(scr)
    scr[0:ns, 0:chans] = top
    if bottom is not None:
        scr[ns : 2 * ns, 0:chans] = bottom
    return scr[...].T


def stack_masked(x, masks):
    return jnp.concatenate([x * m for m in masks], axis=0).astype(jnp.bfloat16)


def merge_masked(y, masks):
    nb = masks[0].shape[0]
    return sum(y[i * nb : (i + 1) * nb] * m for i, m in enumerate(masks))


def toeplitz(krow):
    t = pltpu.roll(jnp.broadcast_to(krow, (LANES, LANES)), 0, axis=1, stride=1, stride_axis=0)
    return jnp.where(iota((LANES, LANES), 1) >= iota((LANES, LANES), 0), t, 0.0).astype(jnp.bfloat16)


def mixer_forward(
    un, qkv_ref, seg_ref, sw_ref, skip_ref, rate_ref, inb_ref, outc_ref,
    mixed_ref, core_ref, s_ref, f_ref, urev_ref, pp_ref, kern_ref,
    tscr, a_scr, b_scr, c_scr, e_scr, u_scr, kscr,
):
    ns, chans = rate_ref.shape
    nb = qkv_ref.shape[1] // chans
    masks, live, keep, carry, same = seg_masks(read_seg(seg_ref, nb), nb)
    flip = flip_matrix()
    keep_rev = mm(keep.astype(jnp.bfloat16), flip)
    rate, in_b, out_c = rate_ref[...], inb_ref[...], outc_ref[...]
    decay = jnp.exp(-rate)
    a_scr[...] = transposed(tscr, rate, rate)
    b_scr[...] = transposed(tscr, in_b * decay, None)
    c_scr[...] = transposed(tscr, out_c, None)
    e_scr[...] = transposed(tscr, jnp.exp(-rate * LANES), None)

    def kern_step(i, e):
        for j in range(8):
            kscr[pl.ds(i * 8 + j, 1), 0:chans] = jnp.sum(e, axis=0, keepdims=True)
            e = e * decay
        return e

    kscr[...] = jnp.zeros_like(kscr)
    lax.fori_loop(0, LANES // 8, kern_step, in_b * out_c)
    kern_ref[...] = kscr[...].T[0:chans]

    def drive_step(i, _):
        for j in range(un):
            c = i * un + j
            rows = pl.ds(pl.multiple_of(c * nb, nb), nb)
            k = qkv_ref[1, rows]
            shifted = sw_ref[0, c] * k
            for lag, prior in enumerate(priors(k, same)):
                shifted = shifted + sw_ref[lag + 1, c] * prior
            u_scr[rows, :] = shifted * qkv_ref[2, rows]
        return 0

    lax.fori_loop(0, chans // un, drive_step, 0)
    yield
    step_rows = 16 * nb

    def rev_step(i, _):
        rows = pl.ds(pl.multiple_of(i * step_rows, step_rows), step_rows)
        urev_ref[rows, :] = mm(u_scr[rows, :].astype(jnp.bfloat16), flip).astype(jnp.bfloat16)
        return 0

    lax.fori_loop(0, chans // 16, rev_step, 0)
    pos = iota((LANES, LANES), 0).astype(jnp.float32)
    factor = jnp.where(iota((LANES, LANES), 1) < ns, 1.0, pos)
    i8 = iota((8, LANES), 0).astype(jnp.float32)
    i16 = iota((LANES // 8, LANES), 0).astype(jnp.float32) * 8.0

    def fresh_step(i, _):
        for j in range(un):
            c = i * un + j
            rows = pl.ds(pl.multiple_of(c * nb, nb), nb)
            a = a_scr[pl.ds(c, 1), :]
            base = jnp.exp(-a * i8)
            tall = jnp.exp(-a * i16)
            p = (tall[:, None, :] * base[None]).reshape(LANES, LANES)
            pp = (p * factor).astype(jnp.bfloat16)
            pp_ref[pl.ds(pl.multiple_of(c * LANES, LANES), LANES), :] = pp
            urk = (urev_ref[rows, :].astype(jnp.float32) * keep_rev).astype(jnp.bfloat16)
            f_ref[rows, :] = mm(urk, pp)
        return 0

    lax.fori_loop(0, chans // un, fresh_step, 0)
    yield
    across = e_scr[0:chans, :]
    b_ext = b_scr[0:chans, :]
    state = jnp.zeros((chans, LANES), jnp.float32)
    for b in range(nb):
        s_ref[pl.ds(b, chans, stride=nb), :] = state + pltpu.roll(state, ns, axis=1)
        fresh = f_ref[pl.ds(b, chans, stride=nb), :]
        state = across * carry[b : b + 1, :] * state + b_ext * fresh

    yield

    def out_step(i, _):
        for j in range(un):
            c = i * un + j
            rows = pl.ds(pl.multiple_of(c * nb, nb), nb)
            t = toeplitz(kern_ref[pl.ds(c, 1), :])
            u = u_scr[rows, :]
            y = merge_masked(mm(stack_masked(u, masks), t), masks)
            sc = (s_ref[rows, :] * c_scr[pl.ds(c, 1), :]).astype(jnp.bfloat16)
            pp = pp_ref[pl.ds(pl.multiple_of(c * LANES, LANES), LANES), :]
            core = y + live * mm(sc, pp, NT) + skip_ref[0, c] * u
            core_ref[rows, :] = core
            u_scr[rows, :] = qkv_ref[0, rows] * core
        return 0

    lax.fori_loop(0, chans // un, out_step, 0)
    yield
    for b in range(nb):
        half = b % 2
        mixed_ref[b // 2, :, half * LANES : (half + 1) * LANES] = u_scr[
            pl.ds(b, chans, stride=nb), :
        ].astype(jnp.bfloat16)


def mixer_backward(
    un, gm_ref, qkv_ref, core_ref, s_ref, f_ref, urev_ref, pp_ref, kern_ref, seg_ref,
    sw_ref, skip_ref, rate_ref, inb_ref, outc_ref,
    dqkv_ref, dsw_ref, drate_ref, dinb_ref, doutc_ref, dskip_ref,
    tscr, b_scr, c_scr, e_scr, g_scr, sh_scr, h_scr, x_scr, dur_scr, dui_scr, dq_scr, dk_scr, dv_scr, gr_scr, red_scr,
):
    ns, chans = rate_ref.shape
    nb = qkv_ref.shape[1] // chans
    masks, live, keep, carry, same = seg_masks(read_seg(seg_ref, nb), nb)
    flip = flip_matrix()
    keep_rev = mm(keep.astype(jnp.bfloat16), flip)
    masks_rev = [mm(m.astype(jnp.bfloat16), flip) for m in masks]
    rate, in_b, out_c = rate_ref[...], inb_ref[...], outc_ref[...]
    decay = jnp.exp(-rate)
    b_scr[...] = transposed(tscr, in_b * decay, None)
    c_scr[...] = transposed(tscr, out_c, None)
    e_scr[...] = transposed(tscr, jnp.exp(-rate * LANES), None)
    red_scr[...] = jnp.zeros_like(red_scr)
    gr_scr[...] = jnp.zeros_like(gr_scr)

    for b in range(nb):
        half = b % 2
        x_scr[pl.ds(b, chans, stride=nb), :] = gm_ref[
            b // 2, :, half * LANES : (half + 1) * LANES
        ].astype(jnp.float32)
    corner = iota((LANES, LANES), 0) + iota((LANES, LANES), 1) >= LANES - 1

    def grad_step(i, _):
        for j in range(un):
            c = i * un + j
            rows = pl.ds(pl.multiple_of(c * nb, nb), nb)
            gm = x_scr[rows, :]
            dq_scr[rows, :] = gm * core_ref[rows, :]
            g = gm * qkv_ref[0, rows]
            g_scr[rows, :] = g
            k = qkv_ref[1, rows]
            shifted = sw_ref[0, c] * k
            for lag, prior in enumerate(priors(k, same)):
                shifted = shifted + sw_ref[lag + 1, c] * prior
            sh_scr[rows, :] = shifted
            red_scr[SHIFT, pl.ds(c, 1), :] = jnp.sum(
                g * shifted * qkv_ref[2, rows], axis=0, keepdims=True
            )
            ur = stack_masked(urev_ref[rows, :].astype(jnp.float32), masks_rev)
            cross = mm(ur, stack_masked(g, masks), TN)
            skew = pltpu.roll(jnp.where(corner, cross, 0.0), 1, axis=1, stride=1, stride_axis=0)
            gr_scr[pl.ds(c, 1), :] = jnp.sum(skew, axis=0, keepdims=True)
            pp = pp_ref[pl.ds(pl.multiple_of(c * LANES, LANES), LANES), :]
            h_scr[rows, :] = mm((g * live).astype(jnp.bfloat16), pp)
        return 0

    lax.fori_loop(0, chans // un, grad_step, 0)
    yield
    across = e_scr[0:chans, :]
    b_ext = b_scr[0:chans, :]
    c_ext = c_scr[0:chans, :]
    zero = jnp.zeros((chans, LANES), jnp.float32)
    adj, acc_out, acc_in, acc_carry = zero, zero, zero, zero
    for b in range(nb - 1, -1, -1):
        here = pl.ds(b, chans, stride=nb)
        h = h_scr[here, :]
        s = s_ref[here, :]
        acc_out = acc_out + s * h
        acc_in = acc_in + (adj + pltpu.roll(adj, ns, axis=1)) * f_ref[here, :]
        acc_carry = acc_carry + carry[b : b + 1, :] * adj * s
        x_scr[here, :] = b_ext * adj
        adj = c_ext * h + across * carry[b : b + 1, :] * adj

    yield

    def back_step(i, _):
        for j in range(un):
            c = i * un + j
            rows = pl.ds(pl.multiple_of(c * nb, nb), nb)
            t = toeplitz(kern_ref[pl.ds(c, 1), :])
            g = g_scr[rows, :]
            inner = merge_masked(mm(stack_masked(g, masks), t, NT), masks)
            pp = pp_ref[pl.ds(pl.multiple_of(c * LANES, LANES), LANES), :]
            dur_scr[rows, :] = (mm(x_scr[rows, :].astype(jnp.bfloat16), pp, NT) * keep_rev).astype(jnp.bfloat16)
            g_scr[rows, :] = inner + skip_ref[0, c] * g
        return 0

    lax.fori_loop(0, chans // un, back_step, 0)
    yield
    step_rows = 16 * nb

    def rev_step(i, _):
        rows = pl.ds(pl.multiple_of(i * step_rows, step_rows), step_rows)
        dui_scr[rows, :] = mm(dur_scr[rows, :], flip)
        return 0

    lax.fori_loop(0, chans // 16, rev_step, 0)

    def last_step(i, _):
        for j in range(un):
            c = i * un + j
            rows = pl.ds(pl.multiple_of(c * nb, nb), nb)
            du = g_scr[rows, :] + dui_scr[rows, :]
            dv_scr[rows, :] = du * sh_scr[rows, :]
            ds = du * qkv_ref[2, rows]
            k = qkv_ref[1, rows]
            lane = iota(k.shape, 1)
            red_scr[0, pl.ds(c, 1), :] = jnp.sum(ds * k, axis=0, keepdims=True)
            dk = sw_ref[0, c] * ds
            for lag, prior in enumerate(priors(k, same)):
                red_scr[lag + 1, pl.ds(c, 1), :] = jnp.sum(ds * prior, axis=0, keepdims=True)
                d = ds * same[lag]
                r = pltpu.roll(d, LANES - (lag + 1), axis=1)
                r2 = pltpu.roll(r, nb - 1, axis=0)
                dk = dk + sw_ref[lag + 1, c] * jnp.where(lane < LANES - (lag + 1), r, r2)
            dk_scr[rows, :] = dk
        return 0

    lax.fori_loop(0, chans // un, last_step, 0)
    yield
    for b in range(nb):
        half = b % 2
        for i, scr in enumerate((dq_scr, dk_scr, dv_scr)):
            dqkv_ref[b // 2, i, :, half * LANES : (half + 1) * LANES] = scr[
                pl.ds(b, chans, stride=nb), :
            ].astype(jnp.bfloat16)
    yield
    for j in range(SHIFT):
        dsw_ref[j : j + 1, :] = jnp.sum(red_scr[j].T, axis=0, keepdims=True)[:, 0:chans]
    dskip_ref[...] = jnp.sum(red_scr[SHIFT].T, axis=0, keepdims=True)[:, 0:chans]
    tscr[...] = gr_scr[...].T

    def kern_back(i, carried):
        e, zeroth, first = carried
        block = tscr[pl.ds(pl.multiple_of(i * 8, 8), 8), 0:chans]
        for j in range(8):
            term = e * block[j : j + 1, :]
            zeroth = zeroth + term
            first = first + term * (i * 8 + j).astype(jnp.float32)
            e = e * decay
        return e, zeroth, first

    blank = jnp.zeros((ns, chans), jnp.float32)
    _, zeroth, first = lax.fori_loop(0, LANES // 8, kern_back, (blank + 1.0, blank, blank))

    def back(x):
        tscr[...] = jnp.zeros_like(tscr)
        tscr[0:chans, :] = x
        y = tscr[...].T
        return y[0:ns, 0:chans], y[ns : 2 * ns, 0:chans]

    d_out, s_h1 = back(acc_out)
    d_inp, ds_f1 = back(acc_in)
    d_carry, _ = back(acc_carry)
    dinb_ref[...] = decay * d_inp + out_c * zeroth
    doutc_ref[...] = d_out + in_b * zeroth
    drate_ref[...] = -(
        out_c * s_h1
        + in_b * decay * (ds_f1 + d_inp)
        + LANES * jnp.exp(-rate * LANES) * d_carry
        + in_b * out_c * first
    )


MESH = pl.DeviceIdType.MESH


class Place:
    def __init__(self, n_dp, n_head, n_tensor):
        self.n_dp, self.n_head, self.n_tensor = n_dp, n_head, n_tensor
        self.dp = lax.axis_index("dp")
        h, t = lax.axis_index("head"), lax.axis_index("tensor")
        self.size = n_head * n_tensor
        ph, xh, yt = h + 1 - 2 * (h % 2), (h + 2) % n_head, 1 - t
        pxh = (ph + 2) % n_head
        slot = lambda a, b: a * n_tensor + b
        self.me, self.p, self.x, self.y, self.d = (
            slot(h, t), slot(ph, t), slot(xh, t), slot(h, yt), slot(xh, yt),
        )
        self.px, self.py, self.pd = slot(pxh, t), slot(ph, yt), slot(pxh, yt)
        self.to_p, self.to_x, self.to_y = {"head": ph}, {"head": xh}, {"tensor": yt}

    def dp_peer(self, step):
        return (self.dp + step) % self.n_dp

    def barrier(self, whole_group, over_dp):
        sem = pltpu.get_barrier_semaphore()

        def greet(where):
            pl.semaphore_signal(sem, inc=1, device_id=where, device_id_type=MESH)

        if whole_group:
            for i in range(1, self.size):
                peer = (self.me + i) % self.size
                greet({"head": peer // self.n_tensor, "tensor": peer % self.n_tensor})
            count = self.size - 1
        else:
            for where in (self.to_p, self.to_x, self.to_y):
                greet(where)
            count = 3
        if over_dp:
            def step(i, _):
                greet({"dp": self.dp_peer(i)})
                return 0

            lax.fori_loop(1, self.n_dp, step, 0)
            count += self.n_dp - 1
        pl.semaphore_wait(sem, count)


def remote(src, dst, ssem, rsem, where):
    return pltpu.make_async_remote_copy(
        src_ref=src, dst_ref=dst, send_sem=ssem, recv_sem=rsem, device_id=where, device_id_type=MESH
    )


class GroupGather:
    COPIES = 11

    def __init__(self, place, ref, ssem, rsem):
        self.ssem, self.rsem = ssem, rsem
        half = ref.shape[1] // 2
        top, low = pl.ds(0, half), pl.ds(half, half)
        pc = place
        full = lambda s: ref.at[s]
        part = lambda s, rows: ref.at[s, rows]
        self.out = [
            (full(pc.me), pc.to_p),
            (part(pc.me, top), pc.to_x), (part(pc.me, low), pc.to_x),
            (part(pc.me, low), pc.to_y), (part(pc.me, top), pc.to_y),
            (part(pc.x, top), pc.to_y), (part(pc.y, low), pc.to_x),
            (full(pc.x), pc.to_p), (full(pc.y), pc.to_p),
            (part(pc.d, top), pc.to_p), (part(pc.d, low), pc.to_p),
        ]
        self.into = [
            full(pc.p), part(pc.x, top), part(pc.x, low), part(pc.y, low), part(pc.y, top),
            part(pc.d, top), part(pc.d, low), full(pc.px), full(pc.py), part(pc.pd, top), part(pc.pd, low),
        ]

    def send(self, *which):
        for i in which:
            src, where = self.out[i]
            remote(src, src, self.ssem.at[i], self.rsem.at[i], where).start()

    def arrive(self, *which):
        for i in which:
            dst = self.into[i]
            remote(dst, dst, self.ssem.at[i], self.rsem.at[i], self.out[i][1]).wait_recv()

    def start(self):
        self.send(1, 3, 2, 4, 0)

    def first(self):
        self.arrive(1)
        self.send(5)
        self.arrive(3)
        self.send(6)

    def second(self):
        self.arrive(2)
        self.send(7)
        self.arrive(4)
        self.send(8)

    def third(self):
        self.arrive(5)
        self.send(9)
        self.arrive(6)
        self.send(10)

    def finish(self):
        self.arrive(0, 7, 8, 9, 10)

    def drain(self):
        for i in range(self.COPIES):
            src, where = self.out[i]
            remote(src, src, self.ssem.at[i], self.rsem.at[i], where).wait_send()


class DepthGather:
    def __init__(self, place, ref, ssem, rsem):
        self.place, self.ref, self.ssem, self.rsem = place, ref, ssem, rsem

    def _copy(self, step, slot, peer):
        return remote(
            self.ref.at[slot], self.ref.at[slot], self.ssem.at[step], self.rsem.at[step], {"dp": peer}
        )

    def _loop(self, body):
        def step(i, _):
            body(i)
            return 0

        lax.fori_loop(1, self.place.n_dp, step, 0)

    def start(self):
        pc = self.place
        self._loop(lambda i: self._copy(i, pc.dp, pc.dp_peer(i)).start())

    def finish(self):
        pc = self.place
        source = lambda i: (pc.dp + pc.n_dp - i) % pc.n_dp
        self._loop(lambda i: self._copy(i, source(i), pc.dp_peer(i)).wait_recv())

    def drain(self):
        pc = self.place
        self._loop(lambda i: self._copy(i, pc.dp, pc.dp_peer(i)).wait_send())


def joined(ref):
    n, rows, columns = ref.shape
    if rows % 16 == 0:
        return ref[...].reshape(n * rows, columns)
    parts = [ref[j].astype(jnp.float32) for j in range(n)]
    return jnp.concatenate(parts, axis=0).astype(ref.dtype)


def row_norm(x):
    centred = x - jnp.mean(x, axis=1, keepdims=True)
    inv = lax.rsqrt(jnp.mean(centred * centred, axis=1, keepdims=True) + 1e-05)
    return centred * inv, inv


class GroupReduce:
    COPIES = 10

    def __init__(self, place, part, land, half_land, last_land, ssem, rsem):
        pc = place
        self.pc = pc
        self.part, self.land, self.half_land, self.last_land = part, land, half_land, last_land
        self.ssem, self.rsem = ssem, rsem
        half = part.shape[1] // 2
        top, low = pl.ds(0, half), pl.ds(half, half)
        self.top, self.low = top, low
        self.mine = [pc.d, pc.x, pc.y, pc.me]
        self.theirs = [pc.pd, pc.px, pc.py, pc.p]
        self.copies = [(part.at[self.theirs[i]], land.at[i], pc.to_p) for i in range(4)] + [
            (part.at[pc.d, top], half_land.at[0], pc.to_x),
            (part.at[pc.d, low], half_land.at[1], pc.to_y),
            (part.at[pc.x, top], last_land.at[0, top], pc.to_x),
            (part.at[pc.y, low], last_land.at[1, low], pc.to_y),
            (part.at[pc.x, low], last_land.at[0, low], pc.to_x),
            (part.at[pc.y, top], last_land.at[1, top], pc.to_y),
        ]

    def _copy(self, i):
        src, dst, where = self.copies[i]
        return remote(src, dst, self.ssem.at[i], self.rsem.at[i], where)

    def give(self, *which):
        for i in which:
            self._copy(i).start()

    def pair(self, i):
        self._copy(i).wait_recv()
        s = self.mine[i]
        self.part[s] = (self.part[s].astype(jnp.float32) + self.land[i].astype(jnp.float32)).astype(
            self.part.dtype
        )

    def far(self):
        self.pair(0)
        self.give(4, 5)
        self.pair(1)
        self.give(6)
        self.pair(2)
        self.give(7)

    def near(self):
        for i, s, rows in ((4, self.pc.y, self.top), (5, self.pc.x, self.low)):
            self._copy(i).wait_recv()
            self.part[s, rows] = (
                self.part[s, rows].astype(jnp.float32) + self.half_land[i - 4].astype(jnp.float32)
            ).astype(self.part.dtype)
            self.give(9 if i == 4 else 8)

    def total(self):
        for i in (6, 7, 8, 9):
            self._copy(i).wait_recv()
        return (
            self.part[self.pc.me].astype(jnp.float32)
            + self.last_land[0].astype(jnp.float32)
            + self.last_land[1].astype(jnp.float32)
        )

    def drain(self):
        for i in range(self.COPIES):
            self._copy(i).wait_send()

    @staticmethod
    def scratch(group, rows, columns):
        bf16 = jnp.bfloat16
        return [
            pltpu.VMEM((group, rows, columns), bf16),
            pltpu.VMEM((4, rows, columns), bf16),
            pltpu.VMEM((2, rows // 2, columns), bf16),
            pltpu.VMEM((2, rows, columns), bf16),
        ]


class GroupSwap:
    def __init__(self, place, src, dst, lsem, ssem, rsem):
        self.pc, self.src, self.dst, self.ssem, self.rsem, self.lsem = place, src, dst, ssem, rsem, lsem

    def _peer(self, i):
        return (self.pc.me + i) % self.pc.size

    def _copy(self, i, slot):
        peer = self._peer(i)
        where = {"head": peer // self.pc.n_tensor, "tensor": peer % self.pc.n_tensor}
        return remote(self.src.at[peer], self.dst.at[slot], self.ssem.at[i], self.rsem.at[i], where)

    def _own(self):
        return pltpu.make_async_copy(self.src.at[self.pc.me], self.dst.at[self.pc.me], self.lsem)

    def start(self):
        for i in range(1, self.pc.size):
            self._copy(i, self.pc.me).start()
        self._own().start()

    def finish(self):
        for i in range(1, self.pc.size):
            self._copy(i, (self.pc.me + self.pc.size - i) % self.pc.size).wait_recv()
        self._own().wait()

    def drain(self):
        for i in range(1, self.pc.size):
            self._copy(i, self.pc.me).wait_send()


class DepthReduce:
    def __init__(self, place, src, land, ssem, rsem):
        self.place, self.src, self.land, self.ssem, self.rsem = place, src, land, ssem, rsem

    def _copy(self, step, mine, slot, peer):
        return remote(
            self.src.at[mine], self.land.at[slot], self.ssem.at[step], self.rsem.at[step], {"dp": peer}
        )

    def _loop(self, body, start):
        return lax.fori_loop(1, self.place.n_dp, body, start)

    def start(self):
        pc = self.place

        def step(i, _):
            self._copy(i, pc.dp_peer(i), pc.dp, pc.dp_peer(i)).start()
            return 0

        self._loop(step, 0)

    def total(self):
        pc = self.place

        def step(i, acc):
            source = (pc.dp + pc.n_dp - i) % pc.n_dp
            self._copy(i, source, source, pc.dp_peer(i)).wait_recv()
            return acc + self.land[source].astype(jnp.float32)

        return self._loop(step, self.src[pc.dp].astype(jnp.float32))

    def drain(self):
        pc = self.place

        def step(i, _):
            self._copy(i, pc.dp_peer(i), pc.dp, pc.dp_peer(i)).wait_send()
            return 0

        self._loop(step, 0)


def split_rows(ref, value):
    n, rows, columns = ref.shape
    if rows % 16 == 0:
        ref[...] = value.astype(ref.dtype).reshape(n, rows, columns)
    else:
        for j in range(n):
            ref[j] = value[j * rows : (j + 1) * rows].astype(ref.dtype)


def row_norm_back(grad, gain, hat, inv):
    scaled = grad * gain
    return inv * (
        scaled
        - jnp.mean(scaled, axis=1, keepdims=True)
        - hat * jnp.mean(scaled * hat, axis=1, keepdims=True)
    )


def gelu_pair(pre):
    cdf = 0.5 * (1.0 + lax.erf(pre * 0.7071067811865476))
    return pre * cdf, cdf + pre * (0.3989422804014327 * jnp.exp(-0.5 * pre * pre))


class GroupSpread:
    def __init__(self, place, ref, ssem, rsem):
        self.pc, self.ref, self.ssem, self.rsem = place, ref, ssem, rsem

    def _copy(self, i, slot):
        peer = (self.pc.me + i) % self.pc.size
        where = {"head": peer // self.pc.n_tensor, "tensor": peer % self.pc.n_tensor}
        return remote(self.ref.at[slot], self.ref.at[slot], self.ssem.at[i], self.rsem.at[i], where)

    def start(self):
        for i in range(1, self.pc.size):
            self._copy(i, self.pc.me).start()

    def finish(self):
        for i in range(1, self.pc.size):
            self._copy(i, (self.pc.me + self.pc.size - i) % self.pc.size).wait_recv()

    def drain(self):
        for i in range(1, self.pc.size):
            self._copy(i, self.pc.me).wait_send()


TAPS_AT, SKIP_AT, PARAM_ROWS = 192, 208, 224
UNROLL = 16


class Names:
    def __init__(self, names, refs):
        assert len(names) == len(refs)
        for name, ref in zip(names, refs):
            setattr(self, name, ref)


def layout(axes, own, feats, rows, chans, units, ns):
    n_dp, n_head, n_tensor = axes
    group = n_head * n_tensor
    f32, bf16 = jnp.float32, jnp.bfloat16
    v = pltpu.VMEM
    dma = lambda *shape: pltpu.SemaphoreType.DMA(shape)
    blocks = group * own // LANES
    conv = chans * blocks
    sq = v((LANES, LANES), f32)
    full = v((conv, LANES), f32)
    out = dict(
        tok=v((own, feats), bf16), cot=v((own, feats), bf16), four=v((4, rows, chans), bf16),
        wqkvo=v((n_dp, rows, 4 * chans), bf16), wup=v((n_dp, rows, units), bf16), wdown=v((n_dp, rows, units), bf16),
        wt=v((4 * chans, feats), bf16), wupt=v((units, feats), bf16), wdownt=v((units, feats), bf16),
        wout=v((group, chans, feats), bf16),
        xn1=v((group, feats, own), bf16), cots=v((group, feats, own), bf16), xn2=v((group, feats, own), bf16),
        act=v((group, units, own), bf16), gpre=v((group, units, own), bf16),
        qkv=v((3, conv, LANES), f32), core=full, s=full, f=full, urev=v((conv, LANES), bf16),
        pp=v((chans * LANES, LANES), bf16), kern=v((chans, LANES), f32),
        mixed=v((group, chans, own), bf16), mixed_in=v((group, chans, own), bf16),
        gmix=v((group, chans, own), bf16), gmix_in=v((group, chans, own), bf16),
        dqkv=v((group, 3, chans, own), bf16),
        t0=sq, t1=sq, t2=sq, t3=sq, t4=sq, t5=sq, gr=sq, red=v((SHIFT + 1, LANES, LANES), f32),
        w0=full, w1=full, w2=full, w3=full, w4=full, w5=full, w6=full, dur=v((conv, LANES), bf16),
        dsw=v((SHIFT, chans), f32), drate=v((ns, chans), f32), dinb=v((ns, chans), f32), doutc=v((ns, chans), f32),
        dskip=v((1, chans), f32),
        hat=v((own, feats), f32), hid=v((own, feats), f32), ghid=v((own, feats), f32),
        up_part=v((n_dp, rows, units), bf16), up_land=v((n_dp, rows, units), bf16),
        dn_part=v((n_dp, rows, units), bf16), dn_land=v((n_dp, rows, units), bf16),
        w_part=v((n_dp, rows, 4 * chans), bf16), w_land=v((n_dp, rows, 4 * chans), bf16),
        params=v((n_dp, PARAM_ROWS, LANES), bf16),
        n1=v((group, 2, feats), f32), n2=v((group, 2, feats), f32), m1=v((n_dp, 2, feats), f32), m2=v((n_dp, 2, feats), f32),
    )
    for name, height, width in (("x", feats, own), ("m", feats, own), ("o", chans, feats)):
        for part, alloc in zip(("part", "land", "half", "last"), GroupReduce.scratch(group, height, width)):
            out[f"{name}_{part}"] = alloc
    for name, count in (
        ("xn1", 11), ("cots", 11), ("wout", 11), ("xn2", 11), ("x2", 10), ("m", 10), ("o", 10), ("x1", 10),
        ("in", group), ("back", group), ("sp1", group), ("sp2", group),
        ("zq", n_dp), ("zu", n_dp), ("zd", n_dp), ("gu", n_dp), ("gd", n_dp), ("gw", n_dp), ("zp", n_dp),
        ("zn1", n_dp), ("zn2", n_dp),
    ):
        out[f"send_{name}"] = dma(count)
        out[f"recv_{name}"] = dma(count)
    out["local"] = dma(12)
    return out


INPUTS = (
    "tok_hbm", "cot_hbm", "q_hbm", "k_hbm", "v_hbm", "o_hbm", "up_hbm", "down_hbm",
    "seg", "gain1", "bias1", "gain2", "bias2", "taps", "rate", "inb", "outc", "skip",
)
OUTPUTS = (
    "res", "gx", "g1", "b1", "g2", "b2", "dq", "dk", "dv", "do", "dup", "ddown",
    "out_taps", "out_rate", "out_inb", "out_outc", "out_skip",
)


def run_beside(body, tasks):
    tasks = list(tasks)
    for _ in body:
        if tasks:
            tasks.pop(0)()
    for task in tasks:
        task()


def block_kernel(axes, names, *refs):
    r = Names(names, refs)
    pc = Place(*axes)
    f32, bf16 = jnp.float32, jnp.bfloat16
    group, chans, feats = r.wout.shape
    own = r.tok.shape[0]
    blocks = own // LANES
    work = []

    def sems(name):
        return getattr(r, f"send_{name}"), getattr(r, f"recv_{name}")

    def make(kind, name, *args):
        made = kind(pc, *args, *sems(name))
        work.append(made)
        return made

    def local(i, src, dst):
        copy = pltpu.make_async_copy(src, dst, r.local.at[i])
        copy.start()
        return copy

    four = [local(i, src, r.four.at[i]) for i, src in enumerate((r.q_hbm, r.k_hbm, r.v_hbm, r.o_hbm))]
    load_tok = local(4, r.tok_hbm, r.tok)
    load_cot = local(5, r.cot_hbm, r.cot)
    load_up = local(6, r.up_hbm, r.wup.at[pc.dp])
    load_down = local(7, r.down_hbm, r.wdown.at[pc.dp])
    pc.barrier(True, True)
    for copy in four:
        copy.wait()
    r.wqkvo[pc.dp] = jnp.concatenate([r.four[i] for i in range(4)], axis=1)
    z_qkvo = make(DepthGather, "zq", r.wqkvo)
    z_up = make(DepthGather, "zu", r.wup)
    z_down = make(DepthGather, "zd", r.wdown)
    xn1_g = make(GroupGather, "xn1", r.xn1)
    cot_g = make(GroupGather, "cots", r.cots)
    out_g = make(GroupGather, "wout", r.wout)
    xn2_g = make(GroupGather, "xn2", r.xn2)
    z_qkvo.start()
    load_tok.wait()
    x = r.tok[...].astype(f32)
    gain1, gain2 = r.gain1[...].reshape(1, feats), r.gain2[...].reshape(1, feats)
    bias1, bias2 = r.bias1[...].reshape(1, feats), r.bias2[...].reshape(1, feats)
    hat1, _ = row_norm(x)
    r.xn1[pc.me] = (hat1 * gain1 + bias1).astype(bf16).T
    xn1_g.start()
    load_up.wait()
    z_up.start()
    load_down.wait()
    z_down.start()
    load_cot.wait()
    r.cots[pc.me] = r.cot[...].T
    xn1_g.first()
    cot_g.start()
    xn1_g.second()
    z_qkvo.finish()
    r.wt[...] = joined(r.wqkvo).T
    r.wout[pc.me] = r.wt[3 * chans :, :]
    out_g.start()

    def project(s):
        y = mm(r.wt[0 : 3 * chans, :], r.xn1[s])
        for i in range(3):
            for h in range(blocks):
                r.qkv[i, pl.ds(s * blocks + h, chans, stride=group * blocks), :] = y[
                    i * chans : (i + 1) * chans, h * LANES : (h + 1) * LANES
                ]

    xn1_g.third()
    xn1_g.finish()
    for s in range(group):
        project(s)

    def cot_first():
        cot_g.first()

    def cot_second():
        cot_g.second()
        out_g.first()

    def late_weights():
        z_up.finish()
        r.wupt[...] = joined(r.wup).T
        out_g.second()

    def cot_third():
        cot_g.third()
        out_g.third()

    mixer = (r.seg, r.taps, r.skip, r.rate, r.inb, r.outc)
    run_beside(
        mixer_forward(
            UNROLL, r.qkv, *mixer, r.mixed, r.core, r.s, r.f, r.urev, r.pp, r.kern,
            r.t0, r.t1, r.t2, r.t3, r.t4, r.w0, r.t5,
        ),
        (cot_first, cot_second, late_weights, cot_third),
    )
    swap_in = make(GroupSwap, "in", r.mixed, r.mixed_in, r.local.at[8])
    swap_in.start()
    out_g.finish()
    cot_g.finish()
    z_down.finish()
    w_down = joined(r.wdown)
    r.wdownt[...] = w_down.T
    w_up = joined(r.wup)
    swap_in.finish()
    mixed_t = r.mixed_in[...].reshape(feats, own)
    wout_t = r.wout[...].reshape(feats, feats)
    hidden = r.tok[...].astype(f32) + mm(mixed_t, wout_t, TN)
    r.hid[...] = hidden
    hat2, inv2 = row_norm(hidden)
    r.xn2[pc.me] = (hat2 * gain2 + bias2).astype(bf16).T
    xn2_g.start()
    r.hat[...] = hat2
    red_x2 = make(GroupReduce, "x2", r.x_part, r.x_land, r.x_half, r.x_last)
    red_m = make(GroupReduce, "m", r.m_part, r.m_land, r.m_half, r.m_last)
    red_o = make(GroupReduce, "o", r.o_part, r.o_land, r.o_half, r.o_last)

    def chunk(s):
        act, slope = gelu_pair(mm(r.wupt[...], r.xn2[s]))
        r.act[s] = act.astype(bf16)
        grad_pre = (mm(r.wdownt[...], r.cots[s]) * slope).astype(bf16)
        r.gpre[s] = grad_pre
        r.x_part[s] = mm(w_up, grad_pre).astype(bf16)

    chunk(pc.me)
    xn2_g.arrive(0)
    chunk(pc.p)
    red_x2.give(3)
    xn2_g.first()
    xn2_g.second()
    chunk(pc.x)
    chunk(pc.y)
    xn2_g.arrive(7)
    chunk(pc.px)
    red_x2.give(1)
    xn2_g.arrive(8)
    chunk(pc.py)
    red_x2.give(2)
    xn2_g.third()
    chunk(pc.d)
    xn2_g.arrive(9, 10)
    chunk(pc.pd)
    red_x2.give(0)
    red_x2.far()
    units = r.act.shape[1]
    grad_up = jnp.zeros((feats, units), f32)
    for s in range(group):
        grad_up = grad_up + mm(r.xn2[s], r.gpre[s], NT)
    split_rows(r.up_part, grad_up)
    sum_up = make(DepthReduce, "gu", r.up_part, r.up_land)
    sum_up.start()
    red_x2.near()
    red_x2.pair(3)
    for i, s in enumerate(red_m.theirs):
        r.m_part[s] = mm(w_down, r.act[s]).astype(bf16)
        red_m.give(i)
    for s in red_m.mine:
        r.m_part[s] = mm(w_down, r.act[s]).astype(bf16)
    grad_down = jnp.zeros((feats, units), f32)
    for s in range(group):
        grad_down = grad_down + mm(r.cots[s], r.act[s], NT)
    split_rows(r.dn_part, grad_down)
    sum_down = make(DepthReduce, "gd", r.dn_part, r.dn_land)
    sum_down.start()
    grad_xn = red_x2.total().T
    hat2 = r.hat[...]
    grad_hidden = r.cot[...].astype(f32) + row_norm_back(grad_xn, gain2, hat2, inv2)
    r.ghid[...] = grad_hidden
    grad_mix = grad_hidden.astype(bf16)
    r.gmix[...] = mm(wout_t, grad_mix, NT).astype(bf16).reshape(group, chans, own)
    swap_back = make(GroupSwap, "back", r.gmix, r.gmix_in, r.local.at[9])
    swap_back.start()
    r.n2[pc.me, 0:1, :] = jnp.sum(grad_xn * hat2, axis=0, keepdims=True)
    r.n2[pc.me, 1:2, :] = jnp.sum(grad_xn, axis=0, keepdims=True)
    spread2 = make(GroupSpread, "sp2", r.n2)
    spread2.start()
    r.o_part[...] = mm(mixed_t, grad_mix).astype(bf16).reshape(group, chans, feats)
    red_o.give(0, 1, 2, 3)
    red_m.far()
    red_o.far()
    swap_back.finish()
    norm2 = make(DepthGather, "zn2", r.m2)

    def near_sums():
        red_m.near()
        red_o.near()
        spread2.finish()
        r.m2[pc.dp] = jnp.sum(r.n2[...], axis=0)
        norm2.start()

    def own_sums():
        red_m.pair(3)
        red_o.pair(3)
        red_x2.drain()
        work.remove(red_x2)

    def last_sums():
        r.res[...] = (r.hid[...] + red_m.total().T).astype(bf16)
        norm2.finish()
        sums = jnp.sum(r.m2[...], axis=0)
        r.g2[...] = sums[0:1]
        r.b2[...] = sums[1:2]

    def depth_sums():
        r.dup[...] = sum_up.total()
        r.ddown[...] = sum_down.total()

    w_joint = joined(r.wqkvo)
    red_x1 = make(GroupReduce, "x1", r.x_part, r.x_land, r.x_half, r.x_last)

    def grads(s):
        return r.dqkv[s].reshape(3 * chans, own)

    def chunk_back(s):
        padded = jnp.concatenate([grads(s), jnp.zeros((chans, own), bf16)], axis=0)
        r.x_part[s] = mm(w_joint, padded).astype(bf16)

    def start_back():
        for i, s in enumerate(red_x1.theirs):
            chunk_back(s)
            red_x1.give(i)
        for s in red_x1.mine:
            chunk_back(s)

    run_beside(
        mixer_backward(
            UNROLL, r.gmix_in, r.qkv, r.core, r.s, r.f, r.urev, r.pp, r.kern, *mixer,
            r.dqkv, r.dsw, r.drate, r.dinb, r.doutc, r.dskip,
            r.t0, r.t1, r.t2, r.t3, r.w0, r.w1, r.w2, r.w3, r.dur, r.w2, r.w4, r.w5, r.w6, r.gr, r.red,
        ),
        (near_sums, own_sums, last_sums, depth_sums, start_back),
    )
    red_x1.far()
    r.params[pc.dp] = jnp.zeros(r.params.shape[1:], bf16)
    ns = r.drate.shape[0]
    pieces = ((0, r.drate, r.out_rate), (ns, r.dinb, r.out_inb), (2 * ns, r.doutc, r.out_outc),
              (TAPS_AT, r.dsw, r.out_taps), (SKIP_AT, r.dskip, r.out_skip))
    for at, ref, _ in pieces:
        r.params[pc.dp, at : at + ref.shape[0], 0:chans] = ref[...].astype(bf16)
    z_par = make(DepthGather, "zp", r.params)
    z_par.start()
    grad_w = jnp.zeros((feats, 3 * chans), f32)
    for s in range(group):
        grad_w = grad_w + mm(r.xn1[s], grads(s), NT)
    split_rows(r.w_part, jnp.concatenate([grad_w, red_o.total().T], axis=1))
    sum_w = make(DepthReduce, "gw", r.w_part, r.w_land)
    sum_w.start()
    red_x1.near()
    red_x1.pair(3)
    hat1, inv1 = row_norm(r.tok[...].astype(f32))
    grad_xn = red_x1.total().T
    r.n1[pc.me, 0:1, :] = jnp.sum(grad_xn * hat1, axis=0, keepdims=True)
    r.n1[pc.me, 1:2, :] = jnp.sum(grad_xn, axis=0, keepdims=True)
    spread1 = make(GroupSpread, "sp1", r.n1)
    spread1.start()
    r.gx[...] = r.ghid[...] + row_norm_back(grad_xn, gain1, hat1, inv1)
    spread1.finish()
    r.m1[pc.dp] = jnp.sum(r.n1[...], axis=0)
    norm1 = make(DepthGather, "zn1", r.m1)
    norm1.start()
    z_par.finish()
    sums = jnp.sum(r.params[...].astype(f32), axis=0)
    for at, ref, out in pieces:
        out[...] = sums[at : at + ref.shape[0], 0:chans]
    norm1.finish()
    sums = jnp.sum(r.m1[...], axis=0)
    r.g1[...] = sums[0:1]
    r.b1[...] = sums[1:2]
    w_sum = sum_w.total()
    for i, ref in enumerate((r.dq, r.dk, r.dv, r.do)):
        ref[...] = w_sum[:, i * chans : (i + 1) * chans]
    for one in work:
        one.drain()


def hand_over(*refs):
    n = len(refs) // 2
    for src, dst in zip(refs[:n], refs[n:]):
        dst[...] = src[...].reshape(dst.shape)


def whole_block(axes, args):
    (tokens, seg, gain1, bias1, gain2, bias2, q, k, v, o, up, down, taps, rate, inb, outc, skip, cot) = args
    own, feats = tokens.shape
    rows, chans = q.shape
    units = up.shape[1]
    f32, bf16 = jnp.float32, jnp.bfloat16
    sds = jax.ShapeDtypeStruct
    vm = pl.BlockSpec(memory_space=pltpu.VMEM)
    sm = pl.BlockSpec(memory_space=pltpu.SMEM)
    hbm = pl.BlockSpec(memory_space=pl.ANY)
    scratch = layout(axes, own, feats, rows, chans, units, rate.shape[0])
    wide, thin = sds((rows, units), f32), sds((rows, chans), f32)
    row = sds((1, feats), f32)
    outs = pl.pallas_call(
        functools.partial(block_kernel, axes, INPUTS + OUTPUTS + tuple(scratch)),
        out_shape=(
            sds((own, feats), bf16), sds((own, feats), f32), row, row, row, row, thin, thin, thin, thin, wide, wide,
            *(sds(a.shape, f32) for a in (taps, rate, inb, outc)), sds((1, chans), f32),
        ),
        in_specs=[hbm] * 8 + [vm] * 5 + [sm] + [vm] * 3 + [sm],
        out_specs=(vm,) * 17,
        scratch_shapes=list(scratch.values()),
        compiler_params=pltpu.CompilerParams(
            collective_id=1, has_side_effects=True, vmem_limit_bytes=63 << 20
        ),
        name="block",
    )(tokens, cot, q, k, v, o, up, down, seg, gain1, bias1, gain2, bias2, taps, rate, inb, outc, skip[None])
    final = [sds(a.shape, a.dtype) for a in outs]
    for i in (2, 3, 4, 5):
        final[i] = sds((feats,), f32)
    final[16] = sds((chans,), f32)
    return pl.pallas_call(
        hand_over, out_shape=tuple(final), in_specs=[vm] * 17, out_specs=(vm,) * 17, name="hand_over",
    )(*outs)


from jax.sharding import PartitionSpec as P

GROUP = ("head", "tensor")


def on_device(*args):
    return whole_block((lax.axis_size("dp"), lax.axis_size("head"), lax.axis_size("tensor")), args)


def solution(mesh):
    rows = P(("dp", "head", "tensor"), None)
    weight = P("dp", GROUP)
    chan = P(None, GROUP)
    in_specs = (rows, P("dp", None)) + (P(),) * 4 + (weight,) * 6 + (chan,) * 4 + (P(GROUP), rows)
    out_specs = (rows, rows) + (P(),) * 4 + (weight,) * 6 + (chan,) * 4 + (P(GROUP),)
    return jax.shard_map(on_device, mesh=mesh, in_specs=in_specs, out_specs=out_specs, check_vma=False)
```

```python
import functools
import jax, jax.numpy as jnp
from jax import lax
from jax.experimental import pallas as pl
from jax.experimental.pallas import tpu as pltpu

LANES = 128
SHIFT = 4
SEQS = 3
PARTS = 2
NT = (((1,), (1,)), ((), ()))
TN = (((0,), (0,)), ((), ()))
NN = (((1,), (0,)), ((), ()))


def mm(left, right, dims=NN):
    return lax.dot_general(left, right, dims, preferred_element_type=jnp.float32)


def iota(shape, axis):
    return lax.broadcasted_iota(jnp.int32, shape, axis)


def seg_masks(seg, nb):
    lane = iota((nb, LANES), 1)
    row = iota((nb, LANES), 0)
    masks = [(seg == k).astype(jnp.float32) for k in range(SEQS)]
    end = jnp.broadcast_to(seg[:, LANES - 1 :], (nb, LANES))
    last = jnp.where(row == 0, -1, pltpu.roll(end, 1, axis=0))
    live = (seg == last).astype(jnp.float32)
    keep = (seg == end).astype(jnp.float32)
    carry = (end == last).astype(jnp.float32)
    same = []
    for j in range(1, SHIFT):
        r = pltpu.roll(seg, j, axis=1)
        r2 = pltpu.roll(r, 1, axis=0)
        prior = jnp.where(lane < j, r2, r)
        ok = (prior == seg) & ((row > 0) | (lane >= j))
        same.append(ok.astype(jnp.float32))
    return masks, live, keep, carry, same


def priors(k, same):
    lane = iota(k.shape, 1)
    out = []
    for j in range(1, SHIFT):
        r = pltpu.roll(k, j, axis=1)
        r2 = pltpu.roll(r, 1, axis=0)
        out.append(jnp.where(lane < j, r2, r) * same[j - 1])
    return out


def flip_matrix():
    return (iota((LANES, LANES), 0) + iota((LANES, LANES), 1) == LANES - 1).astype(jnp.bfloat16)


def read_seg(seg_ref, nb):
    return jnp.concatenate([seg_ref[:, b * LANES : (b + 1) * LANES] for b in range(nb)], axis=0)


def transposed(scr, top, bottom):
    ns, chans = top.shape
    scr[...] = jnp.zeros_like(scr)
    scr[0:ns, 0:chans] = top
    if bottom is not None:
        scr[ns : 2 * ns, 0:chans] = bottom
    return scr[...].T


def stack_masked(x, masks):
    return jnp.concatenate([x * m for m in masks], axis=0).astype(jnp.bfloat16)


def merge_masked(y, masks):
    nb = masks[0].shape[0]
    return sum(y[i * nb : (i + 1) * nb] * m for i, m in enumerate(masks))


def toeplitz(krow):
    t = pltpu.roll(jnp.broadcast_to(krow, (LANES, LANES)), 0, axis=1, stride=1, stride_axis=0)
    return jnp.where(iota((LANES, LANES), 1) >= iota((LANES, LANES), 0), t, 0.0).astype(jnp.bfloat16)


def mixer_forward(
    un, qkv_ref, seg_ref, sw_ref, skip_ref, rate_ref, inb_ref, outc_ref,
    mixed_ref, core_ref, s_ref, f_ref, urev_ref, pp_ref, kern_ref,
    tscr, a_scr, b_scr, c_scr, e_scr, u_scr, kscr,
):
    ns, chans = rate_ref.shape
    nb = qkv_ref.shape[1] // chans
    masks, live, keep, carry, same = seg_masks(read_seg(seg_ref, nb), nb)
    flip = flip_matrix()
    keep_rev = mm(keep.astype(jnp.bfloat16), flip)
    rate, in_b, out_c = rate_ref[...], inb_ref[...], outc_ref[...]
    decay = jnp.exp(-rate)
    a_scr[...] = transposed(tscr, rate, rate)
    b_scr[...] = transposed(tscr, in_b * decay, None)
    c_scr[...] = transposed(tscr, out_c, None)
    e_scr[...] = transposed(tscr, jnp.exp(-rate * LANES), None)

    def kern_step(i, e):
        for j in range(8):
            kscr[pl.ds(i * 8 + j, 1), 0:chans] = jnp.sum(e, axis=0, keepdims=True)
            e = e * decay
        return e

    kscr[...] = jnp.zeros_like(kscr)
    lax.fori_loop(0, LANES // 8, kern_step, in_b * out_c)
    kern_ref[...] = kscr[...].T[0:chans]

    def drive_step(i, _):
        for j in range(un):
            c = i * un + j
            rows = pl.ds(pl.multiple_of(c * nb, nb), nb)
            k = qkv_ref[1, rows]
            shifted = sw_ref[0, c] * k
            for lag, prior in enumerate(priors(k, same)):
                shifted = shifted + sw_ref[lag + 1, c] * prior
            u_scr[rows, :] = shifted * qkv_ref[2, rows]
        return 0

    lax.fori_loop(0, chans // un, drive_step, 0)
    yield
    step_rows = 16 * nb

    def rev_step(i, _):
        rows = pl.ds(pl.multiple_of(i * step_rows, step_rows), step_rows)
        urev_ref[rows, :] = mm(u_scr[rows, :].astype(jnp.bfloat16), flip).astype(jnp.bfloat16)
        return 0

    lax.fori_loop(0, chans // 16, rev_step, 0)
    pos = iota((LANES, LANES), 0).astype(jnp.float32)
    factor = jnp.where(iota((LANES, LANES), 1) < ns, 1.0, pos)
    i8 = iota((8, LANES), 0).astype(jnp.float32)
    i16 = iota((LANES // 8, LANES), 0).astype(jnp.float32) * 8.0

    def fresh_step(i, _):
        for j in range(un):
            c = i * un + j
            rows = pl.ds(pl.multiple_of(c * nb, nb), nb)
            a = a_scr[pl.ds(c, 1), :]
            base = jnp.exp(-a * i8)
            tall = jnp.exp(-a * i16)
            p = (tall[:, None, :] * base[None]).reshape(LANES, LANES)
            pp = (p * factor).astype(jnp.bfloat16)
            pp_ref[pl.ds(pl.multiple_of(c * LANES, LANES), LANES), :] = pp
            urk = (urev_ref[rows, :].astype(jnp.float32) * keep_rev).astype(jnp.bfloat16)
            f_ref[rows, :] = mm(urk, pp)
        return 0

    for part in range(PARTS):
        lax.fori_loop(part * chans // PARTS // un, (part + 1) * chans // PARTS // un, fresh_step, 0)
        yield
    across = e_scr[0:chans, :]
    b_ext = b_scr[0:chans, :]
    state = jnp.zeros((chans, LANES), jnp.float32)
    for b in range(nb):
        s_ref[pl.ds(b, chans, stride=nb), :] = state + pltpu.roll(state, ns, axis=1)
        fresh = f_ref[pl.ds(b, chans, stride=nb), :]
        state = across * carry[b : b + 1, :] * state + b_ext * fresh

    yield

    def out_step(i, _):
        for j in range(un):
            c = i * un + j
            rows = pl.ds(pl.multiple_of(c * nb, nb), nb)
            t = toeplitz(kern_ref[pl.ds(c, 1), :])
            u = u_scr[rows, :]
            y = merge_masked(mm(stack_masked(u, masks), t), masks)
            sc = (s_ref[rows, :] * c_scr[pl.ds(c, 1), :]).astype(jnp.bfloat16)
            pp = pp_ref[pl.ds(pl.multiple_of(c * LANES, LANES), LANES), :]
            core = y + live * mm(sc, pp, NT) + skip_ref[0, c] * u
            core_ref[rows, :] = core
            u_scr[rows, :] = qkv_ref[0, rows] * core
        return 0

    count = chans // PARTS
    for part in range(PARTS):
        lax.fori_loop(part * count // un, (part + 1) * count // un, out_step, 0)
        for b in range(nb):
            half = b % 2
            mixed_ref[b // 2, part * count : (part + 1) * count, half * LANES : (half + 1) * LANES] = u_scr[
                pl.ds(part * count * nb + b, count, stride=nb), :
            ].astype(jnp.bfloat16)
        yield


def mixer_backward(
    un, gm_ref, qkv_ref, core_ref, s_ref, f_ref, urev_ref, pp_ref, kern_ref, seg_ref,
    sw_ref, skip_ref, rate_ref, inb_ref, outc_ref,
    dqkv_ref, dsw_ref, drate_ref, dinb_ref, doutc_ref, dskip_ref,
    tscr, b_scr, c_scr, e_scr, g_scr, sh_scr, h_scr, x_scr, dur_scr, dui_scr, dq_scr, dk_scr, dv_scr, gr_scr, red_scr,
):
    ns, chans = rate_ref.shape
    nb = qkv_ref.shape[1] // chans
    masks, live, keep, carry, same = seg_masks(read_seg(seg_ref, nb), nb)
    flip = flip_matrix()
    keep_rev = mm(keep.astype(jnp.bfloat16), flip)
    masks_rev = [mm(m.astype(jnp.bfloat16), flip) for m in masks]
    rate, in_b, out_c = rate_ref[...], inb_ref[...], outc_ref[...]
    decay = jnp.exp(-rate)
    b_scr[...] = transposed(tscr, in_b * decay, None)
    c_scr[...] = transposed(tscr, out_c, None)
    e_scr[...] = transposed(tscr, jnp.exp(-rate * LANES), None)
    red_scr[...] = jnp.zeros_like(red_scr)
    gr_scr[...] = jnp.zeros_like(gr_scr)

    corner = iota((LANES, LANES), 0) + iota((LANES, LANES), 1) >= LANES - 1

    def grad_step(i, _):
        for j in range(un):
            c = i * un + j
            rows = pl.ds(pl.multiple_of(c * nb, nb), nb)
            gm = x_scr[rows, :]
            dq_scr[rows, :] = gm * core_ref[rows, :]
            g = gm * qkv_ref[0, rows]
            g_scr[rows, :] = g
            k = qkv_ref[1, rows]
            shifted = sw_ref[0, c] * k
            for lag, prior in enumerate(priors(k, same)):
                shifted = shifted + sw_ref[lag + 1, c] * prior
            sh_scr[rows, :] = shifted
            red_scr[SHIFT, pl.ds(c, 1), :] = jnp.sum(
                g * shifted * qkv_ref[2, rows], axis=0, keepdims=True
            )
            ur = stack_masked(urev_ref[rows, :].astype(jnp.float32), masks_rev)
            cross = mm(ur, stack_masked(g, masks), TN)
            skew = pltpu.roll(jnp.where(corner, cross, 0.0), 1, axis=1, stride=1, stride_axis=0)
            gr_scr[pl.ds(c, 1), :] = jnp.sum(skew, axis=0, keepdims=True)
            pp = pp_ref[pl.ds(pl.multiple_of(c * LANES, LANES), LANES), :]
            h_scr[rows, :] = mm((g * live).astype(jnp.bfloat16), pp)
        return 0

    count = chans // PARTS
    for part in range(PARTS):
        for b in range(nb):
            half = b % 2
            x_scr[pl.ds(part * count * nb + b, count, stride=nb), :] = gm_ref[
                b // 2, part * count : (part + 1) * count, half * LANES : (half + 1) * LANES
            ].astype(jnp.float32)
        lax.fori_loop(part * count // un, (part + 1) * count // un, grad_step, 0)
        yield
    for b in range(nb):
        half = b % 2
        dqkv_ref[b // 2, 0, :, half * LANES : (half + 1) * LANES] = dq_scr[
            pl.ds(b, chans, stride=nb), :
        ].astype(jnp.bfloat16)
    across = e_scr[0:chans, :]
    b_ext = b_scr[0:chans, :]
    c_ext = c_scr[0:chans, :]
    zero = jnp.zeros((chans, LANES), jnp.float32)
    adj, acc_out, acc_in, acc_carry = zero, zero, zero, zero
    for b in range(nb - 1, -1, -1):
        here = pl.ds(b, chans, stride=nb)
        h = h_scr[here, :]
        s = s_ref[here, :]
        acc_out = acc_out + s * h
        acc_in = acc_in + (adj + pltpu.roll(adj, ns, axis=1)) * f_ref[here, :]
        acc_carry = acc_carry + carry[b : b + 1, :] * adj * s
        x_scr[here, :] = b_ext * adj
        adj = c_ext * h + across * carry[b : b + 1, :] * adj

    dskip_ref[...] = jnp.sum(red_scr[SHIFT].T, axis=0, keepdims=True)[:, 0:chans]
    tscr[...] = gr_scr[...].T

    def kern_back(i, carried):
        e, zeroth, first = carried
        block = tscr[pl.ds(pl.multiple_of(i * 8, 8), 8), 0:chans]
        for j in range(8):
            term = e * block[j : j + 1, :]
            zeroth = zeroth + term
            first = first + term * (i * 8 + j).astype(jnp.float32)
            e = e * decay
        return e, zeroth, first

    blank = jnp.zeros((ns, chans), jnp.float32)
    _, zeroth, first = lax.fori_loop(0, LANES // 8, kern_back, (blank + 1.0, blank, blank))

    def back(x):
        tscr[...] = jnp.zeros_like(tscr)
        tscr[0:chans, :] = x
        y = tscr[...].T
        return y[0:ns, 0:chans], y[ns : 2 * ns, 0:chans]

    d_out, s_h1 = back(acc_out)
    d_inp, ds_f1 = back(acc_in)
    d_carry, _ = back(acc_carry)
    dinb_ref[...] = decay * d_inp + out_c * zeroth
    doutc_ref[...] = d_out + in_b * zeroth
    drate_ref[...] = -(
        out_c * s_h1
        + in_b * decay * (ds_f1 + d_inp)
        + LANES * jnp.exp(-rate * LANES) * d_carry
        + in_b * out_c * first
    )
    yield

    def back_step(i, _):
        for j in range(un):
            c = i * un + j
            rows = pl.ds(pl.multiple_of(c * nb, nb), nb)
            t = toeplitz(kern_ref[pl.ds(c, 1), :])
            g = g_scr[rows, :]
            inner = merge_masked(mm(stack_masked(g, masks), t, NT), masks)
            pp = pp_ref[pl.ds(pl.multiple_of(c * LANES, LANES), LANES), :]
            dur_scr[rows, :] = (mm(x_scr[rows, :].astype(jnp.bfloat16), pp, NT) * keep_rev).astype(jnp.bfloat16)
            g_scr[rows, :] = inner + skip_ref[0, c] * g
        return 0

    lax.fori_loop(0, chans // un, back_step, 0)
    yield
    step_rows = 16 * nb

    def rev_step(i, _):
        rows = pl.ds(pl.multiple_of(i * step_rows, step_rows), step_rows)
        dui_scr[rows, :] = mm(dur_scr[rows, :], flip)
        return 0

    lax.fori_loop(0, chans // 16, rev_step, 0)

    def last_step(i, _):
        for j in range(un):
            c = i * un + j
            rows = pl.ds(pl.multiple_of(c * nb, nb), nb)
            du = g_scr[rows, :] + dui_scr[rows, :]
            dv_scr[rows, :] = du * sh_scr[rows, :]
            ds = du * qkv_ref[2, rows]
            k = qkv_ref[1, rows]
            lane = iota(k.shape, 1)
            red_scr[0, pl.ds(c, 1), :] = jnp.sum(ds * k, axis=0, keepdims=True)
            dk = sw_ref[0, c] * ds
            for lag, prior in enumerate(priors(k, same)):
                red_scr[lag + 1, pl.ds(c, 1), :] = jnp.sum(ds * prior, axis=0, keepdims=True)
                d = ds * same[lag]
                r = pltpu.roll(d, LANES - (lag + 1), axis=1)
                r2 = pltpu.roll(r, nb - 1, axis=0)
                dk = dk + sw_ref[lag + 1, c] * jnp.where(lane < LANES - (lag + 1), r, r2)
            dk_scr[rows, :] = dk
        return 0

    lax.fori_loop(0, chans // un, last_step, 0)
    yield
    for b in range(nb):
        half = b % 2
        for i, scr in ((1, dk_scr), (2, dv_scr)):
            dqkv_ref[b // 2, i, :, half * LANES : (half + 1) * LANES] = scr[
                pl.ds(b, chans, stride=nb), :
            ].astype(jnp.bfloat16)
    yield
    for j in range(SHIFT):
        dsw_ref[j : j + 1, :] = jnp.sum(red_scr[j].T, axis=0, keepdims=True)[:, 0:chans]


MESH = pl.DeviceIdType.MESH


class Place:
    def __init__(self, n_dp, n_head, n_tensor):
        self.n_dp, self.n_head, self.n_tensor = n_dp, n_head, n_tensor
        self.dp = lax.axis_index("dp")
        h, t = lax.axis_index("head"), lax.axis_index("tensor")
        self.size = n_head * n_tensor
        ph, xh, yt = h + 1 - 2 * (h % 2), (h + 2) % n_head, 1 - t
        pxh = (ph + 2) % n_head
        slot = lambda a, b: a * n_tensor + b
        self.me, self.p, self.x, self.y, self.d = (
            slot(h, t), slot(ph, t), slot(xh, t), slot(h, yt), slot(xh, yt),
        )
        self.px, self.py, self.pd = slot(pxh, t), slot(ph, yt), slot(pxh, yt)
        self.to_p, self.to_x, self.to_y = {"head": ph}, {"head": xh}, {"tensor": yt}

    def dp_peer(self, step):
        return (self.dp + step) % self.n_dp

    def greet_all(self, whole_group, over_dp):
        sem = pltpu.get_barrier_semaphore()

        def greet(where):
            pl.semaphore_signal(sem, inc=1, device_id=where, device_id_type=MESH)

        if whole_group:
            for i in range(1, self.size):
                peer = (self.me + i) % self.size
                greet({"head": peer // self.n_tensor, "tensor": peer % self.n_tensor})
            count = self.size - 1
        else:
            for where in (self.to_p, self.to_x, self.to_y):
                greet(where)
            count = 3
        if over_dp:
            def step(i, _):
                greet({"dp": self.dp_peer(i)})
                return 0

            lax.fori_loop(1, self.n_dp, step, 0)
            count += self.n_dp - 1
        return lambda: pl.semaphore_wait(sem, count)


def remote(src, dst, ssem, rsem, where):
    return pltpu.make_async_remote_copy(
        src_ref=src, dst_ref=dst, send_sem=ssem, recv_sem=rsem, device_id=where, device_id_type=MESH
    )


class GroupGather:
    COPIES = 11

    def __init__(self, place, ref, ssem, rsem):
        self.ssem, self.rsem = ssem, rsem
        half = ref.shape[1] // 2
        top, low = pl.ds(0, half), pl.ds(half, half)
        pc = place
        full = lambda s: ref.at[s]
        part = lambda s, rows: ref.at[s, rows]
        self.out = [
            (full(pc.me), pc.to_p),
            (part(pc.me, top), pc.to_x), (part(pc.me, low), pc.to_x),
            (part(pc.me, low), pc.to_y), (part(pc.me, top), pc.to_y),
            (part(pc.x, top), pc.to_y), (part(pc.y, low), pc.to_x),
            (full(pc.x), pc.to_p), (full(pc.y), pc.to_p),
            (part(pc.d, top), pc.to_p), (part(pc.d, low), pc.to_p),
        ]
        self.into = [
            full(pc.p), part(pc.x, top), part(pc.x, low), part(pc.y, low), part(pc.y, top),
            part(pc.d, top), part(pc.d, low), full(pc.px), full(pc.py), part(pc.pd, top), part(pc.pd, low),
        ]

    def send(self, *which):
        for i in which:
            src, where = self.out[i]
            remote(src, src, self.ssem.at[i], self.rsem.at[i], where).start()

    def arrive(self, *which):
        for i in which:
            dst = self.into[i]
            remote(dst, dst, self.ssem.at[i], self.rsem.at[i], self.out[i][1]).wait_recv()

    def start(self):
        self.send(1, 3, 2, 4, 0)

    def first(self):
        self.arrive(1)
        self.send(5)
        self.arrive(3)
        self.send(6)

    def second(self):
        self.arrive(2)
        self.send(7)
        self.arrive(4)
        self.send(8)

    def third(self):
        self.arrive(5)
        self.send(9)
        self.arrive(6)
        self.send(10)

    def finish(self):
        self.arrive(0, 7, 8, 9, 10)

    def drain(self):
        for i in range(self.COPIES):
            src, where = self.out[i]
            remote(src, src, self.ssem.at[i], self.rsem.at[i], where).wait_send()


class DepthGather:
    def __init__(self, place, ref, ssem, rsem):
        self.place, self.ref, self.ssem, self.rsem = place, ref, ssem, rsem

    def _copy(self, step, slot, peer):
        return remote(
            self.ref.at[slot], self.ref.at[slot], self.ssem.at[step], self.rsem.at[step], {"dp": peer}
        )

    def _loop(self, body):
        def step(i, _):
            body(i)
            return 0

        lax.fori_loop(1, self.place.n_dp, step, 0)

    def start(self):
        pc = self.place
        self._loop(lambda i: self._copy(i, pc.dp, pc.dp_peer(i)).start())

    def finish(self):
        pc = self.place
        source = lambda i: (pc.dp + pc.n_dp - i) % pc.n_dp
        self._loop(lambda i: self._copy(i, source(i), pc.dp_peer(i)).wait_recv())

    def drain(self):
        pc = self.place
        self._loop(lambda i: self._copy(i, pc.dp, pc.dp_peer(i)).wait_send())


class LineGather:
    def __init__(self, place, ref, ssem, rsem):
        self.pc, self.ref, self.ssem, self.rsem = place, ref, ssem, rsem
        self.n, self.at = place.n_dp, place.dp
        self.steps = self.n - 1

    def _copy(self, slot, way):
        return remote(
            self.ref.at[slot], self.ref.at[slot], self.ssem.at[way * self.n + slot], self.rsem.at[slot],
            {"dp": self.at + 1 - 2 * way},
        )

    def _pass(self, slot):
        @pl.when((slot <= self.at) & (self.at < self.n - 1))
        def _():
            self._copy(slot, 0).start()

        @pl.when((slot >= self.at) & (self.at > 0))
        def _():
            self._copy(slot, 1).start()

    def start(self):
        self._pass(self.at)

    def step(self, s):
        below, above = self.at - 1 - s, self.at + 1 + s

        @pl.when(below >= 0)
        def _():
            self._copy(below, 0).wait_recv()

            @pl.when(self.at < self.n - 1)
            def _():
                self._copy(below, 0).start()

        @pl.when(above < self.n)
        def _():
            self._copy(above, 1).wait_recv()

            @pl.when(self.at > 0)
            def _():
                self._copy(above, 1).start()

    def rest(self, first):
        def body(s, _):
            self.step(s)
            return 0

        lax.fori_loop(first, self.steps, body, 0)

    def drain(self):
        def body(slot, _):
            @pl.when((slot <= self.at) & (self.at < self.n - 1))
            def _():
                self._copy(slot, 0).wait_send()

            @pl.when((slot >= self.at) & (self.at > 0))
            def _():
                self._copy(slot, 1).wait_send()

            return 0

        lax.fori_loop(0, self.n, body, 0)


def joined(ref):
    n, rows, columns = ref.shape
    if rows % 16 == 0:
        return ref[...].reshape(n * rows, columns)
    parts = [ref[j].astype(jnp.float32) for j in range(n)]
    return jnp.concatenate(parts, axis=0).astype(ref.dtype)


def row_norm(x):
    centred = x - jnp.mean(x, axis=1, keepdims=True)
    inv = lax.rsqrt(jnp.mean(centred * centred, axis=1, keepdims=True) + 1e-05)
    return centred * inv, inv


class GroupReduce:
    COPIES = 10

    def __init__(self, place, part, land, half_land, last_land, ssem, rsem):
        pc = place
        self.pc = pc
        self.part, self.land, self.half_land, self.last_land = part, land, half_land, last_land
        self.ssem, self.rsem = ssem, rsem
        half = part.shape[1] // 2
        top, low = pl.ds(0, half), pl.ds(half, half)
        self.top, self.low = top, low
        self.mine = [pc.d, pc.x, pc.y, pc.me]
        self.theirs = [pc.pd, pc.px, pc.py, pc.p]
        self.copies = [(part.at[self.theirs[i]], land.at[i], pc.to_p) for i in range(4)] + [
            (part.at[pc.d, top], half_land.at[0], pc.to_x),
            (part.at[pc.d, low], half_land.at[1], pc.to_y),
            (part.at[pc.x, top], last_land.at[0, top], pc.to_x),
            (part.at[pc.y, low], last_land.at[1, low], pc.to_y),
            (part.at[pc.x, low], last_land.at[0, low], pc.to_x),
            (part.at[pc.y, top], last_land.at[1, top], pc.to_y),
        ]

    def _copy(self, i):
        src, dst, where = self.copies[i]
        return remote(src, dst, self.ssem.at[i], self.rsem.at[i], where)

    def give(self, *which):
        for i in which:
            self._copy(i).start()

    def pair(self, i):
        self._copy(i).wait_recv()
        s = self.mine[i]
        self.part[s] = (self.part[s].astype(jnp.float32) + self.land[i].astype(jnp.float32)).astype(
            self.part.dtype
        )

    def side(self):
        self.pair(1)
        self.give(6)
        self.pair(2)
        self.give(7)

    def far(self):
        self.pair(0)
        self.give(4, 5)

    def near(self):
        for i, s, rows in ((4, self.pc.y, self.top), (5, self.pc.x, self.low)):
            self._copy(i).wait_recv()
            self.part[s, rows] = (
                self.part[s, rows].astype(jnp.float32) + self.half_land[i - 4].astype(jnp.float32)
            ).astype(self.part.dtype)
            self.give(9 if i == 4 else 8)

    def total(self):
        for i in (6, 7, 8, 9):
            self._copy(i).wait_recv()
        return (
            self.part[self.pc.me].astype(jnp.float32)
            + self.last_land[0].astype(jnp.float32)
            + self.last_land[1].astype(jnp.float32)
        )

    def drain(self):
        for i in range(self.COPIES):
            self._copy(i).wait_send()

    @staticmethod
    def scratch(group, rows, columns):
        bf16 = jnp.bfloat16
        return [
            pltpu.VMEM((group, rows, columns), bf16),
            pltpu.VMEM((4, rows, columns), bf16),
            pltpu.VMEM((2, rows // 2, columns), bf16),
            pltpu.VMEM((2, rows, columns), bf16),
        ]


class GroupSwap:
    def __init__(self, place, src, dst, lsem, rows, ssem, rsem):
        self.pc, self.src, self.dst, self.ssem, self.rsem, self.lsem = place, src, dst, ssem, rsem, lsem
        self.rows = rows

    def _peer(self, i):
        return (self.pc.me + i) % self.pc.size

    def _copy(self, i, slot):
        peer = self._peer(i)
        where = {"head": peer // self.pc.n_tensor, "tensor": peer % self.pc.n_tensor}
        return remote(
            self.src.at[peer, self.rows], self.dst.at[slot, self.rows], self.ssem.at[i], self.rsem.at[i], where
        )

    def _own(self):
        me = self.pc.me
        return pltpu.make_async_copy(self.src.at[me, self.rows], self.dst.at[me, self.rows], self.lsem)

    def start(self):
        for i in range(1, self.pc.size):
            self._copy(i, self.pc.me).start()
        self._own().start()

    def finish(self):
        for i in range(1, self.pc.size):
            self._copy(i, (self.pc.me + self.pc.size - i) % self.pc.size).wait_recv()
        self._own().wait()

    def drain(self):
        for i in range(1, self.pc.size):
            self._copy(i, self.pc.me).wait_send()


class DepthReduce:
    def __init__(self, place, src, land, ssem, rsem):
        self.place, self.src, self.land, self.ssem, self.rsem = place, src, land, ssem, rsem

    def _copy(self, step, mine, slot, peer):
        return remote(
            self.src.at[mine], self.land.at[slot], self.ssem.at[step], self.rsem.at[step], {"dp": peer}
        )

    def _loop(self, body, start):
        return lax.fori_loop(1, self.place.n_dp, body, start)

    def start(self):
        pc = self.place

        def step(i, _):
            self._copy(i, pc.dp_peer(i), pc.dp, pc.dp_peer(i)).start()
            return 0

        self._loop(step, 0)

    def total(self):
        pc = self.place

        def step(i, acc):
            source = (pc.dp + pc.n_dp - i) % pc.n_dp
            self._copy(i, source, source, pc.dp_peer(i)).wait_recv()
            return acc + self.land[source].astype(jnp.float32)

        return self._loop(step, self.src[pc.dp].astype(jnp.float32))

    def drain(self):
        pc = self.place

        def step(i, _):
            self._copy(i, pc.dp_peer(i), pc.dp, pc.dp_peer(i)).wait_send()
            return 0

        self._loop(step, 0)


def split_rows(ref, value):
    n, rows, columns = ref.shape
    if rows % 16 == 0:
        ref[...] = value.astype(ref.dtype).reshape(n, rows, columns)
    else:
        for j in range(n):
            ref[j] = value[j * rows : (j + 1) * rows].astype(ref.dtype)


def row_norm_back(grad, gain, hat, inv):
    scaled = grad * gain
    return inv * (
        scaled
        - jnp.mean(scaled, axis=1, keepdims=True)
        - hat * jnp.mean(scaled * hat, axis=1, keepdims=True)
    )


def gelu_pair(pre):
    cdf = 0.5 * (1.0 + lax.erf(pre * 0.7071067811865476))
    return pre * cdf, cdf + pre * (0.3989422804014327 * jnp.exp(-0.5 * pre * pre))


class GroupSpread:
    def __init__(self, place, ref, ssem, rsem):
        self.pc, self.ref, self.ssem, self.rsem = place, ref, ssem, rsem

    def _copy(self, i, slot):
        peer = (self.pc.me + i) % self.pc.size
        where = {"head": peer // self.pc.n_tensor, "tensor": peer % self.pc.n_tensor}
        return remote(self.ref.at[slot], self.ref.at[slot], self.ssem.at[i], self.rsem.at[i], where)

    def start(self):
        for i in range(1, self.pc.size):
            self._copy(i, self.pc.me).start()

    def finish(self):
        for i in range(1, self.pc.size):
            self._copy(i, (self.pc.me + self.pc.size - i) % self.pc.size).wait_recv()

    def drain(self):
        for i in range(1, self.pc.size):
            self._copy(i, self.pc.me).wait_send()


SKIP_AT, PARAM_ROWS = 192, 208
UNROLL = 16


class Names:
    def __init__(self, names, refs):
        assert len(names) == len(refs)
        for name, ref in zip(names, refs):
            setattr(self, name, ref)


def layout(axes, own, feats, rows, chans, units, ns):
    n_dp, n_head, n_tensor = axes
    group = n_head * n_tensor
    f32, bf16 = jnp.float32, jnp.bfloat16
    v = pltpu.VMEM
    dma = lambda *shape: pltpu.SemaphoreType.DMA(shape)
    blocks = group * own // LANES
    conv = chans * blocks
    sq = v((LANES, LANES), f32)
    full = v((conv, LANES), f32)
    out = dict(
        tok=v((own, feats), bf16), cot=v((own, feats), bf16), four=v((4, rows, chans), bf16),
        wqkvo=v((n_dp, rows, 4 * chans), bf16), wup=v((n_dp, rows, units), bf16), wdown=v((n_dp, rows, units), bf16),
        wt=v((4 * chans, feats), bf16), wupt=v((units, feats), bf16), wdownt=v((units, feats), bf16),
        wout=v((group, chans, feats), bf16),
        xn1=v((group, feats, own), bf16), cots=v((group, feats, own), bf16), xn2=v((group, feats, own), bf16),
        act=v((group, units, own), bf16), gpre=v((group, units, own), bf16),
        qkv=v((3, conv, LANES), f32), core=full, s=full, f=full, urev=v((conv, LANES), bf16),
        pp=v((chans * LANES, LANES), bf16), kern=v((chans, LANES), f32),
        mixed=v((group, chans, own), bf16), mixed_in=v((group, chans, own), bf16),
        gmix=v((group, chans, own), bf16), gmix_in=v((group, chans, own), bf16),
        dqkv=v((group, 3, chans, own), bf16),
        t0=sq, t1=sq, t2=sq, t3=sq, t4=sq, t5=sq, gr=sq, red=v((SHIFT + 1, LANES, LANES), f32),
        w0=full, w1=full, w2=full, w3=full, w4=full, w5=full, w6=full, dur=v((conv, LANES), bf16),
        dsw=v((SHIFT, chans), f32), drate=v((ns, chans), f32), dinb=v((ns, chans), f32), doutc=v((ns, chans), f32),
        dskip=v((1, chans), f32),
        hat=v((own, feats), f32), hid=v((own, feats), f32), ghid=v((own, feats), f32),
        up_part=v((n_dp, rows, units), bf16), up_land=v((n_dp, rows, units), bf16),
        dn_part=v((n_dp, rows, units), bf16), dn_land=v((n_dp, rows, units), bf16),
        q_part=v((n_dp, rows, chans), bf16), q_land=v((n_dp, rows, chans), bf16),
        o_out=v((n_dp, rows, chans), bf16), o_in=v((n_dp, rows, chans), bf16),
        kv_part=v((n_dp, rows, 2 * chans), bf16), kv_land=v((n_dp, rows, 2 * chans), bf16),
        taps_all=v((n_dp, 8, LANES), f32),
        params=v((n_dp, PARAM_ROWS, LANES), bf16),
        n1=v((group, 2, feats), f32), n2=v((group, 2, feats), f32), m1=v((n_dp, 2, feats), f32), m2=v((n_dp, 2, feats), f32),
    )
    for name, height, width in (("x", feats, own), ("m", feats, own), ("o", chans, feats)):
        for part, alloc in zip(("part", "land", "half", "last"), GroupReduce.scratch(group, height, width)):
            out[f"{name}_{part}"] = alloc
    for name, count in (
        ("xn1", 11), ("cots", 11), ("wout", 11), ("xn2", 11), ("x2", 10), ("m", 10), ("o", 10), ("x1", 10),
        ("in0", group), ("in1", group), ("back0", group), ("back1", group), ("sp1", group), ("sp2", group),
        ("zq", n_dp), ("zu", n_dp), ("zd", n_dp), ("gu", n_dp), ("gd", n_dp), ("gq", n_dp), ("go", n_dp), ("gkv", n_dp), ("zt", n_dp), ("zp", n_dp),
        ("zn1", n_dp), ("zn2", n_dp),
    ):
        out[f"send_{name}"] = dma(count)
        out[f"recv_{name}"] = dma(count)
    out["local"] = dma(12)
    return out


INPUTS = (
    "tok_hbm", "cot_hbm", "q_hbm", "k_hbm", "v_hbm", "o_hbm", "up_hbm", "down_hbm",
    "seg", "gain1", "bias1", "gain2", "bias2", "taps", "rate", "inb", "outc", "skip",
)
OUTPUTS = (
    "res", "gx", "g1", "b1", "g2", "b2", "dq", "dk", "dv", "do", "dup", "ddown",
    "out_taps", "out_rate", "out_inb", "out_outc", "out_skip",
)


def run_beside(body, tasks):
    tasks = list(tasks)
    for _ in body:
        if tasks:
            tasks.pop(0)()
    for task in tasks:
        task()


def block_kernel(axes, names, *refs):
    r = Names(names, refs)
    pc = Place(*axes)
    f32, bf16 = jnp.float32, jnp.bfloat16
    group, chans, feats = r.wout.shape
    own = r.tok.shape[0]
    blocks = own // LANES
    work = []

    def sems(name):
        return getattr(r, f"send_{name}"), getattr(r, f"recv_{name}")

    def make(kind, name, *args):
        made = kind(pc, *args, *sems(name))
        work.append(made)
        return made

    def local(i, src, dst):
        copy = pltpu.make_async_copy(src, dst, r.local.at[i])
        copy.start()
        return copy

    four = [local(i, src, r.four.at[i]) for i, src in enumerate((r.q_hbm, r.k_hbm, r.v_hbm, r.o_hbm))]
    load_tok = local(4, r.tok_hbm, r.tok)
    load_cot = local(5, r.cot_hbm, r.cot)
    load_up = local(6, r.up_hbm, r.wup.at[pc.dp])
    load_down = local(7, r.down_hbm, r.wdown.at[pc.dp])
    meet = pc.greet_all(True, True)
    z_qkvo = make(DepthGather, "zq", r.wqkvo)
    z_up = make(DepthGather, "zu", r.wup)
    z_down = make(DepthGather, "zd", r.wdown)
    xn1_g = make(GroupGather, "xn1", r.xn1)
    cot_g = make(GroupGather, "cots", r.cots)
    out_g = make(GroupGather, "wout", r.wout)
    xn2_g = make(GroupGather, "xn2", r.xn2)
    halves = [pl.ds(i * (chans // PARTS), chans // PARTS) for i in range(PARTS)]
    swap_in = [make(GroupSwap, f"in{i}", r.mixed, r.mixed_in, r.local.at[8 + i], rows) for i, rows in enumerate(halves)]
    swap_back = [make(GroupSwap, f"back{i}", r.gmix, r.gmix_in, r.local.at[10 + i], rows) for i, rows in enumerate(halves)]
    gain1, gain2 = r.gain1[...].reshape(1, feats), r.gain2[...].reshape(1, feats)
    bias1, bias2 = r.bias1[...].reshape(1, feats), r.bias2[...].reshape(1, feats)
    load_tok.wait()
    hat1, _ = row_norm(r.tok[...].astype(f32))
    r.xn1[pc.me] = (hat1 * gain1 + bias1).astype(bf16).T
    for copy in four:
        copy.wait()
    r.wqkvo[pc.dp] = jnp.concatenate([r.four[i] for i in range(4)], axis=1)
    meet()
    xn1_g.start()
    z_qkvo.start()
    load_cot.wait()
    r.cots[pc.me] = r.cot[...].T
    xn1_g.first()
    xn1_g.second()
    z_qkvo.finish()
    load_up.wait()
    z_up.start()
    r.wt[...] = joined(r.wqkvo).T
    r.wout[pc.me] = r.wt[3 * chans :, :]
    out_g.start()
    load_down.wait()

    def project(s):
        y = mm(r.wt[0 : 3 * chans, :], r.xn1[s])
        for i in range(3):
            for h in range(blocks):
                r.qkv[i, pl.ds(s * blocks + h, chans, stride=group * blocks), :] = y[
                    i * chans : (i + 1) * chans, h * LANES : (h + 1) * LANES
                ]

    xn1_g.third()
    xn1_g.finish()
    for s in range(group):
        project(s)

    def after_drive():
        out_g.first()
        out_g.second()
        cot_g.start()

    def after_scan():
        out_g.third()

    def half_out():
        swap_in[0].start()
        z_up.finish()
        z_down.start()

    mixer = (r.seg, r.taps, r.skip, r.rate, r.inb, r.outc)
    run_beside(
        mixer_forward(
            UNROLL, r.qkv, *mixer, r.mixed, r.core, r.s, r.f, r.urev, r.pp, r.kern,
            r.t0, r.t1, r.t2, r.t3, r.t4, r.w0, r.t5,
        ),
        (after_drive, lambda: None, lambda: None, after_scan, half_out, swap_in[1].start),
    )
    cot_g.first()
    out_g.finish()
    cot_g.second()
    w_up = joined(r.wup)
    r.wupt[...] = w_up.T
    wout_t = r.wout[...].reshape(feats, feats)
    swap_in[0].finish()
    swap_in[1].finish()
    mixed_t = r.mixed_in[...].reshape(feats, own)
    hidden = r.tok[...].astype(f32) + mm(mixed_t, wout_t, TN)
    hat2, inv2 = row_norm(hidden)
    r.xn2[pc.me] = (hat2 * gain2 + bias2).astype(bf16).T
    xn2_g.start()
    r.hid[...] = hidden
    r.hat[...] = hat2
    cot_g.third()
    z_down.finish()
    w_down = joined(r.wdown)
    r.wdownt[...] = w_down.T
    cot_g.finish()
    red_x2 = make(GroupReduce, "x2", r.x_part, r.x_land, r.x_half, r.x_last)
    red_m = make(GroupReduce, "m", r.m_part, r.m_land, r.m_half, r.m_last)
    red_o = make(GroupReduce, "o", r.o_part, r.o_land, r.o_half, r.o_last)

    def chunk(s):
        act, slope = gelu_pair(mm(r.wupt[...], r.xn2[s]))
        r.act[s] = act.astype(bf16)
        grad_pre = (mm(r.wdownt[...], r.cots[s]) * slope).astype(bf16)
        r.gpre[s] = grad_pre
        r.x_part[s] = mm(w_up, grad_pre).astype(bf16)

    chunk(pc.me)
    xn2_g.arrive(0)
    chunk(pc.p)
    red_x2.give(3)
    xn2_g.first()
    xn2_g.second()
    chunk(pc.x)
    chunk(pc.y)
    xn2_g.arrive(7)
    chunk(pc.px)
    red_x2.give(1)
    xn2_g.arrive(8)
    chunk(pc.py)
    red_x2.give(2)
    xn2_g.third()
    red_x2.side()
    chunk(pc.d)
    xn2_g.arrive(9, 10)
    chunk(pc.pd)
    red_x2.give(0)
    red_x2.pair(3)
    red_x2.far()
    units = r.act.shape[1]
    grad_up = jnp.zeros((feats, units), f32)
    for s in range(group):
        grad_up = grad_up + mm(r.xn2[s], r.gpre[s], NT)
    split_rows(r.up_part, grad_up)
    sum_up = make(DepthReduce, "gu", r.up_part, r.up_land)
    sum_up.start()
    red_x2.near()
    for i, s in enumerate(red_m.theirs):
        r.m_part[s] = mm(w_down, r.act[s]).astype(bf16)
        red_m.give(i)
    for s in red_m.mine:
        r.m_part[s] = mm(w_down, r.act[s]).astype(bf16)
    grad_down = jnp.zeros((feats, units), f32)
    for s in range(group):
        grad_down = grad_down + mm(r.cots[s], r.act[s], NT)
    split_rows(r.dn_part, grad_down)
    sum_down = make(DepthReduce, "gd", r.dn_part, r.dn_land)
    sum_down.start()
    grad_xn = red_x2.total().T
    hat2 = r.hat[...]
    grad_hidden = r.cot[...].astype(f32) + row_norm_back(grad_xn, gain2, hat2, inv2)
    r.ghid[...] = grad_hidden
    grad_mix = grad_hidden.astype(bf16)
    r.gmix[...] = mm(wout_t, grad_mix, NT).astype(bf16).reshape(group, chans, own)
    swap_back[0].start()
    swap_back[1].start()
    r.n2[pc.me, 0:1, :] = jnp.sum(grad_xn * hat2, axis=0, keepdims=True)
    r.n2[pc.me, 1:2, :] = jnp.sum(grad_xn, axis=0, keepdims=True)
    spread2 = make(GroupSpread, "sp2", r.n2)
    spread2.start()
    r.o_part[...] = mm(mixed_t, grad_mix).astype(bf16).reshape(group, chans, feats)
    red_o.give(0, 1, 2, 3)
    swap_back[0].finish()
    norm2 = make(DepthGather, "zn2", r.m2)

    ns = r.drate.shape[0]
    pieces = ((0, r.drate, r.out_rate), (ns, r.dinb, r.out_inb), (2 * ns, r.doutc, r.out_outc),
              (SKIP_AT, r.dskip, r.out_skip))
    z_par = make(DepthGather, "zp", r.params)
    sum_q = make(DepthReduce, "gq", r.q_part, r.q_land)
    sum_o = make(DepthReduce, "go", r.o_out, r.o_in)
    sum_kv = make(DepthReduce, "gkv", r.kv_part, r.kv_land)

    def second_half():
        swap_back[1].finish()
        red_o.far()
        red_o.side()
        red_m.far()

    def early_sums():
        red_o.near()
        r.params[pc.dp] = jnp.zeros(r.params.shape[1:], bf16)
        for at, ref, _ in pieces:
            r.params[pc.dp, at : at + ref.shape[0], 0:chans] = ref[...].astype(bf16)
        z_par.start()
        grad_q = jnp.zeros((feats, chans), f32)
        for s in range(group):
            grad_q = grad_q + mm(r.xn1[s], r.dqkv[s, 0], NT)
        split_rows(r.q_part, grad_q)
        sum_q.start()

    def mlp_sums():
        red_m.side()
        red_m.near()
        red_x2.drain()
        work.remove(red_x2)

    def out_sums():
        red_o.pair(3)
        split_rows(r.o_out, red_o.total().T)
        sum_o.start()

    w_joint = joined(r.wqkvo)
    red_x1 = make(GroupReduce, "x1", r.x_part, r.x_land, r.x_half, r.x_last)

    def grads(s):
        return r.dqkv[s].reshape(3 * chans, own)

    def chunk_back(s):
        padded = jnp.concatenate([grads(s), jnp.zeros((chans, own), bf16)], axis=0)
        r.x_part[s] = mm(w_joint, padded).astype(bf16)

    def start_back():
        theirs, mine = red_x1.theirs, red_x1.mine
        chunk_back(theirs[0])
        red_x1.give(0)
        chunk_back(mine[0])
        chunk_back(theirs[1])
        red_x1.give(1)
        chunk_back(mine[1])
        grad_kv = jnp.zeros((feats, 2 * chans), f32)
        for s in range(group):
            grad_kv = grad_kv + mm(r.xn1[s], grads(s)[chans:], NT)
        split_rows(r.kv_part, grad_kv)
        sum_kv.start()
        red_x1.far()
        chunk_back(theirs[2])
        red_x1.give(2)
        chunk_back(mine[2])
        chunk_back(theirs[3])
        red_x1.give(3)
        red_x1.side()
        chunk_back(mine[3])

    run_beside(
        mixer_backward(
            UNROLL, r.gmix_in, r.qkv, r.core, r.s, r.f, r.urev, r.pp, r.kern, *mixer,
            r.dqkv, r.dsw, r.drate, r.dinb, r.doutc, r.dskip,
            r.t0, r.t1, r.t2, r.t3, r.w0, r.w1, r.w2, r.w3, r.dur, r.w2, r.w4, r.w5, r.w6, r.gr, r.red,
        ),
        (second_half, lambda: None, early_sums, mlp_sums, out_sums, start_back),
    )
    r.taps_all[pc.dp] = jnp.zeros(r.taps_all.shape[1:], f32)
    r.taps_all[pc.dp, 0:SHIFT, 0:chans] = r.dsw[...]
    z_taps = make(DepthGather, "zt", r.taps_all)
    z_taps.start()
    spread2.finish()
    r.m2[pc.dp] = jnp.sum(r.n2[...], axis=0)
    norm2.start()
    red_x1.near()
    red_x1.pair(3)
    red_m.pair(3)
    r.res[...] = (r.hid[...] + red_m.total().T).astype(bf16)
    r.dup[...] = sum_up.total()
    r.ddown[...] = sum_down.total()
    hat1, inv1 = row_norm(r.tok[...].astype(f32))
    grad_xn = red_x1.total().T
    r.n1[pc.me, 0:1, :] = jnp.sum(grad_xn * hat1, axis=0, keepdims=True)
    r.n1[pc.me, 1:2, :] = jnp.sum(grad_xn, axis=0, keepdims=True)
    spread1 = make(GroupSpread, "sp1", r.n1)
    spread1.start()
    r.gx[...] = r.ghid[...] + row_norm_back(grad_xn, gain1, hat1, inv1)
    spread1.finish()
    r.m1[pc.dp] = jnp.sum(r.n1[...], axis=0)
    norm1 = make(DepthGather, "zn1", r.m1)
    norm1.start()
    z_par.finish()
    sums = jnp.sum(r.params[...].astype(f32), axis=0)
    for at, ref, out in pieces:
        out[...] = sums[at : at + ref.shape[0], 0:chans]
    z_taps.finish()
    r.out_taps[...] = jnp.sum(r.taps_all[...], axis=0)[0:SHIFT, 0:chans]
    norm2.finish()
    sums = jnp.sum(r.m2[...], axis=0)
    r.g2[...] = sums[0:1]
    r.b2[...] = sums[1:2]
    norm1.finish()
    sums = jnp.sum(r.m1[...], axis=0)
    r.g1[...] = sums[0:1]
    r.b1[...] = sums[1:2]
    r.do[...] = sum_o.total()
    r.dq[...] = sum_q.total()
    kv_sum = sum_kv.total()
    r.dk[...] = kv_sum[:, 0:chans]
    r.dv[...] = kv_sum[:, chans:]
    for one in work:
        one.drain()


def hand_over(*refs):
    n = len(refs) // 2
    for src, dst in zip(refs[:n], refs[n:]):
        dst[...] = src[...].reshape(dst.shape)


def whole_block(axes, args):
    (tokens, seg, gain1, bias1, gain2, bias2, q, k, v, o, up, down, taps, rate, inb, outc, skip, cot) = args
    own, feats = tokens.shape
    rows, chans = q.shape
    units = up.shape[1]
    f32, bf16 = jnp.float32, jnp.bfloat16
    sds = jax.ShapeDtypeStruct
    vm = pl.BlockSpec(memory_space=pltpu.VMEM)
    sm = pl.BlockSpec(memory_space=pltpu.SMEM)
    hbm = pl.BlockSpec(memory_space=pl.ANY)
    scratch = layout(axes, own, feats, rows, chans, units, rate.shape[0])
    wide, thin = sds((rows, units), f32), sds((rows, chans), f32)
    row = sds((1, feats), f32)
    outs = pl.pallas_call(
        functools.partial(block_kernel, axes, INPUTS + OUTPUTS + tuple(scratch)),
        out_shape=(
            sds((own, feats), bf16), sds((own, feats), f32), row, row, row, row, thin, thin, thin, thin, wide, wide,
            *(sds(a.shape, f32) for a in (taps, rate, inb, outc)), sds((1, chans), f32),
        ),
        in_specs=[hbm] * 8 + [vm] * 5 + [sm] + [vm] * 3 + [sm],
        out_specs=(vm,) * 17,
        scratch_shapes=list(scratch.values()),
        compiler_params=pltpu.CompilerParams(
            collective_id=1, has_side_effects=True, vmem_limit_bytes=63 << 20
        ),
        name="block",
    )(tokens, cot, q, k, v, o, up, down, seg, gain1, bias1, gain2, bias2, taps, rate, inb, outc, skip[None])
    final = [sds(a.shape, a.dtype) for a in outs]
    for i in (2, 3, 4, 5):
        final[i] = sds((feats,), f32)
    final[16] = sds((chans,), f32)
    return pl.pallas_call(
        hand_over,
        out_shape=tuple(final),
        in_specs=[vm] * 17,
        out_specs=(vm,) * 17,
        name="hand_over",
    )(*outs)


from jax.sharding import PartitionSpec as P

GROUP = ("head", "tensor")


def on_device(*args):
    return whole_block((lax.axis_size("dp"), lax.axis_size("head"), lax.axis_size("tensor")), args)


def solution(mesh):
    rows = P(("dp", "head", "tensor"), None)
    weight = P("dp", GROUP)
    chan = P(None, GROUP)
    in_specs = (rows, P("dp", None)) + (P(),) * 4 + (weight,) * 6 + (chan,) * 4 + (P(GROUP), rows)
    out_specs = (rows, rows) + (P(),) * 4 + (weight,) * 6 + (chan,) * 4 + (P(GROUP),)
    return jax.shard_map(on_device, mesh=mesh, in_specs=in_specs, out_specs=out_specs, check_vma=False)
```

```python
import functools
import jax, jax.numpy as jnp
from jax import lax
from jax.experimental import pallas as pl
from jax.experimental.pallas import tpu as pltpu

LANES = 128
SHIFT = 4
SEQS = 3
PARTS = 2
NT = (((1,), (1,)), ((), ()))
TN = (((0,), (0,)), ((), ()))
NN = (((1,), (0,)), ((), ()))


def mm(left, right, dims=NN):
    return lax.dot_general(left, right, dims, preferred_element_type=jnp.float32)


def iota(shape, axis):
    return lax.broadcasted_iota(jnp.int32, shape, axis)


def seg_masks(seg, nb):
    lane = iota((nb, LANES), 1)
    row = iota((nb, LANES), 0)
    masks = [(seg == k).astype(jnp.float32) for k in range(SEQS)]
    end = jnp.broadcast_to(seg[:, LANES - 1 :], (nb, LANES))
    last = jnp.where(row == 0, -1, pltpu.roll(end, 1, axis=0))
    live = (seg == last).astype(jnp.float32)
    keep = (seg == end).astype(jnp.float32)
    carry = (end == last).astype(jnp.float32)
    same = []
    for j in range(1, SHIFT):
        r = pltpu.roll(seg, j, axis=1)
        r2 = pltpu.roll(r, 1, axis=0)
        prior = jnp.where(lane < j, r2, r)
        ok = (prior == seg) & ((row > 0) | (lane >= j))
        same.append(ok.astype(jnp.float32))
    return masks, live, keep, carry, same


def priors(k, same):
    lane = iota(k.shape, 1)
    out = []
    for j in range(1, SHIFT):
        r = pltpu.roll(k, j, axis=1)
        r2 = pltpu.roll(r, 1, axis=0)
        out.append(jnp.where(lane < j, r2, r) * same[j - 1])
    return out


def flip_matrix():
    return (iota((LANES, LANES), 0) + iota((LANES, LANES), 1) == LANES - 1).astype(jnp.bfloat16)


def read_seg(seg_ref, nb):
    return jnp.concatenate([seg_ref[:, b * LANES : (b + 1) * LANES] for b in range(nb)], axis=0)


def transposed(scr, top, bottom):
    ns, chans = top.shape
    scr[...] = jnp.zeros_like(scr)
    scr[0:ns, 0:chans] = top
    if bottom is not None:
        scr[ns : 2 * ns, 0:chans] = bottom
    return scr[...].T


def stack_masked(x, masks):
    return jnp.concatenate([x * m for m in masks], axis=0).astype(jnp.bfloat16)


def merge_masked(y, masks):
    nb = masks[0].shape[0]
    return sum(y[i * nb : (i + 1) * nb] * m for i, m in enumerate(masks))


def toeplitz(krow):
    t = pltpu.roll(jnp.broadcast_to(krow, (LANES, LANES)), 0, axis=1, stride=1, stride_axis=0)
    return jnp.where(iota((LANES, LANES), 1) >= iota((LANES, LANES), 0), t, 0.0).astype(jnp.bfloat16)


def mixer_forward(
    un, qkv_ref, seg_ref, sw_ref, skip_ref, rate_ref, inb_ref, outc_ref,
    mixed_ref, core_ref, s_ref, f_ref, urev_ref, pp_ref, kern_ref,
    tscr, a_scr, b_scr, c_scr, e_scr, u_scr, kscr,
):
    ns, chans = rate_ref.shape
    nb = qkv_ref.shape[1] // chans
    masks, live, keep, carry, same = seg_masks(read_seg(seg_ref, nb), nb)
    flip = flip_matrix()
    keep_rev = mm(keep.astype(jnp.bfloat16), flip)
    rate, in_b, out_c = rate_ref[...], inb_ref[...], outc_ref[...]
    decay = jnp.exp(-rate)
    a_scr[...] = transposed(tscr, rate, rate)
    b_scr[...] = transposed(tscr, in_b * decay, None)
    c_scr[...] = transposed(tscr, out_c, None)
    e_scr[...] = transposed(tscr, jnp.exp(-rate * LANES), None)

    def kern_step(i, e):
        for j in range(8):
            kscr[pl.ds(i * 8 + j, 1), 0:chans] = jnp.sum(e, axis=0, keepdims=True)
            e = e * decay
        return e

    kscr[...] = jnp.zeros_like(kscr)
    lax.fori_loop(0, LANES // 8, kern_step, in_b * out_c)
    kern_ref[...] = kscr[...].T[0:chans]

    def drive_step(i, _):
        for j in range(un):
            c = i * un + j
            rows = pl.ds(pl.multiple_of(c * nb, nb), nb)
            k = qkv_ref[1, rows]
            shifted = sw_ref[0, c] * k
            for lag, prior in enumerate(priors(k, same)):
                shifted = shifted + sw_ref[lag + 1, c] * prior
            u_scr[rows, :] = shifted * qkv_ref[2, rows]
        return 0

    lax.fori_loop(0, chans // un, drive_step, 0)
    yield
    step_rows = 16 * nb

    def rev_step(i, _):
        rows = pl.ds(pl.multiple_of(i * step_rows, step_rows), step_rows)
        urev_ref[rows, :] = mm(u_scr[rows, :].astype(jnp.bfloat16), flip).astype(jnp.bfloat16)
        return 0

    lax.fori_loop(0, chans // 16, rev_step, 0)
    pos = iota((LANES, LANES), 0).astype(jnp.float32)
    factor = jnp.where(iota((LANES, LANES), 1) < ns, 1.0, pos)
    i8 = iota((8, LANES), 0).astype(jnp.float32)
    i16 = iota((LANES // 8, LANES), 0).astype(jnp.float32) * 8.0

    def fresh_step(i, _):
        for j in range(un):
            c = i * un + j
            rows = pl.ds(pl.multiple_of(c * nb, nb), nb)
            a = a_scr[pl.ds(c, 1), :]
            base = jnp.exp(-a * i8)
            tall = jnp.exp(-a * i16)
            p = (tall[:, None, :] * base[None]).reshape(LANES, LANES)
            pp = (p * factor).astype(jnp.bfloat16)
            pp_ref[pl.ds(pl.multiple_of(c * LANES, LANES), LANES), :] = pp
            urk = (urev_ref[rows, :].astype(jnp.float32) * keep_rev).astype(jnp.bfloat16)
            f_ref[rows, :] = mm(urk, pp)
        return 0

    for part in range(PARTS):
        lax.fori_loop(part * chans // PARTS // un, (part + 1) * chans // PARTS // un, fresh_step, 0)
        yield
    across = e_scr[0:chans, :]
    b_ext = b_scr[0:chans, :]
    state = jnp.zeros((chans, LANES), jnp.float32)
    for b in range(nb):
        s_ref[pl.ds(b, chans, stride=nb), :] = state + pltpu.roll(state, ns, axis=1)
        fresh = f_ref[pl.ds(b, chans, stride=nb), :]
        state = across * carry[b : b + 1, :] * state + b_ext * fresh

    yield

    def out_step(i, _):
        for j in range(un):
            c = i * un + j
            rows = pl.ds(pl.multiple_of(c * nb, nb), nb)
            t = toeplitz(kern_ref[pl.ds(c, 1), :])
            u = u_scr[rows, :]
            y = merge_masked(mm(stack_masked(u, masks), t), masks)
            sc = (s_ref[rows, :] * c_scr[pl.ds(c, 1), :]).astype(jnp.bfloat16)
            pp = pp_ref[pl.ds(pl.multiple_of(c * LANES, LANES), LANES), :]
            core = y + live * mm(sc, pp, NT) + skip_ref[0, c] * u
            core_ref[rows, :] = core
            u_scr[rows, :] = qkv_ref[0, rows] * core
        return 0

    count = chans // PARTS
    for part in range(PARTS):
        lax.fori_loop(part * count // un, (part + 1) * count // un, out_step, 0)
        for b in range(nb):
            half = b % 2
            mixed_ref[b // 2, part * count : (part + 1) * count, half * LANES : (half + 1) * LANES] = u_scr[
                pl.ds(part * count * nb + b, count, stride=nb), :
            ].astype(jnp.bfloat16)
        yield


def mixer_backward(
    un, gm_ref, qkv_ref, core_ref, s_ref, f_ref, urev_ref, pp_ref, kern_ref, seg_ref,
    sw_ref, skip_ref, rate_ref, inb_ref, outc_ref,
    dqkv_ref, dsw_ref, drate_ref, dinb_ref, doutc_ref, dskip_ref,
    tscr, b_scr, c_scr, e_scr, g_scr, sh_scr, h_scr, x_scr, dur_scr, dui_scr, dq_scr, dk_scr, dv_scr, gr_scr, red_scr,
):
    ns, chans = rate_ref.shape
    nb = qkv_ref.shape[1] // chans
    masks, live, keep, carry, same = seg_masks(read_seg(seg_ref, nb), nb)
    flip = flip_matrix()
    keep_rev = mm(keep.astype(jnp.bfloat16), flip)
    masks_rev = [mm(m.astype(jnp.bfloat16), flip) for m in masks]
    rate, in_b, out_c = rate_ref[...], inb_ref[...], outc_ref[...]
    decay = jnp.exp(-rate)
    b_scr[...] = transposed(tscr, in_b * decay, None)
    c_scr[...] = transposed(tscr, out_c, None)
    e_scr[...] = transposed(tscr, jnp.exp(-rate * LANES), None)
    red_scr[...] = jnp.zeros_like(red_scr)
    gr_scr[...] = jnp.zeros_like(gr_scr)

    corner = iota((LANES, LANES), 0) + iota((LANES, LANES), 1) >= LANES - 1

    def grad_step(i, _):
        for j in range(un):
            c = i * un + j
            rows = pl.ds(pl.multiple_of(c * nb, nb), nb)
            gm = x_scr[rows, :]
            dq_scr[rows, :] = gm * core_ref[rows, :]
            g = gm * qkv_ref[0, rows]
            g_scr[rows, :] = g
            k = qkv_ref[1, rows]
            shifted = sw_ref[0, c] * k
            for lag, prior in enumerate(priors(k, same)):
                shifted = shifted + sw_ref[lag + 1, c] * prior
            sh_scr[rows, :] = shifted
            red_scr[SHIFT, pl.ds(c, 1), :] = jnp.sum(
                g * shifted * qkv_ref[2, rows], axis=0, keepdims=True
            )
            ur = stack_masked(urev_ref[rows, :].astype(jnp.float32), masks_rev)
            cross = mm(ur, stack_masked(g, masks), TN)
            skew = pltpu.roll(jnp.where(corner, cross, 0.0), 1, axis=1, stride=1, stride_axis=0)
            gr_scr[pl.ds(c, 1), :] = jnp.sum(skew, axis=0, keepdims=True)
            pp = pp_ref[pl.ds(pl.multiple_of(c * LANES, LANES), LANES), :]
            h_scr[rows, :] = mm((g * live).astype(jnp.bfloat16), pp)
        return 0

    count = chans // PARTS
    for part in range(PARTS):
        for b in range(nb):
            half = b % 2
            x_scr[pl.ds(part * count * nb + b, count, stride=nb), :] = gm_ref[
                b // 2, part * count : (part + 1) * count, half * LANES : (half + 1) * LANES
            ].astype(jnp.float32)
        lax.fori_loop(part * count // un, (part + 1) * count // un, grad_step, 0)
        yield
    for b in range(nb):
        half = b % 2
        dqkv_ref[b // 2, 0, :, half * LANES : (half + 1) * LANES] = dq_scr[
            pl.ds(b, chans, stride=nb), :
        ].astype(jnp.bfloat16)
    across = e_scr[0:chans, :]
    b_ext = b_scr[0:chans, :]
    c_ext = c_scr[0:chans, :]
    zero = jnp.zeros((chans, LANES), jnp.float32)
    adj, acc_out, acc_in, acc_carry = zero, zero, zero, zero
    for b in range(nb - 1, -1, -1):
        here = pl.ds(b, chans, stride=nb)
        h = h_scr[here, :]
        s = s_ref[here, :]
        acc_out = acc_out + s * h
        acc_in = acc_in + (adj + pltpu.roll(adj, ns, axis=1)) * f_ref[here, :]
        acc_carry = acc_carry + carry[b : b + 1, :] * adj * s
        x_scr[here, :] = b_ext * adj
        adj = c_ext * h + across * carry[b : b + 1, :] * adj

    dskip_ref[...] = jnp.sum(red_scr[SHIFT].T, axis=0, keepdims=True)[:, 0:chans]
    tscr[...] = gr_scr[...].T

    def kern_back(i, carried):
        e, zeroth, first = carried
        block = tscr[pl.ds(pl.multiple_of(i * 8, 8), 8), 0:chans]
        for j in range(8):
            term = e * block[j : j + 1, :]
            zeroth = zeroth + term
            first = first + term * (i * 8 + j).astype(jnp.float32)
            e = e * decay
        return e, zeroth, first

    blank = jnp.zeros((ns, chans), jnp.float32)
    _, zeroth, first = lax.fori_loop(0, LANES // 8, kern_back, (blank + 1.0, blank, blank))

    def back(x):
        tscr[...] = jnp.zeros_like(tscr)
        tscr[0:chans, :] = x
        y = tscr[...].T
        return y[0:ns, 0:chans], y[ns : 2 * ns, 0:chans]

    d_out, s_h1 = back(acc_out)
    d_inp, ds_f1 = back(acc_in)
    d_carry, _ = back(acc_carry)
    dinb_ref[...] = decay * d_inp + out_c * zeroth
    doutc_ref[...] = d_out + in_b * zeroth
    drate_ref[...] = -(
        out_c * s_h1
        + in_b * decay * (ds_f1 + d_inp)
        + LANES * jnp.exp(-rate * LANES) * d_carry
        + in_b * out_c * first
    )
    yield

    def back_step(i, _):
        for j in range(un):
            c = i * un + j
            rows = pl.ds(pl.multiple_of(c * nb, nb), nb)
            t = toeplitz(kern_ref[pl.ds(c, 1), :])
            g = g_scr[rows, :]
            inner = merge_masked(mm(stack_masked(g, masks), t, NT), masks)
            pp = pp_ref[pl.ds(pl.multiple_of(c * LANES, LANES), LANES), :]
            dur_scr[rows, :] = (mm(x_scr[rows, :].astype(jnp.bfloat16), pp, NT) * keep_rev).astype(jnp.bfloat16)
            g_scr[rows, :] = inner + skip_ref[0, c] * g
        return 0

    lax.fori_loop(0, chans // un, back_step, 0)
    yield
    step_rows = 16 * nb

    def rev_step(i, _):
        rows = pl.ds(pl.multiple_of(i * step_rows, step_rows), step_rows)
        dui_scr[rows, :] = mm(dur_scr[rows, :], flip)
        return 0

    lax.fori_loop(0, chans // 16, rev_step, 0)

    def last_step(i, _):
        for j in range(un):
            c = i * un + j
            rows = pl.ds(pl.multiple_of(c * nb, nb), nb)
            du = g_scr[rows, :] + dui_scr[rows, :]
            dv_scr[rows, :] = du * sh_scr[rows, :]
            ds = du * qkv_ref[2, rows]
            k = qkv_ref[1, rows]
            lane = iota(k.shape, 1)
            red_scr[0, pl.ds(c, 1), :] = jnp.sum(ds * k, axis=0, keepdims=True)
            dk = sw_ref[0, c] * ds
            for lag, prior in enumerate(priors(k, same)):
                red_scr[lag + 1, pl.ds(c, 1), :] = jnp.sum(ds * prior, axis=0, keepdims=True)
                d = ds * same[lag]
                r = pltpu.roll(d, LANES - (lag + 1), axis=1)
                r2 = pltpu.roll(r, nb - 1, axis=0)
                dk = dk + sw_ref[lag + 1, c] * jnp.where(lane < LANES - (lag + 1), r, r2)
            dk_scr[rows, :] = dk
        return 0

    lax.fori_loop(0, chans // un, last_step, 0)
    yield
    for b in range(nb):
        half = b % 2
        for i, scr in ((1, dk_scr), (2, dv_scr)):
            dqkv_ref[b // 2, i, :, half * LANES : (half + 1) * LANES] = scr[
                pl.ds(b, chans, stride=nb), :
            ].astype(jnp.bfloat16)
    yield
    for j in range(SHIFT):
        dsw_ref[j : j + 1, :] = jnp.sum(red_scr[j].T, axis=0, keepdims=True)[:, 0:chans]


MESH = pl.DeviceIdType.MESH


class Place:
    def __init__(self, n_dp, n_head, n_tensor):
        self.n_dp, self.n_head, self.n_tensor = n_dp, n_head, n_tensor
        self.dp = lax.axis_index("dp")
        h, t = lax.axis_index("head"), lax.axis_index("tensor")
        self.size = n_head * n_tensor
        ph, xh, yt = h + 1 - 2 * (h % 2), (h + 2) % n_head, 1 - t
        pxh = (ph + 2) % n_head
        slot = lambda a, b: a * n_tensor + b
        self.me, self.p, self.x, self.y, self.d = (
            slot(h, t), slot(ph, t), slot(xh, t), slot(h, yt), slot(xh, yt),
        )
        self.px, self.py, self.pd = slot(pxh, t), slot(ph, yt), slot(pxh, yt)
        self.to_p, self.to_x, self.to_y = {"head": ph}, {"head": xh}, {"tensor": yt}

    def dp_peer(self, step):
        return (self.dp + step) % self.n_dp

    def greet_all(self, whole_group, over_dp):
        sem = pltpu.get_barrier_semaphore()

        def greet(where):
            pl.semaphore_signal(sem, inc=1, device_id=where, device_id_type=MESH)

        if whole_group:
            for i in range(1, self.size):
                peer = (self.me + i) % self.size
                greet({"head": peer // self.n_tensor, "tensor": peer % self.n_tensor})
            count = self.size - 1
        else:
            for where in (self.to_p, self.to_x, self.to_y):
                greet(where)
            count = 3
        if over_dp:
            def step(i, _):
                greet({"dp": self.dp_peer(i)})
                return 0

            lax.fori_loop(1, self.n_dp, step, 0)
            count += self.n_dp - 1
        return lambda: pl.semaphore_wait(sem, count)


def remote(src, dst, ssem, rsem, where):
    return pltpu.make_async_remote_copy(
        src_ref=src, dst_ref=dst, send_sem=ssem, recv_sem=rsem, device_id=where, device_id_type=MESH
    )


class GroupGather:
    COPIES = 11

    def __init__(self, place, ref, ssem, rsem):
        self.ssem, self.rsem = ssem, rsem
        half = ref.shape[1] // 2
        top, low = pl.ds(0, half), pl.ds(half, half)
        pc = place
        full = lambda s: ref.at[s]
        part = lambda s, rows: ref.at[s, rows]
        self.out = [
            (full(pc.me), pc.to_p),
            (part(pc.me, top), pc.to_x), (part(pc.me, low), pc.to_x),
            (part(pc.me, low), pc.to_y), (part(pc.me, top), pc.to_y),
            (part(pc.x, top), pc.to_y), (part(pc.y, low), pc.to_x),
            (full(pc.x), pc.to_p), (full(pc.y), pc.to_p),
            (part(pc.d, top), pc.to_p), (part(pc.d, low), pc.to_p),
        ]
        self.into = [
            full(pc.p), part(pc.x, top), part(pc.x, low), part(pc.y, low), part(pc.y, top),
            part(pc.d, top), part(pc.d, low), full(pc.px), full(pc.py), part(pc.pd, top), part(pc.pd, low),
        ]

    def send(self, *which):
        for i in which:
            src, where = self.out[i]
            remote(src, src, self.ssem.at[i], self.rsem.at[i], where).start()

    def arrive(self, *which):
        for i in which:
            dst = self.into[i]
            remote(dst, dst, self.ssem.at[i], self.rsem.at[i], self.out[i][1]).wait_recv()

    def start(self):
        self.send(1, 3, 2, 4, 0)

    def first(self):
        self.arrive(1)
        self.send(5)
        self.arrive(3)
        self.send(6)

    def second(self):
        self.arrive(2)
        self.send(7)
        self.arrive(4)
        self.send(8)

    def third(self):
        self.arrive(5)
        self.send(9)
        self.arrive(6)
        self.send(10)

    def finish(self):
        self.arrive(0, 7, 8, 9, 10)

    def drain(self):
        for i in range(self.COPIES):
            src, where = self.out[i]
            remote(src, src, self.ssem.at[i], self.rsem.at[i], where).wait_send()


class DepthGather:
    def __init__(self, place, ref, ssem, rsem):
        self.place, self.ref, self.ssem, self.rsem = place, ref, ssem, rsem

    def _copy(self, step, slot, peer):
        return remote(
            self.ref.at[slot], self.ref.at[slot], self.ssem.at[step], self.rsem.at[step], {"dp": peer}
        )

    def _loop(self, body):
        def step(i, _):
            body(i)
            return 0

        lax.fori_loop(1, self.place.n_dp, step, 0)

    def start(self):
        pc = self.place
        self._loop(lambda i: self._copy(i, pc.dp, pc.dp_peer(i)).start())

    def finish(self):
        pc = self.place
        source = lambda i: (pc.dp + pc.n_dp - i) % pc.n_dp
        self._loop(lambda i: self._copy(i, source(i), pc.dp_peer(i)).wait_recv())

    def drain(self):
        pc = self.place
        self._loop(lambda i: self._copy(i, pc.dp, pc.dp_peer(i)).wait_send())


class LineGather:
    def __init__(self, place, ref, ssem, rsem):
        self.pc, self.ref, self.ssem, self.rsem = place, ref, ssem, rsem
        self.n, self.at = place.n_dp, place.dp
        self.steps = self.n - 1

    def _copy(self, slot, way):
        return remote(
            self.ref.at[slot], self.ref.at[slot], self.ssem.at[way * self.n + slot], self.rsem.at[slot],
            {"dp": self.at + 1 - 2 * way},
        )

    def _pass(self, slot):
        @pl.when((slot <= self.at) & (self.at < self.n - 1))
        def _():
            self._copy(slot, 0).start()

        @pl.when((slot >= self.at) & (self.at > 0))
        def _():
            self._copy(slot, 1).start()

    def start(self):
        self._pass(self.at)

    def step(self, s):
        below, above = self.at - 1 - s, self.at + 1 + s

        @pl.when(below >= 0)
        def _():
            self._copy(below, 0).wait_recv()

            @pl.when(self.at < self.n - 1)
            def _():
                self._copy(below, 0).start()

        @pl.when(above < self.n)
        def _():
            self._copy(above, 1).wait_recv()

            @pl.when(self.at > 0)
            def _():
                self._copy(above, 1).start()

    def rest(self, first):
        def body(s, _):
            self.step(s)
            return 0

        lax.fori_loop(first, self.steps, body, 0)

    def drain(self):
        def body(slot, _):
            @pl.when((slot <= self.at) & (self.at < self.n - 1))
            def _():
                self._copy(slot, 0).wait_send()

            @pl.when((slot >= self.at) & (self.at > 0))
            def _():
                self._copy(slot, 1).wait_send()

            return 0

        lax.fori_loop(0, self.n, body, 0)


def joined(ref):
    n, rows, columns = ref.shape
    if rows % 16 == 0:
        return ref[...].reshape(n * rows, columns)
    parts = [ref[j].astype(jnp.float32) for j in range(n)]
    return jnp.concatenate(parts, axis=0).astype(ref.dtype)


def row_norm(x):
    centred = x - jnp.mean(x, axis=1, keepdims=True)
    inv = lax.rsqrt(jnp.mean(centred * centred, axis=1, keepdims=True) + 1e-05)
    return centred * inv, inv


class GroupReduce:
    COPIES = 10

    def __init__(self, place, part, land, half_land, last_land, ssem, rsem):
        pc = place
        self.pc = pc
        self.part, self.land, self.half_land, self.last_land = part, land, half_land, last_land
        self.ssem, self.rsem = ssem, rsem
        half = part.shape[1] // 2
        top, low = pl.ds(0, half), pl.ds(half, half)
        self.top, self.low = top, low
        self.mine = [pc.d, pc.x, pc.y, pc.me]
        self.theirs = [pc.pd, pc.px, pc.py, pc.p]
        self.copies = [(part.at[self.theirs[i]], land.at[i], pc.to_p) for i in range(4)] + [
            (part.at[pc.d, top], half_land.at[0], pc.to_x),
            (part.at[pc.d, low], half_land.at[1], pc.to_y),
            (part.at[pc.x, top], last_land.at[0, top], pc.to_x),
            (part.at[pc.y, low], last_land.at[1, low], pc.to_y),
            (part.at[pc.x, low], last_land.at[0, low], pc.to_x),
            (part.at[pc.y, top], last_land.at[1, top], pc.to_y),
        ]

    def _copy(self, i):
        src, dst, where = self.copies[i]
        return remote(src, dst, self.ssem.at[i], self.rsem.at[i], where)

    def give(self, *which):
        for i in which:
            self._copy(i).start()

    def pair(self, i):
        self._copy(i).wait_recv()
        s = self.mine[i]
        self.part[s] = (self.part[s].astype(jnp.float32) + self.land[i].astype(jnp.float32)).astype(
            self.part.dtype
        )

    def side(self):
        self.pair(1)
        self.give(6)
        self.pair(2)
        self.give(7)

    def far(self):
        self.pair(0)
        self.give(4, 5)

    def near(self):
        for i, s, rows in ((4, self.pc.y, self.top), (5, self.pc.x, self.low)):
            self._copy(i).wait_recv()
            self.part[s, rows] = (
                self.part[s, rows].astype(jnp.float32) + self.half_land[i - 4].astype(jnp.float32)
            ).astype(self.part.dtype)
            self.give(9 if i == 4 else 8)

    def total(self):
        for i in (6, 7, 8, 9):
            self._copy(i).wait_recv()
        return (
            self.part[self.pc.me].astype(jnp.float32)
            + self.last_land[0].astype(jnp.float32)
            + self.last_land[1].astype(jnp.float32)
        )

    def drain(self):
        for i in range(self.COPIES):
            self._copy(i).wait_send()

    @staticmethod
    def scratch(group, rows, columns):
        bf16 = jnp.bfloat16
        return [
            pltpu.VMEM((group, rows, columns), bf16),
            pltpu.VMEM((4, rows, columns), bf16),
            pltpu.VMEM((2, rows // 2, columns), bf16),
            pltpu.VMEM((2, rows, columns), bf16),
        ]


class GroupSwap:
    def __init__(self, place, src, dst, lsem, rows, ssem, rsem):
        self.pc, self.src, self.dst, self.ssem, self.rsem, self.lsem = place, src, dst, ssem, rsem, lsem
        self.rows = rows

    def _peer(self, i):
        return (self.pc.me + i) % self.pc.size

    def _copy(self, i, slot):
        peer = self._peer(i)
        where = {"head": peer // self.pc.n_tensor, "tensor": peer % self.pc.n_tensor}
        return remote(
            self.src.at[peer, self.rows], self.dst.at[slot, self.rows], self.ssem.at[i], self.rsem.at[i], where
        )

    def _own(self):
        me = self.pc.me
        return pltpu.make_async_copy(self.src.at[me, self.rows], self.dst.at[me, self.rows], self.lsem)

    def start(self):
        for i in range(1, self.pc.size):
            self._copy(i, self.pc.me).start()
        self._own().start()

    def finish(self):
        for i in range(1, self.pc.size):
            self._copy(i, (self.pc.me + self.pc.size - i) % self.pc.size).wait_recv()
        self._own().wait()

    def drain(self):
        for i in range(1, self.pc.size):
            self._copy(i, self.pc.me).wait_send()


class DepthReduce:
    def __init__(self, place, src, land, ssem, rsem):
        self.place, self.src, self.land, self.ssem, self.rsem = place, src, land, ssem, rsem

    def _copy(self, step, mine, slot, peer):
        return remote(
            self.src.at[mine], self.land.at[slot], self.ssem.at[step], self.rsem.at[step], {"dp": peer}
        )

    def _loop(self, body, start):
        return lax.fori_loop(1, self.place.n_dp, body, start)

    def start(self):
        pc = self.place

        def step(i, _):
            self._copy(i, pc.dp_peer(i), pc.dp, pc.dp_peer(i)).start()
            return 0

        self._loop(step, 0)

    def total(self):
        pc = self.place

        def step(i, acc):
            source = (pc.dp + pc.n_dp - i) % pc.n_dp
            self._copy(i, source, source, pc.dp_peer(i)).wait_recv()
            return acc + self.land[source].astype(jnp.float32)

        return self._loop(step, self.src[pc.dp].astype(jnp.float32))

    def drain(self):
        pc = self.place

        def step(i, _):
            self._copy(i, pc.dp_peer(i), pc.dp, pc.dp_peer(i)).wait_send()
            return 0

        self._loop(step, 0)


def split_rows(ref, value):
    n, rows, columns = ref.shape
    if rows % 16 == 0:
        ref[...] = value.astype(ref.dtype).reshape(n, rows, columns)
    else:
        for j in range(n):
            ref[j] = value[j * rows : (j + 1) * rows].astype(ref.dtype)


def row_norm_back(grad, gain, hat, inv):
    scaled = grad * gain
    return inv * (
        scaled
        - jnp.mean(scaled, axis=1, keepdims=True)
        - hat * jnp.mean(scaled * hat, axis=1, keepdims=True)
    )


def gelu_pair(pre):
    cdf = 0.5 * (1.0 + lax.erf(pre * 0.7071067811865476))
    return pre * cdf, cdf + pre * (0.3989422804014327 * jnp.exp(-0.5 * pre * pre))


class GroupSpread:
    def __init__(self, place, ref, ssem, rsem):
        self.pc, self.ref, self.ssem, self.rsem = place, ref, ssem, rsem

    def _copy(self, i, slot):
        peer = (self.pc.me + i) % self.pc.size
        where = {"head": peer // self.pc.n_tensor, "tensor": peer % self.pc.n_tensor}
        return remote(self.ref.at[slot], self.ref.at[slot], self.ssem.at[i], self.rsem.at[i], where)

    def start(self):
        for i in range(1, self.pc.size):
            self._copy(i, self.pc.me).start()

    def finish(self):
        for i in range(1, self.pc.size):
            self._copy(i, (self.pc.me + self.pc.size - i) % self.pc.size).wait_recv()

    def drain(self):
        for i in range(1, self.pc.size):
            self._copy(i, self.pc.me).wait_send()


SKIP_AT, PARAM_ROWS = 192, 208
UNROLL = 24


class Names:
    def __init__(self, names, refs):
        assert len(names) == len(refs)
        for name, ref in zip(names, refs):
            setattr(self, name, ref)


def layout(axes, own, feats, rows, chans, units, ns, results):
    n_dp, n_head, n_tensor = axes
    group = n_head * n_tensor
    f32, bf16 = jnp.float32, jnp.bfloat16
    v = pltpu.VMEM
    dma = lambda *shape: pltpu.SemaphoreType.DMA(shape)
    blocks = group * own // LANES
    conv = chans * blocks
    sq = v((LANES, LANES), f32)
    full = v((conv, LANES), f32)
    out = dict(
        tok=v((own, feats), bf16), cot=v((own, feats), bf16), four=v((4, rows, chans), bf16),
        wqkvo=v((n_dp, rows, 4 * chans), bf16), wup=v((n_dp, rows, units), bf16), wdown=v((n_dp, rows, units), bf16),
        wt=v((4 * chans, feats), bf16), wupt=v((units, feats), bf16), wdownt=v((units, feats), bf16),
        wout=v((group, chans, feats), bf16),
        xn1=v((group, feats, own), bf16), cots=v((group, feats, own), bf16), xn2=v((group, feats, own), bf16),
        act=v((group, units, own), bf16), gpre=v((group, units, own), bf16),
        qkv=v((3, conv, LANES), f32), core=full, s=full, f=full, urev=v((conv, LANES), bf16),
        pp=v((chans * LANES, LANES), bf16), kern=v((chans, LANES), f32),
        mixed=v((group, chans, own), bf16), mixed_in=v((group, chans, own), bf16),
        gmix=v((group, chans, own), bf16), gmix_in=v((group, chans, own), bf16),
        dqkv=v((group, 3, chans, own), bf16),
        t0=sq, t1=sq, t2=sq, t3=sq, t4=sq, t5=sq, gr=sq, red=v((SHIFT + 1, LANES, LANES), f32),
        w0=full, w1=full, w2=full, w3=full, w4=full, w5=full, w6=full, dur=v((conv, LANES), bf16),
        dsw=v((SHIFT, chans), f32), drate=v((ns, chans), f32), dinb=v((ns, chans), f32), doutc=v((ns, chans), f32),
        dskip=v((1, chans), f32),
        hat=v((own, feats), f32), hid=v((own, feats), f32), ghid=v((own, feats), f32),
        up_part=v((n_dp, rows, units), bf16), up_land=v((n_dp, rows, units), bf16),
        dn_part=v((n_dp, rows, units), bf16), dn_land=v((n_dp, rows, units), bf16),
        q_part=v((n_dp, rows, chans), bf16), q_land=v((n_dp, rows, chans), bf16),
        o_out=v((n_dp, rows, chans), bf16), o_in=v((n_dp, rows, chans), bf16),
        kv_part=v((n_dp, rows, 2 * chans), bf16), kv_land=v((n_dp, rows, 2 * chans), bf16),
        taps_all=v((n_dp, 8, LANES), f32),
        params=v((n_dp, PARAM_ROWS, LANES), bf16),
        n1=v((group, 2, feats), f32), n2=v((group, 2, feats), f32), m1=v((n_dp, 2, feats), f32), m2=v((n_dp, 2, feats), f32),
    )
    out.update(
        seg=v((1, group * own), jnp.int32), rate=v((ns, chans), f32), inb=v((ns, chans), f32), outc=v((ns, chans), f32),
        gain1=v((feats,), f32), bias1=v((feats,), f32), gain2=v((feats,), f32), bias2=v((feats,), f32),
    )
    out.update((name, v(a.shape, a.dtype)) for name, a in zip(RESULTS, results))
    for name, height, width in (("x", feats, own), ("m", feats, own), ("o", chans, feats)):
        for part, alloc in zip(("part", "land", "half", "last"), GroupReduce.scratch(group, height, width)):
            out[f"{name}_{part}"] = alloc
    for name, count in (
        ("xn1", 11), ("cots", 11), ("wout", 11), ("xn2", 11), ("x2", 10), ("m", 10), ("o", 10), ("x1", 10),
        ("in0", group), ("in1", group), ("back0", group), ("back1", group), ("sp1", group), ("sp2", group),
        ("zq", n_dp), ("zu", n_dp), ("zd", n_dp), ("gu", n_dp), ("gd", n_dp), ("gq", n_dp), ("go", n_dp), ("gkv", n_dp), ("zt", n_dp), ("zp", n_dp),
        ("zn1", n_dp), ("zn2", n_dp),
    ):
        out[f"send_{name}"] = dma(count)
        out[f"recv_{name}"] = dma(count)
    out["local"] = dma(12)
    out["small"] = dma(len(SMALL))
    out["given"] = dma(len(RESULTS))
    return out


INPUTS = (
    "tok_hbm", "cot_hbm", "q_hbm", "k_hbm", "v_hbm", "o_hbm", "up_hbm", "down_hbm",
    "seg_hbm", "gain1_hbm", "bias1_hbm", "gain2_hbm", "bias2_hbm", "taps", "rate_hbm", "inb_hbm", "outc_hbm", "skip",
)
RESULTS = (
    "res", "gx", "g1", "b1", "g2", "b2", "dq", "dk", "dv", "do", "dup", "ddown",
    "out_taps", "out_rate", "out_inb", "out_outc", "out_skip",
)
OUTPUTS = tuple(name + "_hbm" for name in RESULTS)
SMALL = ("seg", "gain1", "bias1", "gain2", "bias2", "rate", "inb", "outc")


def run_beside(body, tasks):
    tasks = list(tasks)
    for _ in body:
        if tasks:
            tasks.pop(0)()
    for task in tasks:
        task()


def block_kernel(axes, names, *refs):
    r = Names(names, refs)
    pc = Place(*axes)
    f32, bf16 = jnp.float32, jnp.bfloat16
    group, chans, feats = r.wout.shape
    own = r.tok.shape[0]
    blocks = own // LANES
    work = []

    def sems(name):
        return getattr(r, f"send_{name}"), getattr(r, f"recv_{name}")

    def make(kind, name, *args):
        made = kind(pc, *args, *sems(name))
        work.append(made)
        return made

    def local(i, src, dst):
        copy = pltpu.make_async_copy(src, dst, r.local.at[i])
        copy.start()
        return copy

    load_tok = local(4, r.tok_hbm, r.tok)
    small = []
    for i, name in enumerate(SMALL):
        small.append(pltpu.make_async_copy(getattr(r, name + "_hbm"), getattr(r, name), r.small.at[i]))
        small[-1].start()
    given = []

    def give(*which):
        for name in which:
            i = RESULTS.index(name)
            given.append(pltpu.make_async_copy(getattr(r, name), getattr(r, name + "_hbm"), r.given.at[i]))
            given[-1].start()

    four = [local(i, src, r.four.at[i]) for i, src in enumerate((r.q_hbm, r.k_hbm, r.v_hbm, r.o_hbm))]
    load_cot = local(5, r.cot_hbm, r.cot)
    load_up = local(6, r.up_hbm, r.wup.at[pc.dp])
    load_down = local(7, r.down_hbm, r.wdown.at[pc.dp])
    meet = pc.greet_all(True, True)
    z_qkvo = make(DepthGather, "zq", r.wqkvo)
    z_up = make(DepthGather, "zu", r.wup)
    z_down = make(DepthGather, "zd", r.wdown)
    xn1_g = make(GroupGather, "xn1", r.xn1)
    cot_g = make(GroupGather, "cots", r.cots)
    out_g = make(GroupGather, "wout", r.wout)
    xn2_g = make(GroupGather, "xn2", r.xn2)
    halves = [pl.ds(i * (chans // PARTS), chans // PARTS) for i in range(PARTS)]
    swap_in = [make(GroupSwap, f"in{i}", r.mixed, r.mixed_in, r.local.at[8 + i], rows) for i, rows in enumerate(halves)]
    swap_back = [make(GroupSwap, f"back{i}", r.gmix, r.gmix_in, r.local.at[10 + i], rows) for i, rows in enumerate(halves)]
    for copy in small:
        copy.wait()
    gain1, gain2 = r.gain1[...].reshape(1, feats), r.gain2[...].reshape(1, feats)
    bias1, bias2 = r.bias1[...].reshape(1, feats), r.bias2[...].reshape(1, feats)
    load_tok.wait()
    hat1, _ = row_norm(r.tok[...].astype(f32))
    r.xn1[pc.me] = (hat1 * gain1 + bias1).astype(bf16).T
    for copy in four:
        copy.wait()
    r.wqkvo[pc.dp] = jnp.concatenate([r.four[i] for i in range(4)], axis=1)
    meet()
    xn1_g.start()
    z_qkvo.start()
    load_cot.wait()
    r.cots[pc.me] = r.cot[...].T
    xn1_g.first()
    xn1_g.second()
    z_qkvo.finish()
    load_up.wait()
    z_up.start()
    r.wt[...] = joined(r.wqkvo).T
    r.wout[pc.me] = r.wt[3 * chans :, :]
    out_g.start()
    load_down.wait()

    def project(s):
        y = mm(r.wt[0 : 3 * chans, :], r.xn1[s])
        for i in range(3):
            for h in range(blocks):
                r.qkv[i, pl.ds(s * blocks + h, chans, stride=group * blocks), :] = y[
                    i * chans : (i + 1) * chans, h * LANES : (h + 1) * LANES
                ]

    xn1_g.third()
    xn1_g.finish()
    for s in range(group):
        project(s)

    def after_drive():
        out_g.first()
        out_g.second()
        cot_g.start()

    def after_scan():
        out_g.third()

    def half_out():
        swap_in[0].start()
        z_up.finish()
        z_down.start()

    mixer = (r.seg, r.taps, r.skip, r.rate, r.inb, r.outc)
    run_beside(
        mixer_forward(
            UNROLL, r.qkv, *mixer, r.mixed, r.core, r.s, r.f, r.urev, r.pp, r.kern,
            r.t0, r.t1, r.t2, r.t3, r.t4, r.w0, r.t5,
        ),
        (after_drive, lambda: None, lambda: None, after_scan, half_out, swap_in[1].start),
    )
    cot_g.first()
    out_g.finish()
    cot_g.second()
    w_up = joined(r.wup)
    r.wupt[...] = w_up.T
    wout_t = r.wout[...].reshape(feats, feats)
    swap_in[0].finish()
    swap_in[1].finish()
    mixed_t = r.mixed_in[...].reshape(feats, own)
    hidden = r.tok[...].astype(f32) + mm(mixed_t, wout_t, TN)
    hat2, inv2 = row_norm(hidden)
    r.xn2[pc.me] = (hat2 * gain2 + bias2).astype(bf16).T
    xn2_g.start()
    r.hid[...] = hidden
    r.hat[...] = hat2
    cot_g.third()
    z_down.finish()
    w_down = joined(r.wdown)
    r.wdownt[...] = w_down.T
    cot_g.finish()
    red_x2 = make(GroupReduce, "x2", r.x_part, r.x_land, r.x_half, r.x_last)
    red_m = make(GroupReduce, "m", r.m_part, r.m_land, r.m_half, r.m_last)
    red_o = make(GroupReduce, "o", r.o_part, r.o_land, r.o_half, r.o_last)

    def chunk(s):
        act, slope = gelu_pair(mm(r.wupt[...], r.xn2[s]))
        r.act[s] = act.astype(bf16)
        grad_pre = (mm(r.wdownt[...], r.cots[s]) * slope).astype(bf16)
        r.gpre[s] = grad_pre
        r.x_part[s] = mm(w_up, grad_pre).astype(bf16)

    chunk(pc.me)
    xn2_g.arrive(0)
    chunk(pc.p)
    red_x2.give(3)
    xn2_g.first()
    xn2_g.second()
    chunk(pc.x)
    chunk(pc.y)
    xn2_g.arrive(7)
    chunk(pc.px)
    red_x2.give(1)
    xn2_g.arrive(8)
    chunk(pc.py)
    red_x2.give(2)
    xn2_g.third()
    red_x2.side()
    chunk(pc.d)
    xn2_g.arrive(9, 10)
    chunk(pc.pd)
    red_x2.give(0)
    red_x2.pair(3)
    red_x2.far()
    units = r.act.shape[1]
    grad_up = jnp.zeros((feats, units), f32)
    for s in range(group):
        grad_up = grad_up + mm(r.xn2[s], r.gpre[s], NT)
    split_rows(r.up_part, grad_up)
    sum_up = make(DepthReduce, "gu", r.up_part, r.up_land)
    sum_up.start()
    red_x2.near()
    for i, s in enumerate(red_m.theirs):
        r.m_part[s] = mm(w_down, r.act[s]).astype(bf16)
        red_m.give(i)
    for s in red_m.mine:
        r.m_part[s] = mm(w_down, r.act[s]).astype(bf16)
    grad_down = jnp.zeros((feats, units), f32)
    for s in range(group):
        grad_down = grad_down + mm(r.cots[s], r.act[s], NT)
    split_rows(r.dn_part, grad_down)
    sum_down = make(DepthReduce, "gd", r.dn_part, r.dn_land)
    sum_down.start()
    grad_xn = red_x2.total().T
    hat2 = r.hat[...]
    grad_hidden = r.cot[...].astype(f32) + row_norm_back(grad_xn, gain2, hat2, inv2)
    r.ghid[...] = grad_hidden
    grad_mix = grad_hidden.astype(bf16)
    r.gmix[...] = mm(wout_t, grad_mix, NT).astype(bf16).reshape(group, chans, own)
    swap_back[0].start()
    swap_back[1].start()
    r.n2[pc.me, 0:1, :] = jnp.sum(grad_xn * hat2, axis=0, keepdims=True)
    r.n2[pc.me, 1:2, :] = jnp.sum(grad_xn, axis=0, keepdims=True)
    spread2 = make(GroupSpread, "sp2", r.n2)
    spread2.start()
    r.o_part[...] = mm(mixed_t, grad_mix).astype(bf16).reshape(group, chans, feats)
    red_o.give(0, 1, 2, 3)
    swap_back[0].finish()
    norm2 = make(DepthGather, "zn2", r.m2)

    ns = r.drate.shape[0]
    pieces = ((0, r.drate, r.out_rate), (ns, r.dinb, r.out_inb), (2 * ns, r.doutc, r.out_outc),
              (SKIP_AT, r.dskip, r.out_skip))
    z_par = make(DepthGather, "zp", r.params)
    sum_q = make(DepthReduce, "gq", r.q_part, r.q_land)
    sum_o = make(DepthReduce, "go", r.o_out, r.o_in)
    sum_kv = make(DepthReduce, "gkv", r.kv_part, r.kv_land)

    def second_half():
        swap_back[1].finish()
        red_o.far()
        red_o.side()
        red_m.far()

    def row_of(x):
        return jnp.broadcast_to(jnp.sum(x, axis=1, keepdims=True), (x.shape[0], LANES)).T[0:1]

    def early_sums():
        w_wide = joined(r.wqkvo).astype(f32)
        red_o.near()
        r.params[pc.dp] = jnp.zeros(r.params.shape[1:], bf16)
        for at, ref, _ in pieces:
            r.params[pc.dp, at : at + ref.shape[0], 0:chans] = ref[...].astype(bf16)
        z_par.start()
        grad_q = jnp.zeros((feats, chans), f32)
        for s in range(group):
            grad_q = grad_q + mm(r.xn1[s], r.dqkv[s, 0], NT)
        split_rows(r.q_part, grad_q)
        sum_q.start()
        r.n1[pc.me, 0:1, :] = row_of(grad_q * w_wide[:, 0:chans])

    def mlp_sums():
        red_m.side()
        red_m.near()
        red_x2.drain()
        work.remove(red_x2)

    def out_sums():
        red_o.pair(3)
        split_rows(r.o_out, red_o.total().T)
        sum_o.start()

    w_joint = joined(r.wqkvo)
    red_x1 = make(GroupReduce, "x1", r.x_part, r.x_land, r.x_half, r.x_last)

    def grads(s):
        return r.dqkv[s].reshape(3 * chans, own)

    def chunk_back(s):
        padded = jnp.concatenate([grads(s), jnp.zeros((chans, own), bf16)], axis=0)
        r.x_part[s] = mm(w_joint, padded).astype(bf16)

    spread1 = make(GroupSpread, "sp1", r.n1)
    norm1 = make(DepthGather, "zn1", r.m1)

    def start_back():
        theirs, mine = red_x1.theirs, red_x1.mine
        chunk_back(theirs[0])
        red_x1.give(0)
        chunk_back(mine[0])
        chunk_back(theirs[1])
        red_x1.give(1)
        chunk_back(mine[1])
        grad_kv = jnp.zeros((feats, 2 * chans), f32)
        for s in range(group):
            grad_kv = grad_kv + mm(r.xn1[s], grads(s)[chans:], NT)
        split_rows(r.kv_part, grad_kv)
        sum_kv.start()
        w_wide = w_joint.astype(f32)
        token_sums = jnp.zeros((8, 3 * chans), f32)
        for s in range(group):
            token_sums = token_sums + mm(jnp.ones((8, own), bf16), grads(s), NT)
        r.n1[pc.me, 0:1, :] += row_of(grad_kv * w_wide[:, chans : 3 * chans])
        r.n1[pc.me, 1:2, :] = row_of(w_wide[:, 0 : 3 * chans] * token_sums[0:1])
        spread1.start()
        red_x1.far()
        chunk_back(theirs[2])
        red_x1.give(2)
        chunk_back(mine[2])
        chunk_back(theirs[3])
        red_x1.give(3)
        red_x1.side()
        chunk_back(mine[3])

    run_beside(
        mixer_backward(
            UNROLL, r.gmix_in, r.qkv, r.core, r.s, r.f, r.urev, r.pp, r.kern, *mixer,
            r.dqkv, r.dsw, r.drate, r.dinb, r.doutc, r.dskip,
            r.t0, r.t1, r.t2, r.t3, r.w0, r.w1, r.w2, r.w3, r.dur, r.w2, r.w4, r.w5, r.w6, r.gr, r.red,
        ),
        (second_half, lambda: None, early_sums, mlp_sums, out_sums, start_back),
    )
    r.taps_all[pc.dp] = jnp.zeros(r.taps_all.shape[1:], f32)
    r.taps_all[pc.dp, 0:SHIFT, 0:chans] = r.dsw[...]
    z_taps = make(DepthGather, "zt", r.taps_all)
    z_taps.start()
    spread2.finish()
    r.m2[pc.dp] = jnp.sum(r.n2[...], axis=0)
    norm2.start()
    red_x1.near()
    red_x1.pair(3)
    spread1.finish()
    r.m1[pc.dp] = jnp.sum(r.n1[...], axis=0)
    norm1.start()
    red_m.pair(3)
    r.res[...] = (r.hid[...] + red_m.total().T).astype(bf16)
    give("res")
    r.dup[...] = sum_up.total()
    r.ddown[...] = sum_down.total()
    give("dup", "ddown")
    z_par.finish()
    sums = jnp.sum(r.params[...].astype(f32), axis=0)
    for at, ref, out in pieces:
        out[...] = sums[at : at + ref.shape[0], 0:chans]
    give("out_rate", "out_inb", "out_outc", "out_skip")
    z_taps.finish()
    r.out_taps[...] = jnp.sum(r.taps_all[...], axis=0)[0:SHIFT, 0:chans]
    give("out_taps")
    norm2.finish()
    sums = jnp.sum(r.m2[...], axis=0)
    r.g2[...] = sums[0:1]
    r.b2[...] = sums[1:2]
    give("g2", "b2")
    r.do[...] = sum_o.total()
    r.dq[...] = sum_q.total()
    kv_sum = sum_kv.total()
    r.dk[...] = kv_sum[:, 0:chans]
    r.dv[...] = kv_sum[:, chans:]
    give("dq", "dk", "dv", "do")
    norm1.finish()
    sums = jnp.sum(r.m1[...], axis=0)
    r.g1[...] = (sums[0:1] - bias1 * sums[1:2]) / gain1
    r.b1[...] = sums[1:2]
    give("g1", "b1")
    hat1, inv1 = row_norm(r.tok[...].astype(f32))
    grad_xn = red_x1.total().T
    r.gx[...] = r.ghid[...] + row_norm_back(grad_xn, gain1, hat1, inv1)
    give("gx")
    for one in work:
        one.drain()
    for copy in given:
        copy.wait()


def hand_over(count, *refs):
    src, dst, mid, flat = refs[:count], refs[count : 2 * count], refs[2 * count : 3 * count], refs[3 * count : -2]
    sem_in, sem_out = refs[-2:]
    loads = [pltpu.make_async_copy(a, b, sem_in.at[i]) for i, (a, b) in enumerate(zip(src, mid))]
    for load in loads:
        load.start()
    flat = iter(flat)
    stores = []
    for i, load in enumerate(loads):
        load.wait()
        held = mid[i]
        if src[i].shape != dst[i].shape:
            held = next(flat)
            held[...] = mid[i][...].reshape(held.shape)
        stores.append(pltpu.make_async_copy(held, dst[i], sem_out.at[i]))
        stores[-1].start()
    for store in stores:
        store.wait()


def whole_block(axes, args):
    (tokens, seg, gain1, bias1, gain2, bias2, q, k, v, o, up, down, taps, rate, inb, outc, skip, cot) = args
    own, feats = tokens.shape
    rows, chans = q.shape
    units = up.shape[1]
    f32, bf16 = jnp.float32, jnp.bfloat16
    sds = jax.ShapeDtypeStruct
    vm = pl.BlockSpec(memory_space=pltpu.VMEM)
    sm = pl.BlockSpec(memory_space=pltpu.SMEM)
    hbm = pl.BlockSpec(memory_space=pl.ANY)
    wide, thin = sds((rows, units), f32), sds((rows, chans), f32)
    row = sds((1, feats), f32)
    results = (
        sds((own, feats), bf16), sds((own, feats), f32), row, row, row, row, thin, thin, thin, thin, wide, wide,
        *(sds(a.shape, f32) for a in (taps, rate, inb, outc)), sds((1, chans), f32),
    )
    scratch = layout(axes, own, feats, rows, chans, units, rate.shape[0], results)
    outs = pl.pallas_call(
        functools.partial(block_kernel, axes, INPUTS + OUTPUTS + tuple(scratch)),
        out_shape=results,
        in_specs=[hbm] * 13 + [sm] + [hbm] * 3 + [sm],
        out_specs=(hbm,) * 17,
        scratch_shapes=list(scratch.values()),
        compiler_params=pltpu.CompilerParams(
            collective_id=1, has_side_effects=True, vmem_limit_bytes=67043328
        ),
        name="block",
    )(tokens, cot, q, k, v, o, up, down, seg, gain1, bias1, gain2, bias2, taps, rate, inb, outc, skip[None])
    final = [sds(a.shape, a.dtype) for a in outs]
    for i in (2, 3, 4, 5):
        final[i] = sds((feats,), f32)
    final[16] = sds((chans,), f32)
    held = [pltpu.VMEM(a.shape, a.dtype) for a in outs]
    flat = [pltpu.VMEM(b.shape, b.dtype) for a, b in zip(outs, final) if a.shape != b.shape]
    count = len(outs)
    return pl.pallas_call(
        functools.partial(hand_over, count),
        out_shape=tuple(final),
        in_specs=[hbm] * count,
        out_specs=(hbm,) * count,
        scratch_shapes=held + flat + [pltpu.SemaphoreType.DMA((count,))] * 2,
        name="hand_over",
    )(*outs)


from jax.sharding import PartitionSpec as P

GROUP = ("head", "tensor")


def on_device(*args):
    return whole_block((lax.axis_size("dp"), lax.axis_size("head"), lax.axis_size("tensor")), args)


def solution(mesh):
    rows = P(("dp", "head", "tensor"), None)
    weight = P("dp", GROUP)
    chan = P(None, GROUP)
    in_specs = (rows, P("dp", None)) + (P(),) * 4 + (weight,) * 6 + (chan,) * 4 + (P(GROUP), rows)
    out_specs = (rows, rows) + (P(),) * 4 + (weight,) * 6 + (chan,) * 4 + (P(GROUP),)
    return jax.shard_map(on_device, mesh=mesh, in_specs=in_specs, out_specs=out_specs, check_vma=False)
```

```python
import functools
import jax, jax.numpy as jnp
from jax import lax
from jax.experimental import pallas as pl
from jax.experimental.pallas import tpu as pltpu

LANES = 128
SHIFT = 4
SEQS = 3
PARTS = 2
NT = (((1,), (1,)), ((), ()))
TN = (((0,), (0,)), ((), ()))
NN = (((1,), (0,)), ((), ()))


def mm(left, right, dims=NN):
    return lax.dot_general(left, right, dims, preferred_element_type=jnp.float32)


def iota(shape, axis):
    return lax.broadcasted_iota(jnp.int32, shape, axis)


def seg_masks(seg, nb):
    lane = iota((nb, LANES), 1)
    row = iota((nb, LANES), 0)
    masks = [(seg == k).astype(jnp.float32) for k in range(SEQS)]
    end = jnp.broadcast_to(seg[:, LANES - 1 :], (nb, LANES))
    last = jnp.where(row == 0, -1, pltpu.roll(end, 1, axis=0))
    live = (seg == last).astype(jnp.float32)
    keep = (seg == end).astype(jnp.float32)
    carry = (end == last).astype(jnp.float32)
    same = []
    for j in range(1, SHIFT):
        r = pltpu.roll(seg, j, axis=1)
        r2 = pltpu.roll(r, 1, axis=0)
        prior = jnp.where(lane < j, r2, r)
        ok = (prior == seg) & ((row > 0) | (lane >= j))
        same.append(ok.astype(jnp.float32))
    return masks, live, keep, carry, same


def priors(k, same):
    lane = iota(k.shape, 1)
    out = []
    for j in range(1, SHIFT):
        r = pltpu.roll(k, j, axis=1)
        r2 = pltpu.roll(r, 1, axis=0)
        out.append(jnp.where(lane < j, r2, r) * same[j - 1])
    return out


def flip_matrix():
    return (iota((LANES, LANES), 0) + iota((LANES, LANES), 1) == LANES - 1).astype(jnp.bfloat16)


def read_seg(seg_ref, nb):
    return jnp.concatenate([seg_ref[:, b * LANES : (b + 1) * LANES] for b in range(nb)], axis=0)


def transposed(scr, top, bottom):
    ns, chans = top.shape
    scr[...] = jnp.zeros_like(scr)
    scr[0:ns, 0:chans] = top
    if bottom is not None:
        scr[ns : 2 * ns, 0:chans] = bottom
    return scr[...].T


def stack_masked(x, masks):
    return jnp.concatenate([x * m for m in masks], axis=0).astype(jnp.bfloat16)


def merge_masked(y, masks):
    nb = masks[0].shape[0]
    return sum(y[i * nb : (i + 1) * nb] * m for i, m in enumerate(masks))


def toeplitz(krow):
    t = pltpu.roll(jnp.broadcast_to(krow, (LANES, LANES)), 0, axis=1, stride=1, stride_axis=0)
    return jnp.where(iota((LANES, LANES), 1) >= iota((LANES, LANES), 0), t, 0.0).astype(jnp.bfloat16)


def mixer_forward(
    un, qkv_ref, seg_ref, sw_ref, skip_ref, rate_ref, inb_ref, outc_ref,
    mixed_ref, core_ref, s_ref, f_ref, urev_ref, pp_ref, kern_ref,
    tscr, a_scr, b_scr, c_scr, e_scr, u_scr, kscr,
):
    ns, chans = rate_ref.shape
    nb = qkv_ref.shape[1] // chans
    masks, live, keep, carry, same = seg_masks(read_seg(seg_ref, nb), nb)
    flip = flip_matrix()
    keep_rev = mm(keep.astype(jnp.bfloat16), flip)
    rate, in_b, out_c = rate_ref[...], inb_ref[...], outc_ref[...]
    decay = jnp.exp(-rate)
    a_scr[...] = transposed(tscr, rate, rate)
    b_scr[...] = transposed(tscr, in_b * decay, None)
    c_scr[...] = transposed(tscr, out_c, None)
    e_scr[...] = transposed(tscr, jnp.exp(-rate * LANES), None)

    def kern_step(i, e):
        for j in range(8):
            kscr[pl.ds(i * 8 + j, 1), 0:chans] = jnp.sum(e, axis=0, keepdims=True)
            e = e * decay
        return e

    kscr[...] = jnp.zeros_like(kscr)
    lax.fori_loop(0, LANES // 8, kern_step, in_b * out_c)
    kern_ref[...] = kscr[...].T[0:chans]

    def drive_step(i, _):
        for j in range(un):
            c = i * un + j
            rows = pl.ds(pl.multiple_of(c * nb, nb), nb)
            k = qkv_ref[1, rows]
            shifted = sw_ref[0, c] * k
            for lag, prior in enumerate(priors(k, same)):
                shifted = shifted + sw_ref[lag + 1, c] * prior
            u_scr[rows, :] = shifted * qkv_ref[2, rows]
        return 0

    lax.fori_loop(0, chans // un, drive_step, 0)
    yield
    step_rows = 16 * nb

    def rev_step(i, _):
        rows = pl.ds(pl.multiple_of(i * step_rows, step_rows), step_rows)
        urev_ref[rows, :] = mm(u_scr[rows, :].astype(jnp.bfloat16), flip).astype(jnp.bfloat16)
        return 0

    lax.fori_loop(0, chans // 16, rev_step, 0)
    pos = iota((LANES, LANES), 0).astype(jnp.float32)
    factor = jnp.where(iota((LANES, LANES), 1) < ns, 1.0, pos)
    i8 = iota((8, LANES), 0).astype(jnp.float32)
    i16 = iota((LANES // 8, LANES), 0).astype(jnp.float32) * 8.0

    def fresh_step(i, _):
        for j in range(un):
            c = i * un + j
            rows = pl.ds(pl.multiple_of(c * nb, nb), nb)
            a = a_scr[pl.ds(c, 1), :]
            base = jnp.exp(-a * i8)
            tall = jnp.exp(-a * i16)
            p = (tall[:, None, :] * base[None]).reshape(LANES, LANES)
            pp = (p * factor).astype(jnp.bfloat16)
            pp_ref[pl.ds(pl.multiple_of(c * LANES, LANES), LANES), :] = pp
            urk = (urev_ref[rows, :].astype(jnp.float32) * keep_rev).astype(jnp.bfloat16)
            f_ref[rows, :] = mm(urk, pp)
        return 0

    for part in range(PARTS):
        lax.fori_loop(part * chans // PARTS // un, (part + 1) * chans // PARTS // un, fresh_step, 0)
        yield
    across = e_scr[0:chans, :]
    b_ext = b_scr[0:chans, :]
    state = jnp.zeros((chans, LANES), jnp.float32)
    for b in range(nb):
        s_ref[pl.ds(b, chans, stride=nb), :] = state + pltpu.roll(state, ns, axis=1)
        fresh = f_ref[pl.ds(b, chans, stride=nb), :]
        state = across * carry[b : b + 1, :] * state + b_ext * fresh

    yield

    def out_step(i, _):
        for j in range(un):
            c = i * un + j
            rows = pl.ds(pl.multiple_of(c * nb, nb), nb)
            t = toeplitz(kern_ref[pl.ds(c, 1), :])
            u = u_scr[rows, :]
            y = merge_masked(mm(stack_masked(u, masks), t), masks)
            sc = (s_ref[rows, :] * c_scr[pl.ds(c, 1), :]).astype(jnp.bfloat16)
            pp = pp_ref[pl.ds(pl.multiple_of(c * LANES, LANES), LANES), :]
            core = y + live * mm(sc, pp, NT) + skip_ref[0, c] * u
            core_ref[rows, :] = core
            u_scr[rows, :] = qkv_ref[0, rows] * core
        return 0

    count = chans // PARTS
    for part in range(PARTS):
        lax.fori_loop(part * count // un, (part + 1) * count // un, out_step, 0)
        for b in range(nb):
            half = b % 2
            mixed_ref[b // 2, part * count : (part + 1) * count, half * LANES : (half + 1) * LANES] = u_scr[
                pl.ds(part * count * nb + b, count, stride=nb), :
            ].astype(jnp.bfloat16)
        yield


def mixer_backward(
    un, gm_ref, qkv_ref, core_ref, s_ref, f_ref, urev_ref, pp_ref, kern_ref, seg_ref,
    sw_ref, skip_ref, rate_ref, inb_ref, outc_ref,
    dqkv_ref, dsw_ref, drate_ref, dinb_ref, doutc_ref, dskip_ref,
    tscr, b_scr, c_scr, e_scr, g_scr, sh_scr, h_scr, x_scr, dur_scr, dui_scr, dq_scr, dk_scr, dv_scr, gr_scr, red_scr,
):
    ns, chans = rate_ref.shape
    nb = qkv_ref.shape[1] // chans
    masks, live, keep, carry, same = seg_masks(read_seg(seg_ref, nb), nb)
    flip = flip_matrix()
    keep_rev = mm(keep.astype(jnp.bfloat16), flip)
    masks_rev = [mm(m.astype(jnp.bfloat16), flip) for m in masks]
    rate, in_b, out_c = rate_ref[...], inb_ref[...], outc_ref[...]
    decay = jnp.exp(-rate)
    b_scr[...] = transposed(tscr, in_b * decay, None)
    c_scr[...] = transposed(tscr, out_c, None)
    e_scr[...] = transposed(tscr, jnp.exp(-rate * LANES), None)
    red_scr[...] = jnp.zeros_like(red_scr)
    gr_scr[...] = jnp.zeros_like(gr_scr)

    corner = iota((LANES, LANES), 0) + iota((LANES, LANES), 1) >= LANES - 1

    def grad_step(i, _):
        for j in range(un):
            c = i * un + j
            rows = pl.ds(pl.multiple_of(c * nb, nb), nb)
            gm = x_scr[rows, :]
            dq_scr[rows, :] = gm * core_ref[rows, :]
            g = gm * qkv_ref[0, rows]
            g_scr[rows, :] = g
            k = qkv_ref[1, rows]
            shifted = sw_ref[0, c] * k
            for lag, prior in enumerate(priors(k, same)):
                shifted = shifted + sw_ref[lag + 1, c] * prior
            sh_scr[rows, :] = shifted
            red_scr[SHIFT, pl.ds(c, 1), :] = jnp.sum(
                g * shifted * qkv_ref[2, rows], axis=0, keepdims=True
            )
            ur = stack_masked(urev_ref[rows, :].astype(jnp.float32), masks_rev)
            cross = mm(ur, stack_masked(g, masks), TN)
            skew = pltpu.roll(jnp.where(corner, cross, 0.0), 1, axis=1, stride=1, stride_axis=0)
            gr_scr[pl.ds(c, 1), :] = jnp.sum(skew, axis=0, keepdims=True)
            pp = pp_ref[pl.ds(pl.multiple_of(c * LANES, LANES), LANES), :]
            h_scr[rows, :] = mm((g * live).astype(jnp.bfloat16), pp)
        return 0

    count = chans // PARTS
    for part in range(PARTS):
        for b in range(nb):
            half = b % 2
            x_scr[pl.ds(part * count * nb + b, count, stride=nb), :] = gm_ref[
                b // 2, part * count : (part + 1) * count, half * LANES : (half + 1) * LANES
            ].astype(jnp.float32)
        lax.fori_loop(part * count // un, (part + 1) * count // un, grad_step, 0)
        yield
    for b in range(nb):
        half = b % 2
        dqkv_ref[b // 2, 0, :, half * LANES : (half + 1) * LANES] = dq_scr[
            pl.ds(b, chans, stride=nb), :
        ].astype(jnp.bfloat16)
    across = e_scr[0:chans, :]
    b_ext = b_scr[0:chans, :]
    c_ext = c_scr[0:chans, :]
    zero = jnp.zeros((chans, LANES), jnp.float32)
    adj, acc_out, acc_in, acc_carry = zero, zero, zero, zero
    for b in range(nb - 1, -1, -1):
        here = pl.ds(b, chans, stride=nb)
        h = h_scr[here, :]
        s = s_ref[here, :]
        acc_out = acc_out + s * h
        acc_in = acc_in + (adj + pltpu.roll(adj, ns, axis=1)) * f_ref[here, :]
        acc_carry = acc_carry + carry[b : b + 1, :] * adj * s
        x_scr[here, :] = b_ext * adj
        adj = c_ext * h + across * carry[b : b + 1, :] * adj

    dskip_ref[...] = jnp.sum(red_scr[SHIFT].T, axis=0, keepdims=True)[:, 0:chans]
    tscr[...] = gr_scr[...].T

    def kern_back(i, carried):
        e, zeroth, first = carried
        block = tscr[pl.ds(pl.multiple_of(i * 8, 8), 8), 0:chans]
        for j in range(8):
            term = e * block[j : j + 1, :]
            zeroth = zeroth + term
            first = first + term * (i * 8 + j).astype(jnp.float32)
            e = e * decay
        return e, zeroth, first

    blank = jnp.zeros((ns, chans), jnp.float32)
    _, zeroth, first = lax.fori_loop(0, LANES // 8, kern_back, (blank + 1.0, blank, blank))

    def back(x):
        tscr[...] = jnp.zeros_like(tscr)
        tscr[0:chans, :] = x
        y = tscr[...].T
        return y[0:ns, 0:chans], y[ns : 2 * ns, 0:chans]

    d_out, s_h1 = back(acc_out)
    d_inp, ds_f1 = back(acc_in)
    d_carry, _ = back(acc_carry)
    dinb_ref[...] = decay * d_inp + out_c * zeroth
    doutc_ref[...] = d_out + in_b * zeroth
    drate_ref[...] = -(
        out_c * s_h1
        + in_b * decay * (ds_f1 + d_inp)
        + LANES * jnp.exp(-rate * LANES) * d_carry
        + in_b * out_c * first
    )
    yield

    def back_step(i, _):
        for j in range(un):
            c = i * un + j
            rows = pl.ds(pl.multiple_of(c * nb, nb), nb)
            t = toeplitz(kern_ref[pl.ds(c, 1), :])
            g = g_scr[rows, :]
            inner = merge_masked(mm(stack_masked(g, masks), t, NT), masks)
            pp = pp_ref[pl.ds(pl.multiple_of(c * LANES, LANES), LANES), :]
            dur_scr[rows, :] = (mm(x_scr[rows, :].astype(jnp.bfloat16), pp, NT) * keep_rev).astype(jnp.bfloat16)
            g_scr[rows, :] = inner + skip_ref[0, c] * g
        return 0

    lax.fori_loop(0, chans // un, back_step, 0)
    yield
    step_rows = 16 * nb

    def rev_step(i, _):
        rows = pl.ds(pl.multiple_of(i * step_rows, step_rows), step_rows)
        dui_scr[rows, :] = mm(dur_scr[rows, :], flip)
        return 0

    lax.fori_loop(0, chans // 16, rev_step, 0)

    def last_step(i, _):
        for j in range(un):
            c = i * un + j
            rows = pl.ds(pl.multiple_of(c * nb, nb), nb)
            du = g_scr[rows, :] + dui_scr[rows, :]
            dv_scr[rows, :] = du * sh_scr[rows, :]
            ds = du * qkv_ref[2, rows]
            k = qkv_ref[1, rows]
            lane = iota(k.shape, 1)
            red_scr[0, pl.ds(c, 1), :] = jnp.sum(ds * k, axis=0, keepdims=True)
            dk = sw_ref[0, c] * ds
            for lag, prior in enumerate(priors(k, same)):
                red_scr[lag + 1, pl.ds(c, 1), :] = jnp.sum(ds * prior, axis=0, keepdims=True)
                d = ds * same[lag]
                r = pltpu.roll(d, LANES - (lag + 1), axis=1)
                r2 = pltpu.roll(r, nb - 1, axis=0)
                dk = dk + sw_ref[lag + 1, c] * jnp.where(lane < LANES - (lag + 1), r, r2)
            dk_scr[rows, :] = dk
        return 0

    lax.fori_loop(0, chans // un, last_step, 0)
    yield
    for b in range(nb):
        half = b % 2
        for i, scr in ((1, dk_scr), (2, dv_scr)):
            dqkv_ref[b // 2, i, :, half * LANES : (half + 1) * LANES] = scr[
                pl.ds(b, chans, stride=nb), :
            ].astype(jnp.bfloat16)
    yield
    for j in range(SHIFT):
        dsw_ref[j : j + 1, :] = jnp.sum(red_scr[j].T, axis=0, keepdims=True)[:, 0:chans]


MESH = pl.DeviceIdType.MESH


class Place:
    def __init__(self, n_dp, n_head, n_tensor):
        self.n_dp, self.n_head, self.n_tensor = n_dp, n_head, n_tensor
        self.dp = lax.axis_index("dp")
        h, t = lax.axis_index("head"), lax.axis_index("tensor")
        self.size = n_head * n_tensor
        ph, xh, yt = h + 1 - 2 * (h % 2), (h + 2) % n_head, 1 - t
        pxh = (ph + 2) % n_head
        slot = lambda a, b: a * n_tensor + b
        self.me, self.p, self.x, self.y, self.d = (
            slot(h, t), slot(ph, t), slot(xh, t), slot(h, yt), slot(xh, yt),
        )
        self.px, self.py, self.pd = slot(pxh, t), slot(ph, yt), slot(pxh, yt)
        self.to_p, self.to_x, self.to_y = {"head": ph}, {"head": xh}, {"tensor": yt}

    def dp_peer(self, step):
        return (self.dp + step) % self.n_dp

    def greet_all(self, whole_group, over_dp):
        sem = pltpu.get_barrier_semaphore()

        def greet(where):
            pl.semaphore_signal(sem, inc=1, device_id=where, device_id_type=MESH)

        if whole_group:
            for i in range(1, self.size):
                peer = (self.me + i) % self.size
                greet({"head": peer // self.n_tensor, "tensor": peer % self.n_tensor})
            count = self.size - 1
        else:
            for where in (self.to_p, self.to_x, self.to_y):
                greet(where)
            count = 3
        if over_dp:
            def step(i, _):
                greet({"dp": self.dp_peer(i)})
                return 0

            lax.fori_loop(1, self.n_dp, step, 0)
            count += self.n_dp - 1
        return lambda: pl.semaphore_wait(sem, count)


def remote(src, dst, ssem, rsem, where):
    return pltpu.make_async_remote_copy(
        src_ref=src, dst_ref=dst, send_sem=ssem, recv_sem=rsem, device_id=where, device_id_type=MESH
    )


class GroupGather:
    COPIES = 11

    def __init__(self, place, ref, ssem, rsem):
        self.ssem, self.rsem = ssem, rsem
        half = ref.shape[1] // 2
        top, low = pl.ds(0, half), pl.ds(half, half)
        pc = place
        full = lambda s: ref.at[s]
        part = lambda s, rows: ref.at[s, rows]
        self.out = [
            (full(pc.me), pc.to_p),
            (part(pc.me, top), pc.to_x), (part(pc.me, low), pc.to_x),
            (part(pc.me, low), pc.to_y), (part(pc.me, top), pc.to_y),
            (part(pc.x, top), pc.to_y), (part(pc.y, low), pc.to_x),
            (full(pc.x), pc.to_p), (full(pc.y), pc.to_p),
            (part(pc.d, top), pc.to_p), (part(pc.d, low), pc.to_p),
        ]
        self.into = [
            full(pc.p), part(pc.x, top), part(pc.x, low), part(pc.y, low), part(pc.y, top),
            part(pc.d, top), part(pc.d, low), full(pc.px), full(pc.py), part(pc.pd, top), part(pc.pd, low),
        ]

    def send(self, *which):
        for i in which:
            src, where = self.out[i]
            remote(src, src, self.ssem.at[i], self.rsem.at[i], where).start()

    def arrive(self, *which):
        for i in which:
            dst = self.into[i]
            remote(dst, dst, self.ssem.at[i], self.rsem.at[i], self.out[i][1]).wait_recv()

    def start(self):
        self.send(1, 3, 2, 4, 0)

    def first(self):
        self.arrive(1)
        self.send(5)
        self.arrive(3)
        self.send(6)

    def second(self):
        self.arrive(2)
        self.send(7)
        self.arrive(4)
        self.send(8)

    def third(self):
        self.arrive(5)
        self.send(9)
        self.arrive(6)
        self.send(10)

    def finish(self):
        self.arrive(0, 7, 8, 9, 10)

    def drain(self):
        for i in range(self.COPIES):
            src, where = self.out[i]
            remote(src, src, self.ssem.at[i], self.rsem.at[i], where).wait_send()


class DepthGather:
    def __init__(self, place, ref, ssem, rsem):
        self.place, self.ref, self.ssem, self.rsem = place, ref, ssem, rsem

    def _copy(self, step, slot, peer):
        return remote(
            self.ref.at[slot], self.ref.at[slot], self.ssem.at[step], self.rsem.at[step], {"dp": peer}
        )

    def _loop(self, body):
        def step(i, _):
            body(i)
            return 0

        lax.fori_loop(1, self.place.n_dp, step, 0)

    def start(self):
        pc = self.place
        self._loop(lambda i: self._copy(i, pc.dp, pc.dp_peer(i)).start())

    def finish(self):
        pc = self.place
        source = lambda i: (pc.dp + pc.n_dp - i) % pc.n_dp
        self._loop(lambda i: self._copy(i, source(i), pc.dp_peer(i)).wait_recv())

    def drain(self):
        pc = self.place
        self._loop(lambda i: self._copy(i, pc.dp, pc.dp_peer(i)).wait_send())


class LineGather:
    def __init__(self, place, ref, ssem, rsem):
        self.pc, self.ref, self.ssem, self.rsem = place, ref, ssem, rsem
        self.n, self.at = place.n_dp, place.dp
        self.steps = self.n - 1

    def _copy(self, slot, way):
        return remote(
            self.ref.at[slot], self.ref.at[slot], self.ssem.at[way * self.n + slot], self.rsem.at[slot],
            {"dp": self.at + 1 - 2 * way},
        )

    def _pass(self, slot):
        @pl.when((slot <= self.at) & (self.at < self.n - 1))
        def _():
            self._copy(slot, 0).start()

        @pl.when((slot >= self.at) & (self.at > 0))
        def _():
            self._copy(slot, 1).start()

    def start(self):
        self._pass(self.at)

    def step(self, s):
        below, above = self.at - 1 - s, self.at + 1 + s

        @pl.when(below >= 0)
        def _():
            self._copy(below, 0).wait_recv()

            @pl.when(self.at < self.n - 1)
            def _():
                self._copy(below, 0).start()

        @pl.when(above < self.n)
        def _():
            self._copy(above, 1).wait_recv()

            @pl.when(self.at > 0)
            def _():
                self._copy(above, 1).start()

    def rest(self, first):
        def body(s, _):
            self.step(s)
            return 0

        lax.fori_loop(first, self.steps, body, 0)

    def drain(self):
        def body(slot, _):
            @pl.when((slot <= self.at) & (self.at < self.n - 1))
            def _():
                self._copy(slot, 0).wait_send()

            @pl.when((slot >= self.at) & (self.at > 0))
            def _():
                self._copy(slot, 1).wait_send()

            return 0

        lax.fori_loop(0, self.n, body, 0)


def joined(ref):
    n, rows, columns = ref.shape
    if rows % 16 == 0:
        return ref[...].reshape(n * rows, columns)
    parts = [ref[j].astype(jnp.float32) for j in range(n)]
    return jnp.concatenate(parts, axis=0).astype(ref.dtype)


def row_norm(x):
    centred = x - jnp.mean(x, axis=1, keepdims=True)
    inv = lax.rsqrt(jnp.mean(centred * centred, axis=1, keepdims=True) + 1e-05)
    return centred * inv, inv


class GroupReduce:
    COPIES = 10

    def __init__(self, place, part, land, half_land, last_land, ssem, rsem):
        pc = place
        self.pc = pc
        self.part, self.land, self.half_land, self.last_land = part, land, half_land, last_land
        self.ssem, self.rsem = ssem, rsem
        half = part.shape[1] // 2
        top, low = pl.ds(0, half), pl.ds(half, half)
        self.top, self.low = top, low
        self.mine = [pc.d, pc.x, pc.y, pc.me]
        self.theirs = [pc.pd, pc.px, pc.py, pc.p]
        self.copies = [(part.at[self.theirs[i]], land.at[i], pc.to_p) for i in range(4)] + [
            (part.at[pc.d, top], half_land.at[0], pc.to_x),
            (part.at[pc.d, low], half_land.at[1], pc.to_y),
            (part.at[pc.x, top], last_land.at[0, top], pc.to_x),
            (part.at[pc.y, low], last_land.at[1, low], pc.to_y),
            (part.at[pc.x, low], last_land.at[0, low], pc.to_x),
            (part.at[pc.y, top], last_land.at[1, top], pc.to_y),
        ]

    def _copy(self, i):
        src, dst, where = self.copies[i]
        return remote(src, dst, self.ssem.at[i], self.rsem.at[i], where)

    def give(self, *which):
        for i in which:
            self._copy(i).start()

    def pair(self, i):
        self._copy(i).wait_recv()
        s = self.mine[i]
        self.part[s] = (self.part[s].astype(jnp.float32) + self.land[i].astype(jnp.float32)).astype(
            self.part.dtype
        )

    def side(self):
        self.pair(1)
        self.give(6)
        self.pair(2)
        self.give(7)

    def far(self):
        self.pair(0)
        self.give(4, 5)

    def near(self):
        for i, s, rows in ((4, self.pc.y, self.top), (5, self.pc.x, self.low)):
            self._copy(i).wait_recv()
            self.part[s, rows] = (
                self.part[s, rows].astype(jnp.float32) + self.half_land[i - 4].astype(jnp.float32)
            ).astype(self.part.dtype)
            self.give(9 if i == 4 else 8)

    def total(self):
        for i in (6, 7, 8, 9):
            self._copy(i).wait_recv()
        return (
            self.part[self.pc.me].astype(jnp.float32)
            + self.last_land[0].astype(jnp.float32)
            + self.last_land[1].astype(jnp.float32)
        )

    def drain(self):
        for i in range(self.COPIES):
            self._copy(i).wait_send()

    @staticmethod
    def scratch(group, rows, columns):
        bf16 = jnp.bfloat16
        return [
            pltpu.VMEM((group, rows, columns), bf16),
            pltpu.VMEM((4, rows, columns), bf16),
            pltpu.VMEM((2, rows // 2, columns), bf16),
            pltpu.VMEM((2, rows, columns), bf16),
        ]


class GroupSwap:
    def __init__(self, place, src, dst, lsem, rows, ssem, rsem):
        self.pc, self.src, self.dst, self.ssem, self.rsem, self.lsem = place, src, dst, ssem, rsem, lsem
        self.rows = rows

    def _peer(self, i):
        return (self.pc.me + i) % self.pc.size

    def _copy(self, i, slot):
        peer = self._peer(i)
        where = {"head": peer // self.pc.n_tensor, "tensor": peer % self.pc.n_tensor}
        return remote(
            self.src.at[peer, self.rows], self.dst.at[slot, self.rows], self.ssem.at[i], self.rsem.at[i], where
        )

    def _own(self):
        me = self.pc.me
        return pltpu.make_async_copy(self.src.at[me, self.rows], self.dst.at[me, self.rows], self.lsem)

    def start(self):
        for i in range(1, self.pc.size):
            self._copy(i, self.pc.me).start()
        self._own().start()

    def finish(self):
        for i in range(1, self.pc.size):
            self._copy(i, (self.pc.me + self.pc.size - i) % self.pc.size).wait_recv()
        self._own().wait()

    def drain(self):
        for i in range(1, self.pc.size):
            self._copy(i, self.pc.me).wait_send()


class DepthReduce:
    def __init__(self, place, src, land, ssem, rsem):
        self.place, self.src, self.land, self.ssem, self.rsem = place, src, land, ssem, rsem

    def _copy(self, step, mine, slot, peer):
        return remote(
            self.src.at[mine], self.land.at[slot], self.ssem.at[step], self.rsem.at[step], {"dp": peer}
        )

    def _loop(self, body, start):
        return lax.fori_loop(1, self.place.n_dp, body, start)

    def start(self):
        pc = self.place

        def step(i, _):
            self._copy(i, pc.dp_peer(i), pc.dp, pc.dp_peer(i)).start()
            return 0

        self._loop(step, 0)

    def total(self):
        pc = self.place

        def step(i, acc):
            source = (pc.dp + pc.n_dp - i) % pc.n_dp
            self._copy(i, source, source, pc.dp_peer(i)).wait_recv()
            return acc + self.land[source].astype(jnp.float32)

        return self._loop(step, self.src[pc.dp].astype(jnp.float32))

    def drain(self):
        pc = self.place

        def step(i, _):
            self._copy(i, pc.dp_peer(i), pc.dp, pc.dp_peer(i)).wait_send()
            return 0

        self._loop(step, 0)


def split_rows(ref, value):
    n, rows, columns = ref.shape
    if rows % 16 == 0:
        ref[...] = value.astype(ref.dtype).reshape(n, rows, columns)
    else:
        for j in range(n):
            ref[j] = value[j * rows : (j + 1) * rows].astype(ref.dtype)


def row_norm_back(grad, gain, hat, inv):
    scaled = grad * gain
    return inv * (
        scaled
        - jnp.mean(scaled, axis=1, keepdims=True)
        - hat * jnp.mean(scaled * hat, axis=1, keepdims=True)
    )


def gelu_pair(pre):
    cdf = 0.5 * (1.0 + lax.erf(pre * 0.7071067811865476))
    return pre * cdf, cdf + pre * (0.3989422804014327 * jnp.exp(-0.5 * pre * pre))


class GroupSpread:
    def __init__(self, place, ref, ssem, rsem):
        self.pc, self.ref, self.ssem, self.rsem = place, ref, ssem, rsem

    def _copy(self, i, slot):
        peer = (self.pc.me + i) % self.pc.size
        where = {"head": peer // self.pc.n_tensor, "tensor": peer % self.pc.n_tensor}
        return remote(self.ref.at[slot], self.ref.at[slot], self.ssem.at[i], self.rsem.at[i], where)

    def start(self):
        for i in range(1, self.pc.size):
            self._copy(i, self.pc.me).start()

    def finish(self):
        for i in range(1, self.pc.size):
            self._copy(i, (self.pc.me + self.pc.size - i) % self.pc.size).wait_recv()

    def drain(self):
        for i in range(1, self.pc.size):
            self._copy(i, self.pc.me).wait_send()


SKIP_AT, PARAM_ROWS = 192, 208
UNROLL, UNROLL_BACK = 24, 48


class Names:
    def __init__(self, names, refs):
        assert len(names) == len(refs)
        for name, ref in zip(names, refs):
            setattr(self, name, ref)


def layout(axes, own, feats, rows, chans, units, ns, results):
    n_dp, n_head, n_tensor = axes
    group = n_head * n_tensor
    f32, bf16 = jnp.float32, jnp.bfloat16
    v = pltpu.VMEM
    dma = lambda *shape: pltpu.SemaphoreType.DMA(shape)
    blocks = group * own // LANES
    conv = chans * blocks
    sq = v((LANES, LANES), f32)
    full = v((conv, LANES), f32)
    out = dict(
        tok=v((own, feats), bf16), cot=v((own, feats), bf16), four=v((4, rows, chans), bf16),
        wqkvo=v((n_dp, rows, 4 * chans), bf16), wup=v((n_dp, rows, units), bf16), wdown=v((n_dp, rows, units), bf16),
        wt=v((4 * chans, feats), bf16), wupt=v((units, feats), bf16), wdownt=v((units, feats), bf16),
        wout=v((group, chans, feats), bf16),
        xn1=v((group, feats, own), bf16), cots=v((group, feats, own), bf16), xn2=v((group, feats, own), bf16),
        act=v((group, units, own), bf16), gpre=v((group, units, own), bf16),
        qkv=v((3, conv, LANES), f32), core=full, s=full, f=full, urev=v((conv, LANES), bf16),
        pp=v((chans * LANES, LANES), bf16), kern=v((chans, LANES), f32),
        mixed=v((group, chans, own), bf16), mixed_in=v((group, chans, own), bf16),
        gmix=v((group, chans, own), bf16), gmix_in=v((group, chans, own), bf16),
        dqkv=v((group, 3, chans, own), bf16),
        t0=sq, t1=sq, t2=sq, t3=sq, t4=sq, t5=sq, gr=sq, red=v((SHIFT + 1, LANES, LANES), f32),
        w0=full, w1=full, w2=full, w3=full, w4=full, w5=full, w6=full, dur=v((conv, LANES), bf16),
        dsw=v((SHIFT, chans), f32), drate=v((ns, chans), f32), dinb=v((ns, chans), f32), doutc=v((ns, chans), f32),
        dskip=v((1, chans), f32),
        hat=v((own, feats), f32), hid=v((own, feats), f32), ghid=v((own, feats), f32),
        up_part=v((n_dp, rows, units), bf16), up_land=v((n_dp, rows, units), bf16),
        dn_part=v((n_dp, rows, units), bf16), dn_land=v((n_dp, rows, units), bf16),
        q_part=v((n_dp, rows, chans), bf16), q_land=v((n_dp, rows, chans), bf16),
        o_out=v((n_dp, rows, chans), bf16), o_in=v((n_dp, rows, chans), bf16),
        kv_part=v((n_dp, rows, 2 * chans), bf16), kv_land=v((n_dp, rows, 2 * chans), bf16),
        taps_all=v((n_dp, 8, LANES), f32),
        params=v((n_dp, PARAM_ROWS, LANES), bf16),
        n1=v((group, 2, feats), f32), n2=v((group, 2, feats), f32), m1=v((n_dp, 2, feats), f32), m2=v((n_dp, 2, feats), f32),
    )
    out.update(
        seg=v((1, group * own), jnp.int32), rate=v((ns, chans), f32), inb=v((ns, chans), f32), outc=v((ns, chans), f32),
        gain1=v((feats,), f32), bias1=v((feats,), f32), gain2=v((feats,), f32), bias2=v((feats,), f32),
    )
    out.update((name, v(a.shape, a.dtype)) for name, a in zip(RESULTS, results))
    for name, height, width in (("x", feats, own), ("m", feats, own), ("o", chans, feats)):
        for part, alloc in zip(("part", "land", "half", "last"), GroupReduce.scratch(group, height, width)):
            out[f"{name}_{part}"] = alloc
    for name, count in (
        ("xn1", 11), ("cots", 11), ("wout", 11), ("xn2", 11), ("x2", 10), ("m", 10), ("o", 10), ("x1", 10),
        ("in0", group), ("in1", group), ("back0", group), ("back1", group), ("sp1", group), ("sp2", group),
        ("zq", n_dp), ("zu", n_dp), ("zd", n_dp), ("gu", n_dp), ("gd", n_dp), ("gq", n_dp), ("go", n_dp), ("gkv", n_dp), ("zt", n_dp), ("zp", n_dp),
        ("zn1", n_dp), ("zn2", n_dp),
    ):
        out[f"send_{name}"] = dma(count)
        out[f"recv_{name}"] = dma(count)
    out["local"] = dma(12)
    out["small"] = dma(len(SMALL))
    out["given"] = dma(len(RESULTS))
    return out


INPUTS = (
    "tok_hbm", "cot_hbm", "q_hbm", "k_hbm", "v_hbm", "o_hbm", "up_hbm", "down_hbm",
    "seg_hbm", "gain1_hbm", "bias1_hbm", "gain2_hbm", "bias2_hbm", "taps", "rate_hbm", "inb_hbm", "outc_hbm", "skip",
)
RESULTS = (
    "res", "gx", "g1", "b1", "g2", "b2", "dq", "dk", "dv", "do", "dup", "ddown",
    "out_taps", "out_rate", "out_inb", "out_outc", "out_skip",
)
OUTPUTS = tuple(name + "_hbm" for name in RESULTS)
SMALL = ("seg", "gain1", "bias1", "gain2", "bias2", "rate", "inb", "outc")


def run_beside(body, tasks):
    tasks = list(tasks)
    for _ in body:
        if tasks:
            tasks.pop(0)()
    for task in tasks:
        task()


def block_kernel(axes, names, *refs):
    r = Names(names, refs)
    pc = Place(*axes)
    f32, bf16 = jnp.float32, jnp.bfloat16
    group, chans, feats = r.wout.shape
    own = r.tok.shape[0]
    blocks = own // LANES
    work = []

    def sems(name):
        return getattr(r, f"send_{name}"), getattr(r, f"recv_{name}")

    def make(kind, name, *args):
        made = kind(pc, *args, *sems(name))
        work.append(made)
        return made

    def local(i, src, dst):
        copy = pltpu.make_async_copy(src, dst, r.local.at[i])
        copy.start()
        return copy

    load_tok = local(4, r.tok_hbm, r.tok)
    small = []
    for i, name in enumerate(SMALL):
        small.append(pltpu.make_async_copy(getattr(r, name + "_hbm"), getattr(r, name), r.small.at[i]))
        small[-1].start()
    given = []

    def give(*which):
        for name in which:
            i = RESULTS.index(name)
            given.append(pltpu.make_async_copy(getattr(r, name), getattr(r, name + "_hbm"), r.given.at[i]))
            given[-1].start()

    four = [local(i, src, r.four.at[i]) for i, src in enumerate((r.q_hbm, r.k_hbm, r.v_hbm, r.o_hbm))]
    load_cot = local(5, r.cot_hbm, r.cot)
    load_up = local(6, r.up_hbm, r.wup.at[pc.dp])
    load_down = local(7, r.down_hbm, r.wdown.at[pc.dp])
    meet = pc.greet_all(True, True)
    z_qkvo = make(DepthGather, "zq", r.wqkvo)
    z_up = make(DepthGather, "zu", r.wup)
    z_down = make(DepthGather, "zd", r.wdown)
    xn1_g = make(GroupGather, "xn1", r.xn1)
    cot_g = make(GroupGather, "cots", r.cots)
    out_g = make(GroupGather, "wout", r.wout)
    xn2_g = make(GroupGather, "xn2", r.xn2)
    halves = [pl.ds(i * (chans // PARTS), chans // PARTS) for i in range(PARTS)]
    swap_in = [make(GroupSwap, f"in{i}", r.mixed, r.mixed_in, r.local.at[8 + i], rows) for i, rows in enumerate(halves)]
    swap_back = [make(GroupSwap, f"back{i}", r.gmix, r.gmix_in, r.local.at[10 + i], rows) for i, rows in enumerate(halves)]
    for copy in small:
        copy.wait()
    gain1, gain2 = r.gain1[...].reshape(1, feats), r.gain2[...].reshape(1, feats)
    bias1, bias2 = r.bias1[...].reshape(1, feats), r.bias2[...].reshape(1, feats)
    load_tok.wait()
    hat1, _ = row_norm(r.tok[...].astype(f32))
    r.xn1[pc.me] = (hat1 * gain1 + bias1).astype(bf16).T
    meet()
    xn1_g.start()
    for copy in four:
        copy.wait()
    r.wqkvo[pc.dp] = jnp.concatenate([r.four[i] for i in range(4)], axis=1)
    z_qkvo.start()
    load_cot.wait()
    r.cots[pc.me] = r.cot[...].T
    xn1_g.first()
    xn1_g.second()
    z_qkvo.finish()
    load_up.wait()
    z_up.start()
    r.wt[...] = joined(r.wqkvo).T
    r.wout[pc.me] = r.wt[3 * chans :, :]
    out_g.start()
    load_down.wait()

    def project(s):
        y = mm(r.wt[0 : 3 * chans, :], r.xn1[s])
        for i in range(3):
            for h in range(blocks):
                r.qkv[i, pl.ds(s * blocks + h, chans, stride=group * blocks), :] = y[
                    i * chans : (i + 1) * chans, h * LANES : (h + 1) * LANES
                ]

    xn1_g.third()
    xn1_g.finish()
    for s in range(group):
        project(s)

    def after_drive():
        out_g.first()
        out_g.second()
        cot_g.start()

    def after_scan():
        out_g.third()

    def half_out():
        swap_in[0].start()
        z_up.finish()
        z_down.start()

    mixer = (r.seg, r.taps, r.skip, r.rate, r.inb, r.outc)
    run_beside(
        mixer_forward(
            UNROLL, r.qkv, *mixer, r.mixed, r.core, r.s, r.f, r.urev, r.pp, r.kern,
            r.t0, r.t1, r.t2, r.t3, r.t4, r.w0, r.t5,
        ),
        (after_drive, lambda: None, lambda: None, after_scan, half_out, swap_in[1].start),
    )
    cot_g.first()
    out_g.finish()
    cot_g.second()
    w_up = joined(r.wup)
    r.wupt[...] = w_up.T
    wout_t = r.wout[...].reshape(feats, feats)
    swap_in[0].finish()
    swap_in[1].finish()
    mixed_t = r.mixed_in[...].reshape(feats, own)
    hidden = r.tok[...].astype(f32) + mm(mixed_t, wout_t, TN)
    hat2, inv2 = row_norm(hidden)
    r.xn2[pc.me] = (hat2 * gain2 + bias2).astype(bf16).T
    xn2_g.start()
    r.hid[...] = hidden
    r.hat[...] = hat2
    cot_g.third()
    z_down.finish()
    w_down = joined(r.wdown)
    r.wdownt[...] = w_down.T
    cot_g.finish()
    red_x2 = make(GroupReduce, "x2", r.x_part, r.x_land, r.x_half, r.x_last)
    red_m = make(GroupReduce, "m", r.m_part, r.m_land, r.m_half, r.m_last)
    red_o = make(GroupReduce, "o", r.o_part, r.o_land, r.o_half, r.o_last)

    def chunk(s):
        act, slope = gelu_pair(mm(r.wupt[...], r.xn2[s]))
        r.act[s] = act.astype(bf16)
        grad_pre = (mm(r.wdownt[...], r.cots[s]) * slope).astype(bf16)
        r.gpre[s] = grad_pre
        r.x_part[s] = mm(w_up, grad_pre).astype(bf16)

    chunk(pc.me)
    xn2_g.arrive(0)
    chunk(pc.p)
    red_x2.give(3)
    xn2_g.first()
    xn2_g.second()
    chunk(pc.x)
    chunk(pc.y)
    xn2_g.arrive(7)
    chunk(pc.px)
    red_x2.give(1)
    xn2_g.arrive(8)
    chunk(pc.py)
    red_x2.give(2)
    xn2_g.third()
    red_x2.side()
    chunk(pc.d)
    xn2_g.arrive(9, 10)
    chunk(pc.pd)
    red_x2.give(0)
    red_x2.far()
    red_x2.pair(3)
    units = r.act.shape[1]
    grad_up = jnp.zeros((feats, units), f32)
    for s in range(group):
        grad_up = grad_up + mm(r.xn2[s], r.gpre[s], NT)
    split_rows(r.up_part, grad_up)
    sum_up = make(DepthReduce, "gu", r.up_part, r.up_land)
    sum_up.start()
    red_x2.near()
    for i, s in enumerate(red_m.theirs):
        r.m_part[s] = mm(w_down, r.act[s]).astype(bf16)
        red_m.give(i)
    for s in red_m.mine:
        r.m_part[s] = mm(w_down, r.act[s]).astype(bf16)
    grad_down = jnp.zeros((feats, units), f32)
    for s in range(group):
        grad_down = grad_down + mm(r.cots[s], r.act[s], NT)
    split_rows(r.dn_part, grad_down)
    sum_down = make(DepthReduce, "gd", r.dn_part, r.dn_land)
    sum_down.start()
    grad_xn = red_x2.total().T
    hat2 = r.hat[...]
    grad_hidden = r.cot[...].astype(f32) + row_norm_back(grad_xn, gain2, hat2, inv2)
    r.ghid[...] = grad_hidden
    grad_mix = grad_hidden.astype(bf16)
    r.gmix[...] = mm(wout_t, grad_mix, NT).astype(bf16).reshape(group, chans, own)
    swap_back[0].start()
    swap_back[1].start()
    r.n2[pc.me, 0:1, :] = jnp.sum(grad_xn * hat2, axis=0, keepdims=True)
    r.n2[pc.me, 1:2, :] = jnp.sum(grad_xn, axis=0, keepdims=True)
    spread2 = make(GroupSpread, "sp2", r.n2)
    spread2.start()
    r.o_part[...] = mm(mixed_t, grad_mix).astype(bf16).reshape(group, chans, feats)
    red_o.give(0, 1, 2, 3)
    swap_back[0].finish()
    norm2 = make(DepthGather, "zn2", r.m2)

    ns = r.drate.shape[0]
    pieces = ((0, r.drate, r.out_rate), (ns, r.dinb, r.out_inb), (2 * ns, r.doutc, r.out_outc),
              (SKIP_AT, r.dskip, r.out_skip))
    z_par = make(DepthGather, "zp", r.params)
    sum_q = make(DepthReduce, "gq", r.q_part, r.q_land)
    sum_o = make(DepthReduce, "go", r.o_out, r.o_in)
    sum_kv = make(DepthReduce, "gkv", r.kv_part, r.kv_land)

    def second_half():
        swap_back[1].finish()
        red_o.far()
        red_o.side()
        red_m.far()

    def row_of(x):
        return jnp.broadcast_to(jnp.sum(x, axis=1, keepdims=True), (x.shape[0], LANES)).T[0:1]

    def early_sums():
        w_wide = joined(r.wqkvo).astype(f32)
        red_o.near()
        r.params[pc.dp] = jnp.zeros(r.params.shape[1:], bf16)
        for at, ref, _ in pieces:
            r.params[pc.dp, at : at + ref.shape[0], 0:chans] = ref[...].astype(bf16)
        z_par.start()
        grad_q = jnp.zeros((feats, chans), f32)
        for s in range(group):
            grad_q = grad_q + mm(r.xn1[s], r.dqkv[s, 0], NT)
        split_rows(r.q_part, grad_q)
        sum_q.start()
        r.n1[pc.me, 0:1, :] = row_of(grad_q * w_wide[:, 0:chans])

    def mlp_sums():
        red_m.side()
        red_m.near()
        red_x2.drain()
        work.remove(red_x2)

    def out_sums():
        red_o.pair(3)
        split_rows(r.o_out, red_o.total().T)
        sum_o.start()

    w_joint = joined(r.wqkvo)
    red_x1 = make(GroupReduce, "x1", r.x_part, r.x_land, r.x_half, r.x_last)

    def grads(s):
        return r.dqkv[s].reshape(3 * chans, own)

    def chunk_back(s):
        padded = jnp.concatenate([grads(s), jnp.zeros((chans, own), bf16)], axis=0)
        r.x_part[s] = mm(w_joint, padded).astype(bf16)

    spread1 = make(GroupSpread, "sp1", r.n1)
    norm1 = make(DepthGather, "zn1", r.m1)

    def start_back():
        theirs, mine = red_x1.theirs, red_x1.mine
        for k in range(3):
            chunk_back(theirs[k])
            red_x1.give(k)
            chunk_back(mine[k])
        red_x1.far()
        chunk_back(theirs[3])
        red_x1.give(3)
        red_x1.side()
        chunk_back(mine[3])
        grad_kv = jnp.zeros((feats, 2 * chans), f32)
        for s in range(group):
            grad_kv = grad_kv + mm(r.xn1[s], grads(s)[chans:], NT)
        split_rows(r.kv_part, grad_kv)
        sum_kv.start()
        w_wide = w_joint.astype(f32)
        token_sums = jnp.zeros((8, 3 * chans), f32)
        for s in range(group):
            token_sums = token_sums + mm(jnp.ones((8, own), bf16), grads(s), NT)
        r.n1[pc.me, 0:1, :] += row_of(grad_kv * w_wide[:, chans : 3 * chans])
        r.n1[pc.me, 1:2, :] = row_of(w_wide[:, 0 : 3 * chans] * token_sums[0:1])
        spread1.start()

    run_beside(
        mixer_backward(
            UNROLL_BACK, r.gmix_in, r.qkv, r.core, r.s, r.f, r.urev, r.pp, r.kern, *mixer,
            r.dqkv, r.dsw, r.drate, r.dinb, r.doutc, r.dskip,
            r.t0, r.t1, r.t2, r.t3, r.w0, r.w1, r.w2, r.w3, r.dur, r.w2, r.w4, r.w5, r.w6, r.gr, r.red,
        ),
        (second_half, lambda: None, early_sums, mlp_sums, out_sums, start_back),
    )
    r.taps_all[pc.dp] = jnp.zeros(r.taps_all.shape[1:], f32)
    r.taps_all[pc.dp, 0:SHIFT, 0:chans] = r.dsw[...]
    z_taps = make(DepthGather, "zt", r.taps_all)
    z_taps.start()
    spread2.finish()
    r.m2[pc.dp] = jnp.sum(r.n2[...], axis=0)
    norm2.start()
    red_x1.near()
    red_x1.pair(3)
    spread1.finish()
    r.m1[pc.dp] = jnp.sum(r.n1[...], axis=0)
    norm1.start()
    red_m.pair(3)
    r.res[...] = (r.hid[...] + red_m.total().T).astype(bf16)
    give("res")
    r.dup[...] = sum_up.total()
    r.ddown[...] = sum_down.total()
    give("dup", "ddown")
    z_par.finish()
    sums = jnp.sum(r.params[...].astype(f32), axis=0)
    for at, ref, out in pieces:
        out[...] = sums[at : at + ref.shape[0], 0:chans]
    give("out_rate", "out_inb", "out_outc", "out_skip")
    z_taps.finish()
    r.out_taps[...] = jnp.sum(r.taps_all[...], axis=0)[0:SHIFT, 0:chans]
    give("out_taps")
    norm2.finish()
    sums = jnp.sum(r.m2[...], axis=0)
    r.g2[...] = sums[0:1]
    r.b2[...] = sums[1:2]
    give("g2", "b2")
    r.do[...] = sum_o.total()
    r.dq[...] = sum_q.total()
    kv_sum = sum_kv.total()
    r.dk[...] = kv_sum[:, 0:chans]
    r.dv[...] = kv_sum[:, chans:]
    give("dq", "dk", "dv", "do")
    norm1.finish()
    sums = jnp.sum(r.m1[...], axis=0)
    r.g1[...] = (sums[0:1] - bias1 * sums[1:2]) / gain1
    r.b1[...] = sums[1:2]
    give("g1", "b1")
    hat1, inv1 = row_norm(r.tok[...].astype(f32))
    grad_xn = red_x1.total().T
    r.gx[...] = r.ghid[...] + row_norm_back(grad_xn, gain1, hat1, inv1)
    give("gx")
    for one in work:
        one.drain()
    for copy in given:
        copy.wait()


def hand_over(count, *refs):
    src, dst, mid, flat = refs[:count], refs[count : 2 * count], refs[2 * count : 3 * count], refs[3 * count : -2]
    sem_in, sem_out = refs[-2:]
    loads = [pltpu.make_async_copy(a, b, sem_in.at[i]) for i, (a, b) in enumerate(zip(src, mid))]
    for load in loads:
        load.start()
    flat = iter(flat)
    stores = []
    for i, load in enumerate(loads):
        load.wait()
        held = mid[i]
        if src[i].shape != dst[i].shape:
            held = next(flat)
            held[...] = mid[i][...].reshape(held.shape)
        stores.append(pltpu.make_async_copy(held, dst[i], sem_out.at[i]))
        stores[-1].start()
    for store in stores:
        store.wait()


def whole_block(axes, args):
    (tokens, seg, gain1, bias1, gain2, bias2, q, k, v, o, up, down, taps, rate, inb, outc, skip, cot) = args
    own, feats = tokens.shape
    rows, chans = q.shape
    units = up.shape[1]
    f32, bf16 = jnp.float32, jnp.bfloat16
    sds = jax.ShapeDtypeStruct
    vm = pl.BlockSpec(memory_space=pltpu.VMEM)
    sm = pl.BlockSpec(memory_space=pltpu.SMEM)
    hbm = pl.BlockSpec(memory_space=pl.ANY)
    wide, thin = sds((rows, units), f32), sds((rows, chans), f32)
    row = sds((1, feats), f32)
    results = (
        sds((own, feats), bf16), sds((own, feats), f32), row, row, row, row, thin, thin, thin, thin, wide, wide,
        *(sds(a.shape, f32) for a in (taps, rate, inb, outc)), sds((1, chans), f32),
    )
    scratch = layout(axes, own, feats, rows, chans, units, rate.shape[0], results)
    outs = pl.pallas_call(
        functools.partial(block_kernel, axes, INPUTS + OUTPUTS + tuple(scratch)),
        out_shape=results,
        in_specs=[hbm] * 13 + [sm] + [hbm] * 3 + [sm],
        out_specs=(hbm,) * 17,
        scratch_shapes=list(scratch.values()),
        compiler_params=pltpu.CompilerParams(
            collective_id=1, has_side_effects=True, vmem_limit_bytes=67043328
        ),
        name="block",
    )(tokens, cot, q, k, v, o, up, down, seg, gain1, bias1, gain2, bias2, taps, rate, inb, outc, skip[None])
    final = [sds(a.shape, a.dtype) for a in outs]
    for i in (2, 3, 4, 5):
        final[i] = sds((feats,), f32)
    final[16] = sds((chans,), f32)
    held = [pltpu.VMEM(a.shape, a.dtype) for a in outs]
    flat = [pltpu.VMEM(b.shape, b.dtype) for a, b in zip(outs, final) if a.shape != b.shape]
    count = len(outs)
    return pl.pallas_call(
        functools.partial(hand_over, count),
        out_shape=tuple(final),
        in_specs=[hbm] * count,
        out_specs=(hbm,) * count,
        scratch_shapes=held + flat + [pltpu.SemaphoreType.DMA((count,))] * 2,
        name="hand_over",
    )(*outs)


from jax.sharding import PartitionSpec as P

GROUP = ("head", "tensor")


def on_device(*args):
    return whole_block((lax.axis_size("dp"), lax.axis_size("head"), lax.axis_size("tensor")), args)


def solution(mesh):
    rows = P(("dp", "head", "tensor"), None)
    weight = P("dp", GROUP)
    chan = P(None, GROUP)
    in_specs = (rows, P("dp", None)) + (P(),) * 4 + (weight,) * 6 + (chan,) * 4 + (P(GROUP), rows)
    out_specs = (rows, rows) + (P(),) * 4 + (weight,) * 6 + (chan,) * 4 + (P(GROUP),)
    return jax.shard_map(on_device, mesh=mesh, in_specs=in_specs, out_specs=out_specs, check_vma=False)
```
